32 devices in a mesh: rep: 4 (over y, x), fsdp: 8 (over z, core).
Axes of the slice: x: 2, y: 2, z: 4, core: 2. Of those that a mesh axis runs over, the one named last changes fastest.
Arguments:
- content_stream: bfloat16 [64, 512, 768], P(('rep', 'fsdp')), may hold values from -6 to 6
- query_stream: bfloat16 [64, 512, 768], P(('rep', 'fsdp')), may hold values from -6 to 6
- lengths: int32 [64], P(('rep', 'fsdp')), may hold values from 64 to 512, as said below
- factor_order: int32 [64, 512], P(('rep', 'fsdp')), may hold values from 0 to 511, each once within a row
- qkv_weight: float32 [768, 2304], P('fsdp'), may hold values from -0.21875 to 0.21875
- qv_bias: float32 [1536], P('fsdp'), may hold values from -3 to 3
- out_weight: float32 [768, 768], P('fsdp'), may hold values from -0.625 to 0.625
- out_bias: float32 [768], P('fsdp'), may hold values from -2 to 2
- norm1_gain: float32 [768], P('fsdp'), may hold values from 0.5 to 1.5
- norm1_bias: float32 [768], P('fsdp'), may hold values from -2 to 2
- rel_table: float32 [32, 12], P('fsdp'), may hold values from -4 to 4
- ffn_in_weight: float32 [768, 3072], P('fsdp'), may hold values from -0.21875 to 0.21875
- ffn_in_bias: float32 [3072], P('fsdp'), may hold values from -2 to 2
- ffn_out_weight: float32 [3072, 768], P('fsdp'), may hold values from -0.109375 to 0.109375
- ffn_out_bias: float32 [768], P('fsdp'), may hold values from -2 to 2
- norm2_gain: float32 [768], P('fsdp'), may hold values from 0.5 to 1.5
- norm2_bias: float32 [768], P('fsdp'), may hold values from -2 to 2
- content_cot: bfloat16 [64, 512, 768], P(('rep', 'fsdp')), may hold values from -6 to 6
- query_cot: bfloat16 [64, 512, 768], P(('rep', 'fsdp')), may hold values from -6 to 6
Outputs:
- content_out: bfloat16 [64, 512, 768], P(('rep', 'fsdp'))
- query_out: bfloat16 [64, 512, 768], P(('rep', 'fsdp'))
- content_grad: bfloat16 [64, 512, 768], P(('rep', 'fsdp'))
- query_grad: bfloat16 [64, 512, 768], P(('rep', 'fsdp'))
- qkv_weight_grad: float32 [768, 2304], P('fsdp')
- qv_bias_grad: float32 [1536], P('fsdp')
- out_weight_grad: float32 [768, 768], P('fsdp')
- out_bias_grad: float32 [768], P('fsdp')
- norm1_gain_grad: float32 [768], P('fsdp')
- norm1_bias_grad: float32 [768], P('fsdp')
- rel_table_grad: float32 [32, 12], P('fsdp')
- ffn_in_weight_grad: float32 [768, 3072], P('fsdp')
- ffn_in_bias_grad: float32 [3072], P('fsdp')
- ffn_out_weight_grad: float32 [3072, 768], P('fsdp')
- ffn_out_bias_grad: float32 [768], P('fsdp')
- norm2_gain_grad: float32 [768], P('fsdp')
- norm2_bias_grad: float32 [768], P('fsdp')
The draws below stay inside these ranges and needn't reach their ends.
Inputs may be any that keep to these rules, and one draw needn't show every extreme that they name: `lengths`: the first sequence of the batch has 512 real tokens. `factor_order`: each row is a permutation of the positions.
All inputs are finite; a program needn't handle non-finite values.
Results may differ from the reference program's by a relative error of at most 0.02.
Values may be sent and summed in bfloat16 or wider, within the bound.
A program may use at most 320 MiB of HBM per device.

```python
import math
import jax
import jax.numpy as jnp
import numpy as np
from jax import lax

D = 768
HEADS = 12
HEAD = 64
FF = 3072
BUCKETS = 32
MAX_DIST = 128
LEN = 512
SEQS = 64


def draw_lengths(key, part):
    spread_top = math.isqrt(LEN * 7 // 8) + 1
    shortfall = jax.random.randint(key, (SEQS,), 0, spread_top)
    drawn = LEN - shortfall * shortfall
    return drawn.at[0].set(LEN).astype(jnp.int32)


def with_spikes(values, key, source, target, shards_of, factor):
    def block_of(dim):
        return (jnp.arange(values.shape[dim]) // (values.shape[dim] // shards_of)).reshape((-1,) + (1,) * (values.ndim - 1 - dim))

    near = jax.random.permutation(key, shards_of)[block_of(target)]
    other_side = (block_of(target) + shards_of // 2) % shards_of
    return jnp.where((block_of(source) == near) | (block_of(source) == other_side), factor * values, values)


def block_scale(rng, dims, pieces, least, top_value):
    def one(axis_at, blocks):
        steps = jax.random.uniform(jax.random.fold_in(jax.random.fold_in(rng, 6), axis_at), (blocks,), jnp.float32, least / len(pieces), top_value / len(pieces))
        return jnp.repeat(jnp.exp(steps), dims[axis_at] // blocks).reshape((-1,) + (1,) * (len(dims) - axis_at - 1))

    factor_of = one(*pieces[0])
    for cut in pieces[1:]:
        factor_of = factor_of * one(*cut)
    return factor_of


def bell_draw(key, extent, scale, most, cuts=(), kind=jnp.bfloat16):
    values = jax.random.normal(key, extent, jnp.float32) * scale
    if len(cuts) > 0:
        values = block_scale(key, extent, cuts, -0.22, 0.18) * values
    return jnp.clip(values, min=-most, max=most).astype(kind)


def bell_draw_with(own_key, shape, scale, most, pieces, heavy, kind=jnp.bfloat16):
    values = scale * jax.random.normal(own_key, shape, jnp.float32)
    if pieces:
        values = values * block_scale(own_key, shape, pieces, -0.22, 0.18)
    return jnp.clip(with_spikes(values, jax.random.fold_in(own_key, 3), *heavy), -most, most).astype(kind)


def setup_inputs(seed: int = 0) -> dict:
    seeds = jax.random.split(jax.random.key(seed), 20)
    content_stream = bell_draw(seeds[0], (SEQS, LEN, D), 1.0, 6.0, ((0, 32),))
    query_stream = bell_draw(seeds[1], (SEQS, LEN, D), 1.0, 6.0, ((0, 32),))
    lengths = draw_lengths(jax.random.fold_in(seeds[19], 71), 0)
    factor_order = jax.vmap(lambda own: jax.random.permutation(own, LEN))(jax.random.split(seeds[3], SEQS)).reshape((SEQS, LEN)).astype(jnp.int32)
    qkv_weight = bell_draw(seeds[4], (D, 3 * D), D ** -0.5, 0.21875, ((0, 8),), jnp.float32)
    qv_bias = bell_draw(seeds[5], (2 * D,), 0.5, 3.0, ((0, 8),), jnp.float32)
    out_weight = bell_draw(seeds[6], (D, D), (D // 8) ** -0.5, 0.625, ((0, 8),), jnp.float32)
    out_bias = bell_draw(seeds[7], (D,), 0.3, 2.0, ((0, 8),), jnp.float32)
    norm1_gain = jnp.clip(1.0 + 0.1 * jax.random.normal(seeds[8], (D,), jnp.float32), 0.5, 1.5)
    norm1_bias = bell_draw(seeds[9], (D,), 0.3, 2.0, ((0, 8),), jnp.float32)
    rel_table = bell_draw(seeds[10], (BUCKETS, HEADS), 1.0, 4.0, ((0, 8),), jnp.float32)
    ffn_in_weight = bell_draw(seeds[11], (D, FF), D ** -0.5, 0.21875, ((0, 8),), jnp.float32)
    ffn_in_bias = bell_draw(seeds[12], (FF,), 0.3, 2.0, ((0, 8),), jnp.float32)
    ffn_out_weight = bell_draw(seeds[13], (FF, D), FF ** -0.5, 0.109375, ((0, 8),), jnp.float32)
    ffn_out_bias = bell_draw(seeds[14], (D,), 0.3, 2.0, ((0, 8),), jnp.float32)
    norm2_gain = jnp.clip(1.0 + 0.1 * jax.random.normal(seeds[15], (D,), jnp.float32), 0.5, 1.5)
    norm2_bias = bell_draw(seeds[16], (D,), 0.3, 2.0, ((0, 8),), jnp.float32)
    content_cot = bell_draw_with(seeds[17], (SEQS, LEN, D), 1.0, 6.0, ((0, 32),), (0, 2, 32, 2.75))
    query_cot = bell_draw(seeds[18], (SEQS, LEN, D), 1.0, 6.0, ((0, 32),))
    return dict(content_stream=content_stream, query_stream=query_stream, lengths=lengths, factor_order=factor_order, qkv_weight=qkv_weight, qv_bias=qv_bias, out_weight=out_weight, out_bias=out_bias, norm1_gain=norm1_gain, norm1_bias=norm1_bias, rel_table=rel_table, ffn_in_weight=ffn_in_weight, ffn_in_bias=ffn_in_bias, ffn_out_weight=ffn_out_weight, ffn_out_bias=ffn_out_bias, norm2_gain=norm2_gain, norm2_bias=norm2_bias, content_cot=content_cot, query_cot=query_cot)


@jax.custom_vjp
def low(v):
    return lax.optimization_barrier(v.astype(jnp.bfloat16)).astype(jnp.float32)

@jax.custom_vjp
def low_back(v):
    return v

def low_keep(v):
    return (low(v), None)

def low_pass(kept, grad):
    return (grad,)

def back_keep(v):
    return (v, None)

def back_low(kept, grad):
    return (low(grad),)
low.defvjp(low_keep, low_pass)
low_back.defvjp(back_keep, back_low)
eps_norm = 1e-05
root_half = 0.7071067811865476

def both_round(value):
    return low(low_back(value))

def exact_dot(left_op, right_op):
    return jnp.dot(left_op, right_op, precision=lax.Precision.HIGHEST, preferred_element_type=jnp.float32)

def relative_buckets(length):
    places = np.arange(length)
    offset = places[:, None] - places[None, :]
    half_count = BUCKETS // 2
    result = (offset < 0).astype(np.int64) * half_count
    distance = np.abs(offset)
    exact_count = half_count // 2
    fraction = np.log(np.maximum(distance, 1) / exact_count) / np.log(MAX_DIST / exact_count)
    beyond = exact_count + (fraction * (half_count - exact_count)).astype(np.int64)
    beyond = np.minimum(beyond, half_count - 1)
    result = result + np.where(distance < exact_count, distance, beyond)
    return result.astype(np.int32)

def layer_norm(summed, gain_vec, shift_vec):
    row_mean = lax.optimization_barrier(jnp.mean(summed, -1, keepdims=True))
    centered = summed - row_mean
    variance = lax.optimization_barrier(jnp.mean(centered * centered, -1, keepdims=True))
    return centered * lax.rsqrt(variance + eps_norm) * gain_vec + shift_vec

def gelu_value(hidden_in):
    return 0.5 * hidden_in * (1.0 + jax.scipy.special.erf(hidden_in * root_half))

def key_masks(length_one, rank_row):
    places = jnp.arange(rank_row.shape[0])
    visible = (places < length_one)[None, :]
    first_key = (places == 0)[None, :]
    content_mask = visible & (first_key | (rank_row[None, :] <= rank_row[:, None]))
    query_mask = visible & (first_key | (rank_row[None, :] < rank_row[:, None]))
    return (content_mask, query_mask)

def attend(query_block, key_block, value_block, bias_full, allowed_mask):
    score_scale = 1.0 / math.sqrt(HEAD)
    logits = low_back(jnp.einsum('ihd,jhd->hij', query_block, key_block, precision=lax.Precision.HIGHEST) * score_scale) + bias_full
    logits = jnp.where(allowed_mask[None], logits, -jnp.inf)
    row_max = lax.optimization_barrier(jnp.max(logits, -1, keepdims=True))
    exp_scores = jnp.exp(logits - row_max)
    attn_probs = exp_scores / lax.optimization_barrier(jnp.sum(exp_scores, -1, keepdims=True))
    mixed_heads = jnp.einsum('hij,jhd->ihd', low(attn_probs), value_block, precision=lax.Precision.HIGHEST)
    return both_round(mixed_heads.reshape(query_block.shape[0], -1))

def group_forward(params, content_in, query_in, length_part, order_part, buckets):
    joined_proj, proj_shift, out_proj, out_shift, gain_one, shift_one, bias_table, in_proj, in_shift, out_ffn, ffn_shift, gain_two, shift_two = [low(parameter) for parameter in params]
    group_size, seq_len, width = content_in.shape
    row_count = group_size * seq_len
    head_width = width // HEADS
    content_rows = content_in.reshape(row_count, width)
    query_rows = query_in.reshape(row_count, width)
    content_proj = exact_dot(content_rows, joined_proj)
    content_queries = both_round(content_proj[:, :width] + proj_shift[:width])
    content_keys = both_round(content_proj[:, width:2 * width])
    content_values = both_round(content_proj[:, 2 * width:] + proj_shift[width:])
    stream_queries = both_round(exact_dot(query_rows, joined_proj[:, :width]) + proj_shift[:width])
    bias_full = jnp.transpose(bias_table[buckets], (2, 0, 1))

    def shaped(rows_in):
        return rows_in.reshape(group_size, seq_len, HEADS, head_width)

    def attend_pair(entries):
        own_query, own_keys, own_values, other_query, length_one, rank_row = entries
        content_mask, query_mask = key_masks(length_one, rank_row)
        return (attend(own_query, own_keys, own_values, bias_full, content_mask), attend(other_query, own_keys, own_values, bias_full, query_mask))
    mixed_content, mixed_query = lax.map(jax.checkpoint(attend_pair), (shaped(content_queries), shaped(content_keys), shaped(content_values), shaped(stream_queries), length_part, order_part))
    mixed_rows = jnp.concatenate([mixed_content.reshape(row_count, width), mixed_query.reshape(row_count, width)], 0)
    input_rows = jnp.concatenate([content_rows, query_rows], 0)
    branch = low_back(exact_dot(mixed_rows, out_proj) + out_shift)
    first_low = low(layer_norm(input_rows + branch, gain_one, shift_one))
    hidden_in = low_back(exact_dot(first_low, in_proj) + in_shift)
    hidden_low = low(gelu_value(hidden_in))
    ffn_rows = low_back(exact_dot(hidden_low, out_ffn) + ffn_shift)
    final_rows = layer_norm(first_low + ffn_rows, gain_two, shift_two)
    return (final_rows[:row_count].reshape(group_size, seq_len, width), final_rows[row_count:].reshape(group_size, seq_len, width))

def reference(content_stream, query_stream, lengths, factor_order, qkv_weight, qv_bias, out_weight, out_bias, norm1_gain, norm1_bias, rel_table, ffn_in_weight, ffn_in_bias, ffn_out_weight, ffn_out_bias, norm2_gain, norm2_bias, content_cot, query_cot):
    params = (qkv_weight, qv_bias, out_weight, out_bias, norm1_gain, norm1_bias, rel_table, ffn_in_weight, ffn_in_bias, ffn_out_weight, ffn_out_bias, norm2_gain, norm2_bias)
    group_size = math.gcd(SEQS, 8)
    blocks = SEQS // group_size
    buckets = jnp.asarray(relative_buckets(LEN))
    valid_rows = (jnp.arange(LEN)[None, :] < lengths[:, None]).astype(jnp.float32)[..., None]

    def grouped(array_in):
        return array_in.reshape((blocks, group_size) + array_in.shape[1:])
    inputs = (grouped(content_stream.astype(jnp.float32)), grouped(query_stream.astype(jnp.float32)), grouped(lengths), grouped(factor_order), grouped(content_cot.astype(jnp.float32) * valid_rows), grouped(query_cot.astype(jnp.float32) * valid_rows))

    def scan_step(totals, entries):
        content_in, query_in, length_part, order_part, cot_content, cot_query = entries

        def forward(params_in, content_arg, query_arg):
            return group_forward(params_in, content_arg, query_arg, length_part, order_part, buckets)
        outputs, pullback = jax.vjp(forward, params, content_in, query_in)
        grad_params, grad_content, grad_query = pullback((cot_content, cot_query))
        return (jax.tree.map(jnp.add, totals, grad_params), (outputs[0], outputs[1], grad_content, grad_query))
    starts = tuple((jnp.zeros_like(parameter) for parameter in params))
    totals, (out_content, out_query, grad_content, grad_query) = lax.scan(scan_step, starts, inputs)

    def whole(array_in):
        return array_in.reshape(SEQS, LEN, D).astype(jnp.bfloat16)
    return (whole(out_content), whole(out_query), whole(grad_content), whole(grad_query), totals[0], totals[1], totals[2], totals[3], totals[4], totals[5], totals[6], totals[7], totals[8], totals[9], totals[10], totals[11], totals[12])
```

```python
import functools, math
import jax, jax.numpy as jnp, numpy as np
from jax import lax
from jax.experimental import pallas as pl
from jax.experimental.pallas import tpu as pltpu
from jax.sharding import PartitionSpec as P

HEADS = 12
HEAD = 64
BUCKETS = 32
MAX_DIST = 128
LANE = 128
NEAR = 512
MASKED = -1e30
LOG2E = 1.4426950408889634
LN2 = 0.6931471805599453
F32 = jnp.float32
BF16 = jnp.bfloat16


def bucket_of(offset):
    half_count = BUCKETS // 2
    result = (offset < 0).astype(np.int64) * half_count
    distance = np.abs(offset)
    exact_count = half_count // 2
    fraction = np.log(np.maximum(distance, 1) / exact_count) / np.log(MAX_DIST / exact_count)
    beyond = exact_count + (fraction * (half_count - exact_count)).astype(np.int64)
    beyond = np.minimum(beyond, half_count - 1)
    result = result + np.where(distance < exact_count, distance, beyond)
    return result.astype(np.int32)


def nt(a, b):
    return lax.dot_general(a, b, (((1,), (1,)), ((), ())), preferred_element_type=F32)


def nn(a, b):
    return lax.dot_general(a, b, (((1,), (0,)), ((), ())), preferred_element_type=F32)


def signed_places():
    places = np.arange(NEAR)
    return np.where(places < NEAR - LANE + 0, places, places - NEAR)


def near_onehot(sign):
    offset = sign * (signed_places() - LANE)
    return (bucket_of(offset)[None, :] == np.arange(BUCKETS)[:, None]).astype(np.float32)


def skewed(row, width):
    wide = jnp.broadcast_to(row, (LANE, NEAR))
    return pltpu.roll(wide, 0, 1, stride=1, stride_axis=0)[:, :width]


def tile_bias(near, far_pos, far_neg, seq_len, sign):
    blocks = seq_len // LANE
    rows = []
    for rb in range(blocks):
        parts = []
        for cb in range(blocks):
            e = cb - rb
            if abs(e) <= 1:
                parts.append(near[:, (e + 1) * LANE : (e + 2) * LANE])
            else:
                parts.append(jnp.broadcast_to(far_pos if e * sign > 0 else far_neg, (LANE, LANE)))
        rows.append(jnp.concatenate(parts, 1))
    return rows


def head_lanes(shape, t):
    lane = lax.broadcasted_iota(jnp.int32, shape, 1)
    return (lane >= t * HEAD) & (lane < (t + 1) * HEAD)


def fwd_kernel(len_ref, q_ref, k_ref, v_ref, g_ref, ord_ref, near_ref, far_ref, oc_ref, og_ref, lc_ref, lg_ref, mask_ref):
    hp = pl.program_id(0)
    s = pl.program_id(1)
    seq_len = q_ref.shape[0]
    blocks = seq_len // LANE

    @pl.when(hp == 0)
    def _():
        own = ord_ref[pl.ds(s, 1), :].astype(F32)
        cols = jnp.broadcast_to(own, (LANE, seq_len)).T
        place = lax.broadcasted_iota(jnp.int32, (LANE, seq_len), 1)
        keep = place < len_ref[s]
        for rb in range(blocks):
            col = cols[rb * LANE : (rb + 1) * LANE, :]
            rank = jnp.concatenate([col] * blocks, 1)
            ok = keep & ((place == 0) | (own <= rank))
            mask_ref[s, rb * LANE : (rb + 1) * LANE, :] = jnp.where(ok, 0.0, MASKED)

    keys = k_ref[...]
    values = jnp.concatenate([v_ref[...], jnp.ones((seq_len, LANE), BF16)], 1)
    lane = lax.broadcasted_iota(jnp.int32, (seq_len, LANE), 1)
    outs = [[], []]
    totals = [jnp.zeros((seq_len, LANE), F32), jnp.zeros((seq_len, LANE), F32)]
    for t in range(2):
        head = hp * 2 + t
        sel = head_lanes((seq_len, LANE), t)
        near = skewed(near_ref[pl.ds(head, 1), :], 3 * LANE)
        far = far_ref[pl.ds(head, 1), :]
        bias = tile_bias(near, far[:, 0:1], far[:, 1:2], seq_len, -1)
        for stream in range(2):
            src = q_ref if stream == 0 else g_ref
            query = jnp.where(sel, src[...], jnp.zeros((), BF16))
            raw = nt(query, keys)
            probs = []
            maxes = []
            for rb in range(blocks):
                part = raw[rb * LANE : (rb + 1) * LANE, :] + (bias[rb] + mask_ref[s, rb * LANE : (rb + 1) * LANE, :])
                if stream == 1:
                    r = lax.broadcasted_iota(jnp.int32, (LANE, LANE), 0)
                    c = lax.broadcasted_iota(jnp.int32, (LANE, LANE), 1)
                    hit = r == c
                    if rb == 0:
                        hit = hit & (c != 0)
                    diag = jnp.where(hit, MASKED, part[:, rb * LANE : (rb + 1) * LANE])
                    pieces = []
                    if rb > 0:
                        pieces.append(part[:, : rb * LANE])
                    pieces.append(diag)
                    if rb < blocks - 1:
                        pieces.append(part[:, (rb + 1) * LANE :])
                    part = jnp.concatenate(pieces, 1)
                top = jnp.max(part, 1, keepdims=True)
                probs.append(jnp.exp2(part - top).astype(BF16))
                maxes.append(jnp.broadcast_to(top, (LANE, LANE)))
            prob = jnp.concatenate(probs, 0)
            mixed = nn(prob, values)
            total = mixed[:, LANE:]
            outs[stream].append(mixed[:, :LANE] / total)
            log_total = jnp.concatenate(maxes, 0) + jnp.log2(total)
            hi = log_total.astype(BF16).astype(F32)
            totals[stream] = jnp.where(lane == head, -hi, jnp.where(lane == head + HEAD, hi - log_total, totals[stream]))
    first = head_lanes((seq_len, LANE), 0)
    oc_ref[...] = jnp.where(first, outs[0][0], outs[0][1]).astype(BF16)
    og_ref[...] = jnp.where(first, outs[1][0], outs[1][1]).astype(BF16)
    mine = (lane == hp * 2) | (lane == hp * 2 + 1) | (lane == hp * 2 + HEAD) | (lane == hp * 2 + 1 + HEAD)
    for ref, total in ((lc_ref, totals[0]), (lg_ref, totals[1])):
        low = total.astype(BF16)

        @pl.when(hp == 0)
        def _():
            ref[s] = low

        @pl.when(hp > 0)
        def _():
            ref[s] = jnp.where(mine, low, ref[s])


def attention_forward(qkv, qg, lengths, order, table):
    rows, width = qg.shape
    seqs, seq_len = order.shape
    pairs = width // LANE
    near = jnp.dot(table.astype(F32).T, jnp.asarray(near_onehot(-1)), precision=lax.Precision.HIGHEST) * LOG2E
    tab2 = table.astype(F32).T * LOG2E
    far = jnp.concatenate([tab2[:, BUCKETS // 2 - 1 : BUCKETS // 2], tab2[:, BUCKETS - 1 : BUCKETS]], 1)
    block = lambda off: pl.BlockSpec((seq_len, LANE), lambda h, s, off=off: (s, off + h))
    whole = lambda a: pl.BlockSpec(a.shape, lambda h, s: (0,) * a.ndim)
    return pl.pallas_call(
        fwd_kernel,
        grid=(pairs, seqs),
        in_specs=[
            pl.BlockSpec(memory_space=pltpu.SMEM),
            block(0), block(pairs), block(2 * pairs), block(0),
            whole(order), whole(near), whole(far),
        ],
        out_specs=[block(0), block(0),
                   pl.BlockSpec((seqs, seq_len, LANE), lambda h, s: (0, 0, 0)),
                   pl.BlockSpec((seqs, seq_len, LANE), lambda h, s: (0, 0, 0))],
        out_shape=[jax.ShapeDtypeStruct((rows, width), BF16)] * 2 + [jax.ShapeDtypeStruct((seqs, seq_len, LANE), BF16)] * 2,
        scratch_shapes=[pltpu.VMEM((seqs, seq_len, seq_len), F32)],
        compiler_params=pltpu.CompilerParams(dimension_semantics=("arbitrary", "arbitrary"), vmem_limit_bytes=56 * 2**20),
        name="attention_forward",
    )(lengths, qkv, qkv, qkv, qg, order, near, far)


def bwd_kernel(len_ref, q_ref, k_ref, v_ref, g_ref, dc_ref, dg_ref, oc_ref, og_ref, lc_ref, lg_ref, ord_ref, near_ref, far_ref,
               dq_ref, dk_ref, dv_ref, dqg_ref, sums_ref, mask_ref, acc_ref, ds_ref):
    hp = pl.program_id(0)
    s = pl.program_id(1)
    last = pl.num_programs(1) - 1
    seq_len = q_ref.shape[0]
    blocks = seq_len // LANE
    half = seq_len // 2

    @pl.when(hp == 0)
    def _():
        own = ord_ref[pl.ds(s, 1), :].astype(F32)
        cols = jnp.broadcast_to(own, (LANE, seq_len)).T
        for rb in range(blocks):
            col = cols[rb * LANE : (rb + 1) * LANE, :]
            rank = jnp.concatenate([col] * blocks, 1)
            place = lax.broadcasted_iota(jnp.int32, (LANE, seq_len), 0) + rb * LANE
            ok = (place < len_ref[s]) & ((place == 0) | (rank <= own))
            mask_ref[s, rb * LANE : (rb + 1) * LANE, :] = jnp.where(ok, 0.0, MASKED)

    lane = lax.broadcasted_iota(jnp.int32, (seq_len, LANE), 1)
    ones = jnp.ones((seq_len, LANE), BF16)
    zero = jnp.zeros((), BF16)
    keys = k_ref[...]
    keys_wide = jnp.concatenate([keys, ones], 1)
    values_wide = jnp.concatenate([v_ref[...], ones], 1)
    keys_turned = keys.astype(F32).T.astype(BF16)
    lane_r = lax.broadcasted_iota(jnp.int32, (LANE, LANE), 0)
    lane_c = lax.broadcasted_iota(jnp.int32, (LANE, LANE), 1)
    pick = (lane_r // HEAD == lane_c).astype(BF16)
    grad_keys = None
    grad_values = None
    grad_query = [[], []]
    streams = []
    for src, grad, out, tot in ((q_ref, dc_ref, oc_ref, lc_ref), (g_ref, dg_ref, og_ref, lg_ref)):
        g = grad[...]
        delta = nn((g.astype(F32) * out[...].astype(F32)).astype(BF16), pick)
        hi = delta.astype(BF16)
        streams.append((src[...], g, -delta, tot[0]))
    for t in range(2):
        head = hp * 2 + t
        sel = head_lanes((seq_len, LANE), t)
        near = skewed(near_ref[pl.ds(head, 1), :], 3 * LANE)
        far = far_ref[pl.ds(head, 1), :]
        bias = tile_bias(near, far[:, 0:1], far[:, 1:2], seq_len, 1)
        for c0 in range(0, seq_len, half):
            both = None
            for stream in range(2):
                q, g, delta, tot = streams[stream]
                q = jnp.where(sel, q, zero)[c0 : c0 + half]
                g = jnp.where(sel, g, zero)[c0 : c0 + half]
                d = delta[c0 : c0 + half]
                ln = lane[c0 : c0 + half]
                tt = jnp.where((ln == head) | (ln == head + HEAD), tot[c0 : c0 + half], zero)
                dd = jnp.where(ln == t, d, 0.0)
                dhi = dd.astype(BF16)
                dlo = pltpu.roll(dd - dhi.astype(F32), HEAD, 1).astype(BF16)
                raw = nt(keys_wide, jnp.concatenate([q, tt], 1))
                dpr = nt(values_wide, jnp.concatenate([g, dhi + dlo], 1))
                probs, grads = [], []
                for rb in range(blocks):
                    sl = slice(rb * LANE, (rb + 1) * LANE)
                    part = raw[sl] + (bias[rb][:, c0 : c0 + half] + mask_ref[s, sl, c0 : c0 + half])
                    r0 = rb * LANE
                    if stream == 1 and c0 <= r0 < c0 + half:
                        hit = lane_r == lane_c
                        if rb == 0:
                            hit = hit & (lane_r != 0)
                        x0 = r0 - c0
                        diag = jnp.where(hit, MASKED, part[:, x0 : x0 + LANE])
                        pieces = []
                        if x0 > 0:
                            pieces.append(part[:, :x0])
                        pieces.append(diag)
                        if x0 + LANE < half:
                            pieces.append(part[:, x0 + LANE :])
                        part = jnp.concatenate(pieces, 1)
                    p = jnp.exp2(part)
                    probs.append(p.astype(BF16))
                    grads.append(p * dpr[sl])
                low = [x.astype(BF16) for x in grads]
                prob = jnp.concatenate(probs, 0)
                gl = jnp.concatenate(low, 0)
                gv = nn(prob, g)
                gk = nn(gl, q)
                grad_values = gv if grad_values is None else grad_values + gv
                grad_keys = gk if grad_keys is None else grad_keys + gk
                grad_query[stream].append(nn(keys_turned[t * HEAD : (t + 1) * HEAD], gl))
                both = grads if both is None else [a + b for a, b in zip(both, grads)]
            sums = {}
            for rb in range(blocks):
                for cb in range(half // LANE):
                    e = cb + c0 // LANE - rb
                    e = max(-2, min(2, e))
                    x = both[rb][:, cb * LANE : (cb + 1) * LANE]
                    sums[e] = x if e not in sums else sums[e] + x
            for e, x in sums.items():
                lanes = slice((e + 2) * LANE, (e + 3) * LANE)
                fresh = c0 == 0
                if fresh:
                    @pl.when(s == 0)
                    def _():
                        acc_ref[t, :, lanes] = x

                    @pl.when(s > 0)
                    def _():
                        acc_ref[t, :, lanes] = acc_ref[t, :, lanes] + x
                else:
                    acc_ref[t, :, lanes] = acc_ref[t, :, lanes] + x
            if c0 == 0:
                for e in range(-2, 3):
                    if e not in sums:
                        @pl.when(s == 0)
                        def _():
                            acc_ref[t, :, (e + 2) * LANE : (e + 3) * LANE] = jnp.zeros((LANE, LANE), F32)
    count = seq_len // half
    scale = 1.0 / math.sqrt(HEAD)
    for stream, ref in ((0, dq_ref), (1, dqg_ref)):
        pieces = grad_query[stream]
        top = jnp.concatenate(pieces[:count], 1)
        bot = jnp.concatenate(pieces[count:], 1)
        ref[...] = (jnp.concatenate([top, bot], 0) * scale).T.astype(BF16)
    dk_ref[...] = (grad_keys * LN2).astype(BF16)
    dv_ref[...] = grad_values.astype(BF16)

    @pl.when(s == last)
    def _():
        for t in range(2):
            near = jnp.concatenate([acc_ref[t, :, LANE : 4 * LANE], jnp.zeros((LANE, LANE), F32)], 1)
            mirror = (lane_r + lane_c == LANE - 1).astype(F32)
            flipped = lax.dot_general(mirror, near, (((1,), (0,)), ((), ())), precision=lax.Precision.HIGHEST, preferred_element_type=F32)
            turned = pltpu.roll(flipped, 0, 1, stride=1, stride_axis=0)
            row = jnp.sum(turned, 0, keepdims=True)
            below = jnp.sum(acc_ref[t, :, :LANE], 0, keepdims=True)
            above = jnp.sum(acc_ref[t, :, 4 * LANE :], 0, keepdims=True)
            sums_ref[pl.ds(hp * 2 + t, 1), :] = jnp.concatenate([row, below, above], 1)


def attention_backward(qkv, qg, grad_c, grad_g, out_c, out_g, tot_c, tot_g, lengths, order, table):
    rows, width = qg.shape
    seqs, seq_len = order.shape
    pairs = width // LANE
    near = jnp.dot(table.astype(F32).T, jnp.asarray(near_onehot(1)), precision=lax.Precision.HIGHEST) * LOG2E
    tab2 = table.astype(F32).T * LOG2E
    far = jnp.concatenate([tab2[:, BUCKETS // 2 - 1 : BUCKETS // 2], tab2[:, BUCKETS - 1 : BUCKETS]], 1)
    block = lambda off: pl.BlockSpec((seq_len, LANE), lambda h, s, off=off: (s, off + h))
    whole = lambda a: pl.BlockSpec(a.shape, lambda h, s: (0,) * a.ndim)
    tot = pl.BlockSpec((1, seq_len, LANE), lambda h, s: (s, 0, 0))
    outs = pl.pallas_call(
        bwd_kernel,
        grid=(pairs, seqs),
        in_specs=[
            pl.BlockSpec(memory_space=pltpu.SMEM),
            block(0), block(pairs), block(2 * pairs), block(0),
            block(0), block(0), block(0), block(0), tot, tot,
            whole(order), whole(near), whole(far),
        ],
        out_specs=[block(0)] * 4 + [pl.BlockSpec((2 * pairs, NEAR + 2 * LANE), lambda h, s: (0, 0))],
        out_shape=[jax.ShapeDtypeStruct((rows, width), BF16)] * 4 + [jax.ShapeDtypeStruct((2 * pairs, NEAR + 2 * LANE), F32)],
        scratch_shapes=[pltpu.VMEM((seqs, seq_len, seq_len), F32), pltpu.VMEM((2, LANE, 5 * LANE), F32), pltpu.VMEM((8, LANE), F32)],
        compiler_params=pltpu.CompilerParams(dimension_semantics=("arbitrary", "arbitrary"), vmem_limit_bytes=56 * 2**20),
        name="attention_backward",
    )(lengths, qkv, qkv, qkv, qg, grad_c, grad_g, out_c, out_g, tot_c, tot_g, order, near, far)
    sums = outs[4]
    fold = np.zeros((NEAR + 2 * LANE, BUCKETS), np.float32)
    fold[:NEAR] = np.roll(near_onehot(1).T, LANE - 1, 0)
    fold[NEAR : NEAR + LANE, BUCKETS - 1] = 1
    fold[NEAR + LANE :, BUCKETS // 2 - 1] = 1
    grad_table = jnp.dot(sums, jnp.asarray(fold), precision=lax.Precision.HIGHEST).T
    return list(outs[:4]) + [grad_table]


eps_norm = 1e-05
root_half = 0.7071067811865476
inv_root_tau = 0.3989422804014327


def norm_forward(summed, gain_vec, shift_vec):
    row_mean = jnp.mean(summed, -1, keepdims=True)
    centered = summed - row_mean
    inverse = lax.rsqrt(jnp.mean(centered * centered, -1, keepdims=True) + eps_norm)
    normed = centered * inverse
    return (normed * gain_vec + shift_vec, normed, inverse)


def norm_backward(upstream, normed, inverse, gain_vec):
    scaled = upstream * gain_vec
    centered = (
        scaled
        - jnp.mean(scaled, -1, keepdims=True)
        - normed * jnp.mean(scaled * normed, -1, keepdims=True)
    )
    return (inverse * centered, jnp.sum(upstream * normed, 0), jnp.sum(upstream, 0))


def gelu_value(hidden_in):
    return 0.5 * hidden_in * (1.0 + lax.erf(hidden_in * root_half))


def gelu_slope(hidden_in):
    return (
        0.5 * (1.0 + lax.erf(hidden_in * root_half))
        + hidden_in * jnp.exp(-0.5 * hidden_in * hidden_in) * inv_root_tau
    )


def rows_inner(left_op, right_op):
    return lax.dot_general(
        left_op, right_op, (((0,), (0,)), ((), ())), preferred_element_type=jnp.float32
    )


def times_transpose(left_op, right_op):
    return lax.dot_general(
        left_op, right_op, (((1,), (1,)), ((), ())), preferred_element_type=jnp.float32
    )


def pack(parts):
    flat = jnp.concatenate([p.reshape(-1) for p in parts])
    return jnp.pad(flat, (0, -flat.shape[0] % LANE))


def on_device(content_stream, query_stream, lengths, factor_order, qkv_weight, qv_bias, out_weight, out_bias, norm1_gain, norm1_bias, rel_table, ffn_in_weight, ffn_in_bias, ffn_out_weight, ffn_out_bias, norm2_gain, norm2_bias, content_cot, query_cot):
    seq_count, seq_len, width = content_stream.shape
    row_count = seq_count * seq_len
    gather = lambda a: lax.all_gather(a, "fsdp", axis=0, tiled=True)
    small = (qv_bias, out_bias, norm1_gain, norm1_bias, rel_table, ffn_in_bias, ffn_out_bias, norm2_gain, norm2_bias)
    packed = lax.all_gather(pack([p.astype(BF16) for p in small]), "fsdp", axis=0, tiled=False)
    full = []
    at = 0
    for p in small:
        full.append(packed[:, at : at + p.size].reshape((-1,) + p.shape[1:]).astype(F32))
        at += p.size
    proj_shift, out_shift, gain_one, shift_one, table, in_shift, ffn_shift, gain_two, shift_two = full
    joined_proj = gather(qkv_weight.astype(BF16))
    out_proj = gather(out_weight.astype(BF16))
    in_proj = gather(ffn_in_weight.astype(BF16))
    out_ffn = gather(ffn_out_weight.astype(BF16))
    content_rows = content_stream.reshape(row_count, width)
    query_rows = query_stream.reshape(row_count, width)
    scale = LOG2E / math.sqrt(HEAD)
    shift = jnp.concatenate([proj_shift[:width] * scale, jnp.zeros((width,), F32), proj_shift[width:]])
    factor = jnp.concatenate([jnp.full((width,), scale, F32), jnp.ones((2 * width,), F32)])
    qkv = (jnp.dot(content_rows, joined_proj, preferred_element_type=F32) * factor + shift).astype(BF16)
    qg = (jnp.dot(query_rows, joined_proj[:, :width], preferred_element_type=F32) * scale + shift[:width]).astype(BF16)
    mixed_c, mixed_g, tot_c, tot_g = attention_forward(qkv, qg, lengths, factor_order, table)
    mixed_rows = jnp.concatenate([mixed_c, mixed_g], 0)
    input_rows = jnp.concatenate([content_rows, query_rows], 0).astype(F32)
    branch = jnp.dot(mixed_rows, out_proj, preferred_element_type=F32) + out_shift
    first_out, normed_one, inverse_one = norm_forward(input_rows + branch, gain_one, shift_one)
    first_low = first_out.astype(BF16)
    hidden_in = jnp.dot(first_low, in_proj, preferred_element_type=F32) + in_shift
    hidden_low = gelu_value(hidden_in).astype(BF16)
    ffn_rows = jnp.dot(hidden_low, out_ffn, preferred_element_type=F32) + ffn_shift
    final_rows, normed_two, inverse_two = norm_forward(first_low.astype(F32) + ffn_rows, gain_two, shift_two)
    valid_rows = (jnp.arange(seq_len)[None, :] < lengths[:, None]).reshape(row_count, 1).astype(F32)
    valid_both = jnp.concatenate([valid_rows, valid_rows], 0)
    upstream = jnp.concatenate([content_cot.reshape(row_count, width), query_cot.reshape(row_count, width)], 0).astype(F32) * valid_both
    grad_sum_two, grad_gain_two, grad_shift_two = norm_backward(upstream, normed_two, inverse_two, gain_two)
    grad_ffn = grad_sum_two.astype(BF16)
    grad_ffn_shift = jnp.sum(grad_ffn.astype(F32), 0)
    grad_out_ffn = rows_inner(hidden_low, grad_ffn)
    grad_hidden = (times_transpose(grad_ffn, out_ffn) * gelu_slope(hidden_in)).astype(BF16)
    grad_in_shift = jnp.sum(grad_hidden.astype(F32), 0)
    grad_in_proj = rows_inner(first_low, grad_hidden)
    grad_first = grad_sum_two + times_transpose(grad_hidden, in_proj)
    scatter = lambda a: lax.psum_scatter(a.astype(BF16), "fsdp", scatter_dimension=0, tiled=True)
    part_in = scatter(grad_in_proj)
    part_out = scatter(grad_out_ffn)
    grad_sum_one, grad_gain_one, grad_shift_one = norm_backward(grad_first, normed_one, inverse_one, gain_one)
    grad_branch = grad_sum_one.astype(BF16)
    grad_out_shift = jnp.sum(grad_branch.astype(F32), 0)
    grad_out_proj = rows_inner(mixed_rows, grad_branch)
    part_proj = scatter(grad_out_proj)
    grad_mixed = times_transpose(grad_branch, out_proj).astype(BF16)
    grad_cq, grad_k, grad_v, grad_sq, grad_table = attention_backward(qkv, qg, grad_mixed[:row_count], grad_mixed[row_count:], mixed_c, mixed_g, tot_c, tot_g, lengths, factor_order, table)
    grad_joined_rows = jnp.concatenate([grad_cq, grad_k, grad_v], -1)
    grad_joined = rows_inner(content_rows, grad_joined_rows)
    grad_joined = jnp.concatenate([grad_joined[:, :width] + rows_inner(query_rows, grad_sq), grad_joined[:, width:]], 1)
    part_joined = scatter(grad_joined)
    grad_proj_shift = jnp.concatenate([jnp.sum(grad_cq.astype(F32), 0) + jnp.sum(grad_sq.astype(F32), 0), jnp.sum(grad_v.astype(F32), 0)])
    content_grad_rows = grad_sum_one[:row_count] + times_transpose(grad_joined_rows, joined_proj)
    query_grad_rows = grad_sum_one[row_count:] + times_transpose(grad_sq, joined_proj[:, :width])
    grads_small = (grad_proj_shift, grad_out_shift, grad_gain_one, grad_shift_one, grad_table, grad_in_shift, grad_ffn_shift, grad_gain_two, grad_shift_two)
    own = lax.axis_index("fsdp")
    packed_grads = jnp.concatenate([g.reshape(packed.shape[0], -1) for g in grads_small], 1)
    packed_grads = lax.psum(packed_grads, ("rep", "fsdp"))
    mine = lax.dynamic_slice_in_dim(packed_grads, own, 1, 0)[0]
    outs_small = []
    at = 0
    for p in small:
        outs_small.append(mine[at : at + p.size].reshape(p.shape))
        at += p.size
    g_shift, g_out_shift, g_gain_one, g_shift_one, g_table, g_in_shift, g_ffn_shift, g_gain_two, g_shift_two = outs_small
    over = lambda a: lax.psum(a, "rep").astype(F32)
    block_shape = (seq_count, seq_len, width)
    return (
        final_rows[:row_count].reshape(block_shape).astype(BF16),
        final_rows[row_count:].reshape(block_shape).astype(BF16),
        content_grad_rows.reshape(block_shape).astype(BF16),
        query_grad_rows.reshape(block_shape).astype(BF16),
        over(part_joined), g_shift, over(part_proj), g_out_shift, g_gain_one, g_shift_one, g_table,
        over(part_in), g_in_shift, over(part_out), g_ffn_shift, g_gain_two, g_shift_two,
    )


def solution(mesh):
    in_specs = (
        P(("rep", "fsdp"), None, None),
        P(("rep", "fsdp"), None, None),
        P(("rep", "fsdp")),
        P(("rep", "fsdp"), None),
        P("fsdp", None),
        P("fsdp"),
        P("fsdp", None),
        P("fsdp"),
        P("fsdp"),
        P("fsdp"),
        P("fsdp", None),
        P("fsdp", None),
        P("fsdp"),
        P("fsdp", None),
        P("fsdp"),
        P("fsdp"),
        P("fsdp"),
        P(("rep", "fsdp"), None, None),
        P(("rep", "fsdp"), None, None),
    )
    out_specs = (
        P(("rep", "fsdp"), None, None),
        P(("rep", "fsdp"), None, None),
        P(("rep", "fsdp"), None, None),
        P(("rep", "fsdp"), None, None),
        P("fsdp", None),
        P("fsdp"),
        P("fsdp", None),
        P("fsdp"),
        P("fsdp"),
        P("fsdp"),
        P("fsdp", None),
        P("fsdp", None),
        P("fsdp"),
        P("fsdp", None),
        P("fsdp"),
        P("fsdp"),
        P("fsdp"),
    )
    return jax.shard_map(
        on_device, mesh=mesh, in_specs=in_specs, out_specs=out_specs, check_vma=False
    )
```

```python
import functools
import math

import jax
import jax.numpy as jnp
import numpy as np
from jax import lax
from jax.experimental import pallas as pl
from jax.experimental.pallas import tpu as pltpu
from jax.sharding import PartitionSpec as P

HEADS = 12
HEAD = 64
BUCKETS = 32
MAX_DIST = 128
LANE = 128
NEAR = 512
ROWS = 16
TABLE_ROW = 12
MASKED = -1e30
LOG2E = 1.4426950408889634
LN2 = 0.6931471805599453
F32 = jnp.float32
BF16 = jnp.bfloat16
MESH = pl.DeviceIdType.MESH
VMEM_BYTES = 60 * 2**20
eps_norm = 1e-05
root_half = 0.7071067811865476
inv_root_tau = 0.3989422804014327


def bucket_of(offset):
    half_count = BUCKETS // 2
    result = (offset < 0).astype(np.int64) * half_count
    distance = np.abs(offset)
    exact_count = half_count // 2
    fraction = np.log(np.maximum(distance, 1) / exact_count) / np.log(MAX_DIST / exact_count)
    beyond = exact_count + (fraction * (half_count - exact_count)).astype(np.int64)
    beyond = np.minimum(beyond, half_count - 1)
    result = result + np.where(distance < exact_count, distance, beyond)
    return result.astype(np.int32)


def nt(a, b):
    return lax.dot_general(a, b, (((1,), (1,)), ((), ())), preferred_element_type=F32)


def nn(a, b):
    return lax.dot_general(a, b, (((1,), (0,)), ((), ())), preferred_element_type=F32)


def signed_places():
    places = np.arange(NEAR)
    return np.where(places < NEAR - LANE, places, places - NEAR)


def near_onehot(sign):
    offset = sign * (signed_places() - LANE)
    return (bucket_of(offset)[None, :] == np.arange(BUCKETS)[:, None]).astype(np.float32)


def skewed(row, width):
    wide = jnp.broadcast_to(row, (LANE, NEAR))
    return pltpu.roll(wide, 0, 1, stride=1, stride_axis=0)[:, :width]


def tile_bias(near, far_pos, far_neg, seq_len, sign):
    blocks = seq_len // LANE
    rows = []
    for rb in range(blocks):
        parts = []
        for cb in range(blocks):
            e = cb - rb
            if abs(e) <= 1:
                parts.append(near[:, (e + 1) * LANE : (e + 2) * LANE])
            else:
                parts.append(jnp.broadcast_to(far_pos if e * sign > 0 else far_neg, (LANE, LANE)))
        rows.append(jnp.concatenate(parts, 1))
    return rows


def head_lanes(shape, t):
    lane = lax.broadcasted_iota(jnp.int32, shape, 1)
    return (lane >= t * HEAD) & (lane < (t + 1) * HEAD)


def flip(v, m):
    a, b = v // 2, v % 2
    if m & 2:
        a = 1 - a
    if m & 1:
        b = 1 - b
    return a * 2 + b


def table_onehot(sign, shards):
    per_shard = BUCKETS // shards
    result = np.zeros((shards * ROWS, NEAR + LANE), np.float32)
    near = near_onehot(sign)
    for bucket in range(BUCKETS):
        row = bucket // per_shard * ROWS + TABLE_ROW + bucket % per_shard
        result[row, :NEAR] = near[bucket]
        result[row, NEAR] = bucket == BUCKETS // 2 - 1
        result[row, NEAR + 1] = bucket == BUCKETS - 1
    return jnp.asarray(result, BF16)


class Links:
    def __init__(self, send, recv):
        self.send, self.recv = send, recv
        self.r = lax.axis_index("rep")
        self.f = lax.axis_index("fsdp")
        self.y, self.x = self.r // 2, self.r % 2
        self.z, self.c = self.f // 2, self.f % 2
        self.xr, self.yr = flip(self.r, 1), flip(self.r, 2)
        self.sib = self.z * 2 + 1 - self.c

    def along(self, s):
        return ((self.z + s) % 4) * 2 + self.c

    def copy(self, at, src, dst, rep, fsdp):
        return pltpu.make_async_remote_copy(
            src_ref=src, dst_ref=dst, send_sem=self.send.at[at], recv_sem=self.recv.at[at],
            device_id={"rep": rep, "fsdp": fsdp}, device_id_type=MESH)

    def barrier(self):
        sem = pltpu.get_barrier_semaphore()
        peers = [(self.r, self.along(s)) for s in (1, 2, 3)]
        peers += [(self.xr, self.f), (self.yr, self.f), (self.r, self.sib)]
        for rep, fsdp in peers:
            pl.semaphore_signal(sem, inc=1, device_id={"rep": rep, "fsdp": fsdp}, device_id_type=MESH)
        pl.semaphore_wait(sem, len(peers))


def quarter_of(ref, rows, cols, owner, q, part=None):
    pr, pc = rows // 2, cols // 2
    r0, c0 = owner * rows + (q // 2) * pr, (q % 2) * pc
    if part is not None:
        if pr % 32 == 0:
            r0, pr = r0 + part * (pr // 2), pr // 2
        else:
            first = (pc // LANE + 1) // 2 * LANE
            c0, pc = (c0, first) if part == 0 else (c0 + first, pc - first)
    return ref.at[pl.ds(pl.multiple_of(r0, 16), pr), pl.ds(pl.multiple_of(c0, LANE), pc)]


class Gather(Links):
    SLOTS = 12

    def __init__(self, shapes, shards, fulls, send, recv):
        super().__init__(send, recv)
        self.shapes, self.shards, self.fulls = shapes, shards, fulls

    def z_send(self, w, s):
        rows, cols = self.shapes[w]
        src = quarter_of(self.shards[w], rows, cols, 0, self.r)
        dst = quarter_of(self.fulls[w], rows, cols, self.f, self.r)
        return self.copy((w, s, 0), src, dst, self.r, self.along(s))

    def hop(self, w, s, slot, q, rep, fsdp, part=None):
        rows, cols = self.shapes[w]
        place = quarter_of(self.fulls[w], rows, cols, self.along(4 - s), q, part)
        return self.copy((w, s, slot), place, place, rep, fsdp)

    def own_place(self, w):
        rows = self.shapes[w][0]
        return self.fulls[w].at[pl.ds(pl.multiple_of(self.f * rows, 16), rows), :]

    def own_sib(self, w):
        return self.copy((w, 0, 0), self.shards[w], self.own_place(w), self.r, self.sib)

    def own_here(self, w):
        return pltpu.make_async_copy(self.shards[w], self.own_place(w), self.send.at[w, 0, 1])

    def h_x(self, w, s):
        return self.hop(w, s, 1, self.r, self.xr, self.f)

    def h_y(self, w, s):
        return self.hop(w, s, 2, self.r, self.yr, self.f)

    def h_dy(self, w, s):
        return self.hop(w, s, 3, self.xr, self.yr, self.f, 0)

    def h_dx(self, w, s):
        return self.hop(w, s, 4, self.yr, self.xr, self.f, 1)

    def h_sib(self, w, s, m):
        return self.hop(w, s, 5 + m, flip(self.r, m), self.r, self.sib)

    def start(self, w):
        for s in (1, 2, 3):
            self.z_send(w, s).start()
        self.own_sib(w).start()
        self.own_here(w).start()

    def relay_z(self, w, s):
        self.z_send(w, s).wait_recv()
        self.h_x(w, s).start()
        self.h_y(w, s).start()
        self.h_sib(w, s, 0).start()

    def relay_xy(self, w, s):
        self.h_x(w, s).wait_recv()
        self.h_dy(w, s).start()
        self.h_sib(w, s, 1).start()
        self.h_y(w, s).wait_recv()
        self.h_dx(w, s).start()
        self.h_sib(w, s, 2).start()

    def relay_diag(self, w, s):
        self.h_dy(w, s).wait_recv()
        self.h_dx(w, s).wait_recv()
        self.h_sib(w, s, 3).start()

    def arrive(self, w):
        for s in (1, 2, 3):
            for m in range(4):
                self.h_sib(w, s, m).wait_recv()
        self.own_sib(w).wait_recv()
        self.own_here(w).wait()

    def drain(self, w):
        for s in (1, 2, 3):
            for d in (self.z_send(w, s), self.h_x(w, s), self.h_y(w, s), self.h_dy(w, s), self.h_dx(w, s)):
                d.wait_send()
            for m in range(4):
                self.h_sib(w, s, m).wait_send()
        self.own_sib(w).wait_send()

    def small_place(self, owner):
        return self.small_full.at[pl.ds(pl.multiple_of(owner * ROWS, ROWS), ROWS), :]

    def small_copies(self):
        w = len(self.shapes)
        far = [self.copy((w, s, 0), self.small_shard, self.small_place(self.f), self.r, self.along(s)) for s in (1, 2, 3)]
        own = self.copy((w, 0, 0), self.small_shard, self.small_place(self.f), self.r, self.sib)
        here = pltpu.make_async_copy(self.small_shard, self.small_place(self.f), self.send.at[w, 0, 1])
        sib = []
        for s in (1, 2, 3):
            place = self.small_place(self.along(4 - s))
            sib.append(self.copy((w, s, 1), place, place, self.r, self.sib))
        return far, own, here, sib


class Reduce(Links):
    SLOTS = 8

    def __init__(self, shapes, grads, outs, bufs, send, recv):
        super().__init__(send, recv)
        self.shapes, self.grads, self.outs, self.bufs = shapes, grads, outs, bufs

    @staticmethod
    def scratch(shapes):
        out = []
        for rows, cols in shapes:
            out += [
                pltpu.VMEM((4, rows, cols), BF16),
                pltpu.VMEM((4, rows, cols), BF16),
                pltpu.VMEM((2, rows, cols // 2), BF16),
                pltpu.VMEM((2, rows // 2, cols), BF16),
                pltpu.VMEM((4, rows // 2, cols // 2), BF16),
                pltpu.VMEM((3, rows // 2, cols // 2), BF16),
                pltpu.VMEM((rows // 2, cols // 2), BF16),
            ]
        return out

    def shard(self, w, s, core):
        rows = self.shapes[w][0]
        at = pl.multiple_of((((self.z + s) % 4) * 2 + core) * rows, 16)
        return self.grads[w].at[pl.ds(at, rows), :]

    def half_rows(self, w, bit):
        h = self.shapes[w][0] // 2
        return pl.ds(pl.multiple_of(bit * h, 16), h)

    def half_cols(self, w, bit):
        h = self.shapes[w][1] // 2
        return pl.ds(pl.multiple_of(bit * h, 128), h)

    def core_copy(self, w, s):
        return self.copy((w, s, 0), self.shard(w, s, 1 - self.c), self.bufs[w][1].at[s], self.r, self.sib)

    def core_load(self, w, s):
        return pltpu.make_async_copy(self.shard(w, s, self.c), self.bufs[w][0].at[s], self.send.at[w, s, 7])

    def start(self, w, s):
        self.core_copy(w, s).start()
        self.core_load(w, s).start()

    def x_first(self, s):
        return s % 2 == 1

    def first_copy(self, w, s):
        own, hx, hy = self.bufs[w][0], self.bufs[w][2], self.bufs[w][3]
        if self.x_first(s):
            return self.copy((w, s, 1), own.at[s, :, self.half_cols(w, 1 - self.x)], hx.at[s // 2], self.xr, self.f)
        return self.copy((w, s, 1), own.at[s, self.half_rows(w, 1 - self.y), :], hy.at[s // 2], self.yr, self.f)

    def add_core(self, w, s):
        self.core_copy(w, s).wait_recv()
        self.core_load(w, s).wait()
        own, got = self.bufs[w][0], self.bufs[w][1]
        own[s] = own[s] + got[s]
        self.first_copy(w, s).start()

    def second_copy(self, w, s):
        own, quarter = self.bufs[w][0], self.bufs[w][4]
        if self.x_first(s):
            src = own.at[s, self.half_rows(w, 1 - self.y), self.half_cols(w, self.x)]
            return self.copy((w, s, 2), src, quarter.at[s], self.yr, self.f)
        src = own.at[s, self.half_rows(w, self.y), self.half_cols(w, 1 - self.x)]
        return self.copy((w, s, 2), src, quarter.at[s], self.xr, self.f)

    def add_first(self, w, s):
        self.first_copy(w, s).wait_recv()
        own, hx, hy = self.bufs[w][0], self.bufs[w][2], self.bufs[w][3]
        if self.x_first(s):
            at = (s, slice(None), self.half_cols(w, self.x))
            own[at] = own[at] + hx[s // 2]
        else:
            at = (s, self.half_rows(w, self.y), slice(None))
            own[at] = own[at] + hy[s // 2]
        self.second_copy(w, s).start()

    def far_copy(self, w, s):
        own, far = self.bufs[w][0], self.bufs[w][5]
        src = own.at[s, self.half_rows(w, self.y), self.half_cols(w, self.x)]
        return self.copy((w, s, 3), src, far.at[s - 1], self.r, self.along(s))

    def add_second(self, w, s):
        self.second_copy(w, s).wait_recv()
        own, quarter = self.bufs[w][0], self.bufs[w][4]
        at = (s, self.half_rows(w, self.y), self.half_cols(w, self.x))
        own[at] = own[at] + quarter[s]
        if s > 0:
            self.far_copy(w, s).start()

    def place(self, w, q, part=None):
        rows, cols = self.shapes[w]
        h = rows // 2
        r0, n = (q // 2) * h, h
        if part is not None:
            n = h // 32 * 16 if part == 0 else h - h // 32 * 16
            r0 = r0 if part == 0 else r0 + h // 32 * 16
        return self.outs[w].at[pl.ds(pl.multiple_of(r0, 16), n), self.half_cols(w, q % 2)]

    def out_local(self, w):
        return pltpu.make_async_copy(self.bufs[w][6], self.place(w, self.r), self.send.at[w, 0, 3])

    def out_x(self, w):
        return self.copy((w, 0, 4), self.bufs[w][6], self.place(w, self.r), self.xr, self.f)

    def out_y(self, w):
        return self.copy((w, 0, 5), self.bufs[w][6], self.place(w, self.r), self.yr, self.f)

    def out_dy(self, w):
        p = self.place(w, flip(self.r, 1), 0)
        return self.copy((w, 1, 4), p, p, self.yr, self.f)

    def out_dx(self, w):
        p = self.place(w, flip(self.r, 2), 1)
        return self.copy((w, 1, 5), p, p, self.xr, self.f)

    def total(self, w):
        own, far, done = self.bufs[w][0], self.bufs[w][5], self.bufs[w][6]
        for s in (1, 2, 3):
            self.far_copy(w, s).wait_recv()
        at = (0, self.half_rows(w, self.y), self.half_cols(w, self.x))
        done[...] = (own[at].astype(F32) + far[0].astype(F32) + far[1].astype(F32) + far[2].astype(F32)).astype(BF16)
        self.out_x(w).start()
        self.out_y(w).start()
        self.out_local(w).start()

    def relay(self, w):
        self.out_x(w).wait_recv()
        self.out_dy(w).start()
        self.out_y(w).wait_recv()
        self.out_dx(w).start()

    def finish(self, w):
        for s in range(4):
            self.core_copy(w, s).wait_send()
            self.first_copy(w, s).wait_send()
            self.second_copy(w, s).wait_send()
            if s:
                self.far_copy(w, s).wait_send()
        self.out_local(w).wait()
        self.out_x(w).wait_send()
        self.out_y(w).wait_send()
        for d in (self.out_dy(w), self.out_dx(w)):
            d.wait_send()
            d.wait_recv()


def plan(red, n, order):
    items = [(w, s) for w in order for s in (1, 2, 3, 0)]
    ticks = []
    m = len(items)
    for k in range(m + 4):
        acts = []
        if k < m:
            acts.append(functools.partial(red.add_core, *items[k]))
        if 0 <= k - 2 < m:
            acts.append(functools.partial(red.add_first, *items[k - 2]))
        if 0 <= k - 4 < m:
            w, s = items[k - 4]
            acts.append(functools.partial(red.add_second, w, s))
            if s == 0:
                j = order.index(w)
                if j > 0:
                    acts.append(functools.partial(red.total, order[j - 1]))
                if j > 1:
                    acts.append(functools.partial(red.relay, order[j - 2]))
        ticks.append(acts)
    tail = [functools.partial(red.total, order[-1])]
    if n > 1:
        tail.append(functools.partial(red.relay, order[-2]))
    tail.append(functools.partial(red.relay, order[-1]))
    ticks.append(tail)
    ticks.append([functools.partial(red.finish, w) for w in order])
    return items, ticks


def spread_rows(small, row, step, count, unit):
    width = count * unit
    lane = lax.broadcasted_iota(jnp.int32, (8, width), 1)
    total = jnp.zeros((8, width), F32)
    for k in range(count):
        one = jnp.broadcast_to(small[row[k] : row[k] + 1, :], (8, LANE))
        wide = jnp.concatenate([one, jnp.zeros((8, width - LANE), F32)], 1)
        wide = jnp.where(lane < unit, wide, 0.0)
        total = total + (pltpu.roll(wide, k * unit, 1) if k else wide)
    return total[0:1]


def fill_mask(mask_ref, ord_ref, limit, s, seq_len, turned):
    blocks = seq_len // LANE
    own = ord_ref[pl.ds(s, 1), :].astype(F32)
    cols = jnp.broadcast_to(own, (LANE, seq_len)).T
    for rb in range(blocks):
        col = cols[rb * LANE : (rb + 1) * LANE, :]
        rank = jnp.concatenate([col] * blocks, 1)
        place = lax.broadcasted_iota(jnp.int32, (LANE, seq_len), 0 if turned else 1)
        if turned:
            place = place + rb * LANE
        order = (rank <= own) if turned else (own <= rank)
        ok = (place < limit) & ((place == 0) | order)
        mask_ref[s, rb * LANE : (rb + 1) * LANE, :] = jnp.where(ok, 0.0, MASKED)


def fill_near(near_ref, small, onehot_ref):
    near_ref[...] = lax.dot_general(small, onehot_ref[...], (((0,), (0,)), ((), ())), preferred_element_type=F32) * LOG2E


def attention_step(hp, s, proj, mask_ref, near_ref, put_out, put_total):
    query_c, keys, value, query_g = proj
    seq_len = keys.shape[0]
    blocks = seq_len // LANE
    values = jnp.concatenate([value, jnp.ones((seq_len, LANE), BF16)], 1)
    lane = lax.broadcasted_iota(jnp.int32, (seq_len, LANE), 1)
    diag_r = lax.broadcasted_iota(jnp.int32, (LANE, LANE), 0)
    diag_c = lax.broadcasted_iota(jnp.int32, (LANE, LANE), 1)
    outs = [[], []]
    totals = [jnp.zeros((seq_len, LANE), F32), jnp.zeros((seq_len, LANE), F32)]
    for t in range(2):
        head = hp * 2 + t
        sel = head_lanes((seq_len, LANE), t)
        head_row = near_ref[pl.ds(head, 1), :]
        near = skewed(head_row[:, :NEAR], 3 * LANE)
        bias = tile_bias(near, head_row[:, NEAR : NEAR + 1], head_row[:, NEAR + 1 : NEAR + 2], seq_len, -1)
        for stream in range(2):
            query = jnp.where(sel, query_g if stream else query_c, jnp.zeros((), BF16))
            raw = nt(query, keys)
            probs = []
            maxes = []
            for rb in range(blocks):
                part = raw[rb * LANE : (rb + 1) * LANE, :] + (bias[rb] + mask_ref[s, rb * LANE : (rb + 1) * LANE, :])
                if stream == 1:
                    hit = diag_r == diag_c
                    if rb == 0:
                        hit = hit & (diag_c != 0)
                    pieces = []
                    if rb > 0:
                        pieces.append(part[:, : rb * LANE])
                    pieces.append(jnp.where(hit, MASKED, part[:, rb * LANE : (rb + 1) * LANE]))
                    if rb < blocks - 1:
                        pieces.append(part[:, (rb + 1) * LANE :])
                    part = jnp.concatenate(pieces, 1)
                top = jnp.max(part, 1, keepdims=True)
                probs.append(jnp.exp2(part - top).astype(BF16))
                maxes.append(jnp.broadcast_to(top, (LANE, LANE)))
            mixed = nn(jnp.concatenate(probs, 0), values)
            total = mixed[:, LANE:]
            outs[stream].append(mixed[:, :LANE] / total)
            log_total = jnp.concatenate(maxes, 0) + jnp.log2(total)
            hi = log_total.astype(BF16).astype(F32)
            totals[stream] = jnp.where(lane == head, -hi, jnp.where(lane == head + HEAD, hi - log_total, totals[stream]))
    first = head_lanes((seq_len, LANE), 0)
    mine = (lane == hp * 2) | (lane == hp * 2 + 1) | (lane == hp * 2 + HEAD) | (lane == hp * 2 + 1 + HEAD)
    for stream in range(2):
        put_out(stream, jnp.where(first, outs[stream][0], outs[stream][1]).astype(BF16))
        put_total(stream, totals[stream].astype(BF16), mine)


def forward_kernel(shapes, linked, len_ref, content_ref, query_ref, ord_ref, onehot_ref, *refs):
    n = len(shapes)
    if linked:
        shards, small_shard, refs = refs[:n], refs[n], refs[n + 1 :]
        full_refs, refs = refs[: n - 1], refs[n - 1 :]
        joined_out, small_out, refs = refs[0], refs[1], refs[2:]
    else:
        joined_in, small_in, refs = refs[0], refs[1], refs[2:]
    mixed_ref, total_ref, proj_out, joined_ref, small_ref, proj_ref, mask_ref, near_ref, own_sem = refs[:9]
    hp = pl.program_id(0)
    s = pl.program_id(1)
    step = hp * pl.num_programs(1) + s
    steps = (HEADS // 2) * total_ref.shape[1]
    seqs = total_ref.shape[1]
    seq_len = total_ref.shape[2]
    row_count, width = content_ref.shape
    if linked:
        send, recv = refs[9:]
        net = Gather(shapes, shards, (joined_ref,) + tuple(full_refs), send, recv)
        net.small_shard, net.small_full = small_shard, small_ref
    proj_copy = pltpu.make_async_copy(proj_ref, proj_out, own_sem.at[0])

    @pl.when(step == 0)
    def _():
        if linked:
            net.barrier()
            far, own, here, sib = net.small_copies()
            for d in far + [own, here]:
                d.start()
            for w in range(n):
                net.start(w)
            for s0 in range(seqs):
                fill_mask(mask_ref, ord_ref, len_ref[s0], s0, seq_len, False)
            for d, e in zip(far, sib):
                d.wait_recv()
                e.start()
            for k in (1, 2, 3):
                net.relay_z(0, k)
            for k in (1, 2, 3):
                net.relay_xy(0, k)
            for k in (1, 2, 3):
                net.relay_z(1, k)
            for k in (1, 2, 3):
                net.relay_diag(0, k)
            for k in (1, 2, 3):
                net.relay_z(2, k)
            for d in far:
                d.wait_send()
            for d in [own] + sib:
                d.wait_send()
                d.wait_recv()
            here.wait()
            net.arrive(0)
            pltpu.make_async_copy(joined_ref, joined_out, own_sem.at[1]).start()
            pltpu.make_async_copy(small_ref, small_out, own_sem.at[2]).start()
        else:
            fetch = (pltpu.make_async_copy(joined_in, joined_ref, own_sem.at[1]), pltpu.make_async_copy(small_in, small_ref, own_sem.at[2]))
            for d in fetch:
                d.start()
            for s0 in range(seqs):
                fill_mask(mask_ref, ord_ref, len_ref[s0], s0, seq_len, False)
            for d in fetch:
                d.wait()
        fill_near(near_ref, small_ref[...], onehot_ref)
        small = small_ref[...].astype(F32)
        shards_all = small.shape[0] // ROWS
        unit = width // shards_all
        half = shards_all // 2
        shift_q = spread_rows(small, [k // 2 * ROWS + k % 2 for k in range(2 * half)], 0, 2 * half, unit)
        shift_v = spread_rows(small, [(half + k // 2) * ROWS + k % 2 for k in range(2 * half)], 0, 2 * half, unit)
        scale = LOG2E / math.sqrt(HEAD)
        chunk = 256

        @pl.loop(0, row_count // chunk)
        def _(i):
            rows = pl.ds(pl.multiple_of(i * chunk, chunk), chunk)
            rows_c = content_ref[rows, :]
            proj_ref[rows, 0:width] = ((nn(rows_c, joined_ref[:, 0:width]) + shift_q) * scale).astype(BF16)
            proj_ref[rows, width : 2 * width] = nn(rows_c, joined_ref[:, width : 2 * width]).astype(BF16)
            proj_ref[rows, 2 * width : 3 * width] = (nn(rows_c, joined_ref[:, 2 * width : 3 * width]) + shift_v).astype(BF16)
            proj_ref[rows, 3 * width : 4 * width] = ((nn(query_ref[rows, :], joined_ref[:, 0:width]) + shift_q) * scale).astype(BF16)

        proj_copy.start()

    if linked:
        agenda = {
            1: [(net.relay_xy, 1, (1, 2, 3))],
            3: [(net.relay_z, 3, (1, 2, 3))],
            4: [(net.relay_xy, 2, (1,))],
            5: [(net.relay_xy, 2, (2,)), (net.relay_diag, 1, (1, 2, 3))],
            6: [(net.relay_xy, 2, (3,))],
            8: [(net.relay_diag, 2, (1, 2)), (net.relay_xy, 3, (1,))],
            9: [(net.relay_diag, 2, (3,)), (net.relay_xy, 3, (2,))],
            10: [(net.relay_xy, 3, (3,))],
        }
        for at, acts in agenda.items():

            @pl.when(step == min(at, steps - 1))
            def _():
                for act, w, ks in acts:
                    for k in ks:
                        act(w, k)

    here_rows = pl.ds(pl.multiple_of(s * seq_len, seq_len), seq_len)
    column = lambda k: pl.ds(pl.multiple_of(k * width + hp * LANE, LANE), LANE)
    proj = [proj_ref[here_rows, column(k)] for k in range(4)]

    def put_out(stream, value):
        mixed_ref[stream] = value

    def put_total(stream, value, mine):
        @pl.when(hp == 0)
        def _():
            total_ref[stream, s] = value

        @pl.when(hp > 0)
        def _():
            total_ref[stream, s] = jnp.where(mine, value, total_ref[stream, s])

    attention_step(hp, s, proj, mask_ref, near_ref, put_out, put_total)

    @pl.when(step == steps - 1)
    def _():
        proj_copy.wait()
        if linked:
            pltpu.make_async_copy(joined_ref, joined_out, own_sem.at[1]).wait()
            pltpu.make_async_copy(small_ref, small_out, own_sem.at[2]).wait()
            for k in (1, 2, 3):
                net.relay_diag(3, k)
            for w in range(n):
                if w:
                    net.arrive(w)
                net.drain(w)


def forward_attention(linked, content_rows, query_rows, lengths, order, weights, small):
    row_count, width = content_rows.shape
    seqs, seq_len = order.shape
    pairs = width // LANE
    shards = 8 if linked else small.shape[0] // ROWS
    onehot = table_onehot(-1, shards)
    shapes = [w.shape for w in weights] if linked else []
    n = len(shapes)
    anywhere = pl.BlockSpec(memory_space=pl.ANY)
    inside = pl.BlockSpec(memory_space=pltpu.VMEM)
    block3 = pl.BlockSpec((2, seq_len, LANE), lambda h, s: (0, s, h))
    joined_shape = (width, 3 * width)
    small_shape = (shards * ROWS, LANE)
    out_specs, out_shape = [], []
    if linked:
        out_specs += [anywhere] * (n + 1)
        out_shape += [jax.ShapeDtypeStruct((8 * a, b), BF16) for a, b in shapes[1:]]
        out_shape += [jax.ShapeDtypeStruct(joined_shape, BF16), jax.ShapeDtypeStruct(small_shape, BF16)]
    out_specs += [block3, pl.BlockSpec((2, seqs, seq_len, LANE), lambda h, s: (0, 0, 0, 0)), anywhere]
    out_shape += [
        jax.ShapeDtypeStruct((2, row_count, width), BF16),
        jax.ShapeDtypeStruct((2, seqs, seq_len, LANE), BF16),
        jax.ShapeDtypeStruct((row_count, 4 * width), BF16),
    ]
    scratch = [
        pltpu.VMEM(joined_shape, BF16),
        pltpu.VMEM(small_shape, BF16),
        pltpu.VMEM((row_count, 4 * width), BF16),
        pltpu.VMEM((seqs, seq_len, seq_len), F32),
        pltpu.VMEM((LANE, NEAR + LANE), F32),
        pltpu.SemaphoreType.DMA((3,)),
    ]
    if linked:
        scratch += [pltpu.SemaphoreType.DMA((n + 1, 4, Gather.SLOTS)), pltpu.SemaphoreType.DMA((n + 1, 4, Gather.SLOTS))]
    flops = 2 * row_count * width * 4 * width + 8 * row_count * seq_len * width
    return pl.pallas_call(
        functools.partial(forward_kernel, shapes, linked),
        grid=(pairs, seqs),
        in_specs=[pl.BlockSpec(memory_space=pltpu.SMEM), inside, inside, inside, inside] + [anywhere] * (n + 1 if linked else 2),
        out_specs=out_specs,
        out_shape=out_shape,
        scratch_shapes=scratch,
        cost_estimate=pl.CostEstimate(flops=flops, bytes_accessed=30 * 2**20, transcendentals=4 * row_count * seq_len * HEADS),
        compiler_params=pltpu.CompilerParams(
            dimension_semantics=("arbitrary", "arbitrary"), vmem_limit_bytes=VMEM_BYTES,
            **(dict(collective_id=0, has_side_effects=True) if linked else {})),
        name="attention_forward",
    )(lengths, content_rows, query_rows, order, onehot, *(list(weights) + [small]))


def backward_kernel(shapes, linked, len_ref, q_ref, k_ref, v_ref, g_ref, dc_ref, dg_ref, oc_ref, og_ref, tot_ref, ord_ref, small_ref, onehot_ref, *refs):
    n = len(shapes)
    grads, refs = refs[:n], refs[n:]
    outs, refs = refs[:n], refs[n:]
    grad_ref, sums_ref, mask_ref, acc_ref, near_ref = refs[:5]
    refs = refs[5:]
    hp = pl.program_id(0)
    s = pl.program_id(1)
    last = pl.num_programs(1) - 1
    step = hp * pl.num_programs(1) + s
    seq_len = q_ref.shape[0]
    blocks = seq_len // LANE
    half = seq_len // 2
    steps = (HEADS // 2) * ord_ref.shape[0]
    if linked:
        bufs = [refs[7 * w : 7 * w + 7] for w in range(n)]
        send, recv = refs[7 * n :]
        net = Reduce(shapes, grads, outs, bufs, send, recv)
        items, ticks = plan(net, n, list(range(n)))

        @pl.when(step == 0)
        def _():
            net.barrier()
            for w, k in items:
                net.start(w, k)

        tail = ticks[-2:]
        ticks = ticks[:-2]
        for at in range(1, steps):
            acts = [a for i, t in enumerate(ticks) if 1 + i * (steps - 1) // len(ticks) == at for a in t]

            @pl.when(step == at)
            def _():
                for act in acts:
                    act()

    @pl.when(hp == 0)
    def _():
        fill_mask(mask_ref, ord_ref, len_ref[s], s, seq_len, True)

    @pl.when(step == 0)
    def _():
        fill_near(near_ref, small_ref[...], onehot_ref)

    lane = lax.broadcasted_iota(jnp.int32, (seq_len, LANE), 1)
    ones = jnp.ones((seq_len, LANE), BF16)
    zero = jnp.zeros((), BF16)
    keys = k_ref[...]
    keys_wide = jnp.concatenate([keys, ones], 1)
    values_wide = jnp.concatenate([v_ref[...], ones], 1)
    keys_turned = keys.astype(F32).T.astype(BF16)
    lane_r = lax.broadcasted_iota(jnp.int32, (LANE, LANE), 0)
    lane_c = lax.broadcasted_iota(jnp.int32, (LANE, LANE), 1)
    pick = (lane_r // HEAD == lane_c).astype(BF16)
    grad_keys = None
    grad_values = None
    grad_query = [[], []]
    streams = []
    for src, grad, out, tot in ((q_ref, dc_ref, oc_ref, tot_ref[0, 0]), (g_ref, dg_ref, og_ref, tot_ref[1, 0])):
        g = grad[...]
        delta = nn((g.astype(F32) * out[...].astype(F32)).astype(BF16), pick)
        streams.append((src[...], g, -delta, tot))
    for t in range(2):
        head = hp * 2 + t
        sel = head_lanes((seq_len, LANE), t)
        head_row = near_ref[pl.ds(head, 1), :]
        near = skewed(head_row[:, :NEAR], 3 * LANE)
        bias = tile_bias(near, head_row[:, NEAR : NEAR + 1], head_row[:, NEAR + 1 : NEAR + 2], seq_len, 1)
        for c0 in range(0, seq_len, half):
            both = None
            for stream in range(2):
                q, g, delta, tot = streams[stream]
                q = jnp.where(sel, q, zero)[c0 : c0 + half]
                g = jnp.where(sel, g, zero)[c0 : c0 + half]
                d = delta[c0 : c0 + half]
                ln = lane[c0 : c0 + half]
                tt = jnp.where((ln == head) | (ln == head + HEAD), tot[c0 : c0 + half], zero)
                dd = jnp.where(ln == t, d, 0.0)
                dhi = dd.astype(BF16)
                dlo = pltpu.roll(dd - dhi.astype(F32), HEAD, 1).astype(BF16)
                raw = nt(keys_wide, jnp.concatenate([q, tt], 1))
                dpr = nt(values_wide, jnp.concatenate([g, dhi + dlo], 1))
                probs, grads = [], []
                for rb in range(blocks):
                    sl = slice(rb * LANE, (rb + 1) * LANE)
                    part = raw[sl] + (bias[rb][:, c0 : c0 + half] + mask_ref[s, sl, c0 : c0 + half])
                    r0 = rb * LANE
                    if stream == 1 and c0 <= r0 < c0 + half:
                        hit = lane_r == lane_c
                        if rb == 0:
                            hit = hit & (lane_r != 0)
                        x0 = r0 - c0
                        diag = jnp.where(hit, MASKED, part[:, x0 : x0 + LANE])
                        pieces = []
                        if x0 > 0:
                            pieces.append(part[:, :x0])
                        pieces.append(diag)
                        if x0 + LANE < half:
                            pieces.append(part[:, x0 + LANE :])
                        part = jnp.concatenate(pieces, 1)
                    p = jnp.exp2(part)
                    probs.append(p.astype(BF16))
                    grads.append(p * dpr[sl])
                low = [x.astype(BF16) for x in grads]
                prob = jnp.concatenate(probs, 0)
                gl = jnp.concatenate(low, 0)
                gv = nn(prob, g)
                gk = nn(gl, q)
                grad_values = gv if grad_values is None else grad_values + gv
                grad_keys = gk if grad_keys is None else grad_keys + gk
                grad_query[stream].append(nn(keys_turned[t * HEAD : (t + 1) * HEAD], gl))
                both = grads if both is None else [a + b for a, b in zip(both, grads)]
            sums = {}
            for rb in range(blocks):
                for cb in range(half // LANE):
                    e = cb + c0 // LANE - rb
                    e = max(-2, min(2, e))
                    x = both[rb][:, cb * LANE : (cb + 1) * LANE]
                    sums[e] = x if e not in sums else sums[e] + x
            for e, x in sums.items():
                lanes = slice((e + 2) * LANE, (e + 3) * LANE)
                fresh = c0 == 0
                if fresh:
                    @pl.when(s == 0)
                    def _():
                        acc_ref[t, :, lanes] = x

                    @pl.when(s > 0)
                    def _():
                        acc_ref[t, :, lanes] = acc_ref[t, :, lanes] + x
                else:
                    acc_ref[t, :, lanes] = acc_ref[t, :, lanes] + x
            if c0 == 0:
                for e in range(-2, 3):
                    if e not in sums:
                        @pl.when(s == 0)
                        def _():
                            acc_ref[t, :, (e + 2) * LANE : (e + 3) * LANE] = jnp.zeros((LANE, LANE), F32)
    count = seq_len // half
    scale = 1.0 / math.sqrt(HEAD)
    for stream, ref in ((0, 0), (1, 3)):
        pieces = grad_query[stream]
        top = jnp.concatenate(pieces[:count], 1)
        bot = jnp.concatenate(pieces[count:], 1)
        grad_ref[ref] = (jnp.concatenate([top, bot], 0) * scale).T.astype(BF16)
    grad_ref[1] = (grad_keys * LN2).astype(BF16)
    grad_ref[2] = grad_values.astype(BF16)

    @pl.when(s == last)
    def _():
        for t in range(2):
            near = jnp.concatenate([acc_ref[t, :, LANE : 4 * LANE], jnp.zeros((LANE, LANE), F32)], 1)
            mirror = (lane_r + lane_c == LANE - 1).astype(F32)
            flipped = lax.dot_general(mirror, near, (((1,), (0,)), ((), ())), precision=lax.Precision.HIGHEST, preferred_element_type=F32)
            turned = pltpu.roll(flipped, 0, 1, stride=1, stride_axis=0)
            row = jnp.sum(turned, 0, keepdims=True)
            below = jnp.sum(acc_ref[t, :, :LANE], 0, keepdims=True)
            above = jnp.sum(acc_ref[t, :, 4 * LANE :], 0, keepdims=True)
            sums_ref[pl.ds(hp * 2 + t, 1), :] = jnp.concatenate([row, below, above], 1)

    if linked:

        @pl.when(step == steps - 1)
        def _():
            for acts in tail:
                for act in acts:
                    act()


def backward_attention(linked, proj, grad_mixed, mixed, totals, lengths, order, small, weight_grads):
    rows, width = grad_mixed.shape
    seqs, seq_len = order.shape
    pairs = width // LANE
    onehot = table_onehot(1, small.shape[0] // ROWS)
    shapes = [(g.shape[0] // 8, g.shape[1]) for g in weight_grads]
    n = len(shapes)
    block = lambda off: pl.BlockSpec((seq_len, LANE), lambda h, s, off=off: (s, off + h))
    low = pl.BlockSpec((seq_len, LANE), lambda h, s: (seqs + s, h))
    anywhere = pl.BlockSpec(memory_space=pl.ANY)
    inside = pl.BlockSpec(memory_space=pltpu.VMEM)
    sums_shape = (2 * pairs, NEAR + 2 * LANE)
    scratch = [
        pltpu.VMEM((seqs, seq_len, seq_len), F32),
        pltpu.VMEM((2, LANE, 5 * LANE), F32),
        pltpu.VMEM((LANE, NEAR + LANE), F32),
    ]
    if linked:
        scratch += Reduce.scratch(shapes)
        scratch += [pltpu.SemaphoreType.DMA((n, 4, Reduce.SLOTS)), pltpu.SemaphoreType.DMA((n, 4, Reduce.SLOTS))]
    outs = pl.pallas_call(
        functools.partial(backward_kernel, shapes, linked),
        grid=(pairs, seqs),
        in_specs=[
            pl.BlockSpec(memory_space=pltpu.SMEM),
            block(0), block(pairs), block(2 * pairs), block(3 * pairs),
            block(0), low, block(0), low,
            pl.BlockSpec((2, 1, seq_len, LANE), lambda h, s: (0, s, 0, 0)),
            inside, inside, inside,
        ] + [anywhere] * n,
        out_specs=[anywhere] * n + [pl.BlockSpec((4, seq_len, LANE), lambda h, s: (0, s, h)), pl.BlockSpec(sums_shape, lambda h, s: (0, 0))],
        out_shape=[jax.ShapeDtypeStruct(a, BF16) for a in shapes] + [jax.ShapeDtypeStruct((4, rows // 2, width), BF16), jax.ShapeDtypeStruct(sums_shape, F32)],
        scratch_shapes=scratch,
        cost_estimate=pl.CostEstimate(flops=20 * rows * seq_len * width, bytes_accessed=30 * 2**20, transcendentals=2 * rows * seq_len * HEADS),
        compiler_params=pltpu.CompilerParams(
            dimension_semantics=("arbitrary", "arbitrary"), vmem_limit_bytes=VMEM_BYTES,
            **(dict(collective_id=1, has_side_effects=True) if linked else {})),
        name="attention_backward",
    )(lengths, proj, proj, proj, proj, grad_mixed, grad_mixed, mixed, mixed, totals, order, small, onehot, *weight_grads)
    sums = outs[n + 1]
    fold = np.zeros((sums_shape[1], BUCKETS), np.float32)
    fold[:NEAR] = np.roll(near_onehot(1).T, LANE - 1, 0)
    fold[NEAR : NEAR + LANE, BUCKETS - 1] = 1
    fold[NEAR + LANE :, BUCKETS // 2 - 1] = 1
    grad_table = jnp.dot(sums, jnp.asarray(fold), precision=lax.Precision.HIGHEST).T
    return outs[:n], outs[n], grad_table


def small_reduce(net, w, part, out, bufs):
    own, core, across_x, across_y, far = bufs
    rows = 4 * ROWS
    mine = part.at[pl.ds(pl.multiple_of(net.c * rows, rows), rows), :]
    other = part.at[pl.ds(pl.multiple_of((1 - net.c) * rows, rows), rows), :]
    load = pltpu.make_async_copy(mine, own.at[0], net.send.at[w, 0, 7])
    to_core = net.copy((w, 0, 0), other, core, net.r, net.sib)
    to_x = net.copy((w, 0, 1), own.at[1], across_x, net.xr, net.f)
    to_y = net.copy((w, 0, 2), own.at[2], across_y, net.yr, net.f)
    z_rows = lambda s: pl.ds(pl.multiple_of((net.z + s) % 4 * ROWS, ROWS), ROWS)
    to_far = [net.copy((w, s, 3), own.at[3, z_rows(s), :], far.at[s - 1], net.r, net.along(s)) for s in (1, 2, 3)]

    def first():
        load.start()
        to_core.start()

    def second():
        load.wait()
        to_core.wait_recv()
        own[1] = own[0] + core[...]
        to_x.start()

    def third():
        to_x.wait_recv()
        own[2] = own[1] + across_x[...]
        to_y.start()

    def fourth():
        to_y.wait_recv()
        own[3] = own[2] + across_y[...]
        for d in to_far:
            d.start()

    def fifth():
        for d in to_far:
            d.wait_recv()
        out[...] = own[3, z_rows(0), :] + far[0] + far[1] + far[2]
        for d in [to_core, to_x, to_y] + to_far:
            d.wait_send()

    return first, second, third, fourth, fifth


def reduce_kernel(shapes, n, *refs):
    grads, small_part, refs = refs[:n], refs[n], refs[n + 1 :]
    outs, small_out, refs = refs[:n], refs[n], refs[n + 1 :]
    bufs = [refs[7 * w : 7 * w + 7] for w in range(n)]
    small_bufs, (send, recv) = refs[7 * n : 7 * n + 5], refs[7 * n + 5 :]
    net = Reduce(shapes, grads, outs, bufs, send, recv)
    first, second, third, fourth, fifth = small_reduce(net, n, small_part, small_out, small_bufs)
    net.barrier()
    items, ticks = plan(net, n, list(range(n)))
    first()
    for w, k in items:
        net.start(w, k)
    extra = {1: second, 4: third, 6: fourth}
    for i, acts in enumerate(ticks):
        for act in acts:
            act()
        if i in extra:
            extra[i]()
    fifth()


def reduce_rest(weight_grads, small_grads):
    n = len(weight_grads)
    shapes = [(g.shape[0] // 8, g.shape[1]) for g in weight_grads]
    anywhere = pl.BlockSpec(memory_space=pl.ANY)
    inside = pl.BlockSpec(memory_space=pltpu.VMEM)
    rows = 4 * ROWS
    scratch = Reduce.scratch(shapes)
    scratch += [pltpu.VMEM((4, rows, LANE), F32)] + [pltpu.VMEM((rows, LANE), F32)] * 3 + [pltpu.VMEM((3, ROWS, LANE), F32)]
    scratch += [pltpu.SemaphoreType.DMA((n + 1, 4, Reduce.SLOTS)), pltpu.SemaphoreType.DMA((n + 1, 4, Reduce.SLOTS))]
    return pl.pallas_call(
        functools.partial(reduce_kernel, shapes, n),
        out_shape=[jax.ShapeDtypeStruct(a, BF16) for a in shapes] + [jax.ShapeDtypeStruct((ROWS, LANE), F32)],
        in_specs=[anywhere] * (n + 1),
        out_specs=[anywhere] * n + [inside],
        scratch_shapes=scratch,
        compiler_params=pltpu.CompilerParams(collective_id=2, has_side_effects=True, vmem_limit_bytes=VMEM_BYTES),
        name="reduce_rest",
    )(*weight_grads, small_grads)


def norm_forward(summed, gain_vec, shift_vec):
    row_mean = jnp.mean(summed, -1, keepdims=True)
    centered = summed - row_mean
    inverse = lax.rsqrt(jnp.mean(centered * centered, -1, keepdims=True) + eps_norm)
    normed = centered * inverse
    return (normed * gain_vec + shift_vec, normed, inverse)


def norm_backward(upstream, normed, inverse, gain_vec):
    scaled = upstream * gain_vec
    centered = (
        scaled
        - jnp.mean(scaled, -1, keepdims=True)
        - normed * jnp.mean(scaled * normed, -1, keepdims=True)
    )
    return (inverse * centered, jnp.sum(upstream * normed, 0), jnp.sum(upstream, 0))


def gelu_value(hidden_in):
    return 0.5 * hidden_in * (1.0 + lax.erf(hidden_in * root_half))


def gelu_slope(hidden_in):
    return (
        0.5 * (1.0 + lax.erf(hidden_in * root_half))
        + hidden_in * jnp.exp(-0.5 * hidden_in * hidden_in) * inv_root_tau
    )


def rows_inner(left_op, right_op):
    return lax.dot_general(
        left_op, right_op, (((0,), (0,)), ((), ())), preferred_element_type=jnp.float32
    )


def times_transpose(left_op, right_op):
    return lax.dot_general(
        left_op, right_op, (((1,), (1,)), ((), ())), preferred_element_type=jnp.float32
    )


def pack_small(groups, shards):
    rows = []
    for g in groups:
        g = g.reshape(shards, -1, g.shape[-1]) if g.ndim > 1 else g
        rows.append(g)
    wide = [jnp.pad(g, ((0, 0), (0, 0), (0, LANE - g.shape[2]))) for g in rows]
    joined = jnp.concatenate(wide, 1)
    joined = jnp.pad(joined, ((0, 0), (0, ROWS - joined.shape[1]), (0, 0)))
    return joined.reshape(shards * ROWS, LANE)


def on_device(axes, content_stream, query_stream, lengths, factor_order, qkv_weight, qv_bias, out_weight, out_bias, norm1_gain, norm1_bias, rel_table, ffn_in_weight, ffn_in_bias, ffn_out_weight, ffn_out_bias, norm2_gain, norm2_bias, content_cot, query_cot):
    linked = axes == (4, 8)
    shards = axes[1]
    seq_count, seq_len, width = content_stream.shape
    row_count = seq_count * seq_len
    unit = width // shards
    small_args = (qv_bias, out_bias, norm1_gain, norm1_bias, ffn_out_bias, norm2_gain, norm2_bias, ffn_in_bias)
    small = pack_small([p.reshape(1, -1, unit) for p in small_args] + [rel_table[None]], 1).astype(BF16)
    weights = [w.astype(BF16) for w in (qkv_weight, out_weight, ffn_in_weight, ffn_out_weight)]
    content_rows = content_stream.reshape(row_count, width)
    query_rows = query_stream.reshape(row_count, width)
    if linked:
        out_proj, in_proj, out_ffn, joined_proj, small, mixed, totals, proj = forward_attention(
            True, content_rows, query_rows, lengths, factor_order, weights, small)
    else:
        gather = lambda a: lax.all_gather(a, "fsdp", axis=0, tiled=True)
        joined_proj, out_proj, in_proj, out_ffn = [gather(w) for w in weights]
        small = gather(small)
        mixed, totals, proj = forward_attention(False, content_rows, query_rows, lengths, factor_order, [joined_proj], small)
    vectors = small.reshape(shards, ROWS, LANE)[:, :, :unit].astype(F32)
    flat = vectors.transpose(1, 0, 2).reshape(ROWS, width)
    out_shift, gain_one, shift_one, ffn_shift, gain_two, shift_two = [flat[k] for k in range(2, 8)]
    in_shift = vectors[:, 8:12].reshape(-1)
    mixed_rows = mixed.reshape(2 * row_count, width)
    input_rows = jnp.concatenate([content_rows, query_rows], 0).astype(F32)
    branch = jnp.dot(mixed_rows, out_proj, preferred_element_type=F32) + out_shift
    first_out, normed_one, inverse_one = norm_forward(input_rows + branch, gain_one, shift_one)
    first_low = first_out.astype(BF16)
    hidden_in = jnp.dot(first_low, in_proj, preferred_element_type=F32) + in_shift
    hidden_low = gelu_value(hidden_in).astype(BF16)
    ffn_rows = jnp.dot(hidden_low, out_ffn, preferred_element_type=F32) + ffn_shift
    final_rows, normed_two, inverse_two = norm_forward(first_low.astype(F32) + ffn_rows, gain_two, shift_two)
    valid_rows = (jnp.arange(seq_len)[None, :] < lengths[:, None]).reshape(row_count, 1).astype(F32)
    valid_both = jnp.concatenate([valid_rows, valid_rows], 0)
    upstream = jnp.concatenate([content_cot.reshape(row_count, width), query_cot.reshape(row_count, width)], 0).astype(F32) * valid_both
    grad_sum_two, grad_gain_two, grad_shift_two = norm_backward(upstream, normed_two, inverse_two, gain_two)
    grad_ffn = grad_sum_two.astype(BF16)
    grad_ffn_shift = jnp.sum(grad_ffn.astype(F32), 0)
    grad_out_ffn = rows_inner(hidden_low, grad_ffn).astype(BF16)
    grad_hidden = (times_transpose(grad_ffn, out_ffn) * gelu_slope(hidden_in)).astype(BF16)
    grad_in_shift = jnp.sum(grad_hidden.astype(F32), 0)
    grad_in_proj = rows_inner(first_low, grad_hidden).astype(BF16)
    grad_first = grad_sum_two + times_transpose(grad_hidden, in_proj)
    grad_sum_one, grad_gain_one, grad_shift_one = norm_backward(grad_first, normed_one, inverse_one, gain_one)
    grad_branch = grad_sum_one.astype(BF16)
    grad_out_shift = jnp.sum(grad_branch.astype(F32), 0)
    grad_out_proj = rows_inner(mixed_rows, grad_branch).astype(BF16)
    grad_mixed = times_transpose(grad_branch, out_proj).astype(BF16)
    ready = [grad_in_proj, grad_out_ffn, grad_out_proj] if linked else []
    early, grads, grad_table = backward_attention(linked, proj, grad_mixed, mixed_rows, totals, lengths, factor_order, small, ready)
    grad_q = rows_inner(content_rows, grads[0]) + rows_inner(query_rows, grads[3])
    grad_joined = jnp.concatenate([grad_q, rows_inner(content_rows, grads[1]), rows_inner(content_rows, grads[2])], 1).astype(BF16)
    low_sums = jnp.sum(grads.astype(F32), 1)
    grad_proj_shift = jnp.concatenate([low_sums[0] + low_sums[3], low_sums[2]])
    small_grads = (grad_proj_shift, grad_out_shift, grad_gain_one, grad_shift_one, grad_ffn_shift, grad_gain_two, grad_shift_two, grad_in_shift)
    packed = pack_small([g.reshape(shards, -1, unit) for g in small_grads] + [grad_table.reshape(shards, -1, HEADS)], shards)
    if linked:
        packed = packed.reshape(4, 2, ROWS, LANE).transpose(1, 0, 2, 3).reshape(8 * ROWS, LANE)
        sum_joined, mine = reduce_rest([grad_joined], packed)
        sum_in, sum_out, sum_proj = early
    else:
        scatter = lambda a: lax.psum(lax.psum_scatter(a, "fsdp", scatter_dimension=0, tiled=True), "rep")
        sum_joined, sum_in, sum_out, sum_proj = [scatter(a) for a in (grad_joined, grad_in_proj, grad_out_ffn, grad_out_proj)]
        mine = scatter(packed)
    sum_joined, sum_in, sum_out, sum_proj = [a.astype(F32) for a in (sum_joined, sum_in, sum_out, sum_proj)]
    content_grad_rows = grad_sum_one[:row_count] + (
        times_transpose(grads[0], joined_proj[:, :width])
        + times_transpose(grads[1], joined_proj[:, width : 2 * width])
        + times_transpose(grads[2], joined_proj[:, 2 * width :])
    )
    query_grad_rows = grad_sum_one[row_count:] + times_transpose(grads[3], joined_proj[:, :width])
    vec = lambda k: mine[k, :unit]
    block_shape = (seq_count, seq_len, width)
    return (
        final_rows[:row_count].reshape(block_shape).astype(BF16),
        final_rows[row_count:].reshape(block_shape).astype(BF16),
        content_grad_rows.reshape(block_shape).astype(BF16),
        query_grad_rows.reshape(block_shape).astype(BF16),
        sum_joined,
        mine[0:2, :unit].reshape(-1),
        sum_proj,
        vec(2),
        vec(3),
        vec(4),
        mine[TABLE_ROW : TABLE_ROW + rel_table.shape[0], :HEADS],
        sum_in,
        mine[8:12, :unit].reshape(-1),
        sum_out,
        vec(5),
        vec(6),
        vec(7),
    )


def solution(mesh):
    in_specs = (
        P(("rep", "fsdp"), None, None),
        P(("rep", "fsdp"), None, None),
        P(("rep", "fsdp")),
        P(("rep", "fsdp"), None),
        P("fsdp", None),
        P("fsdp"),
        P("fsdp", None),
        P("fsdp"),
        P("fsdp"),
        P("fsdp"),
        P("fsdp", None),
        P("fsdp", None),
        P("fsdp"),
        P("fsdp", None),
        P("fsdp"),
        P("fsdp"),
        P("fsdp"),
        P(("rep", "fsdp"), None, None),
        P(("rep", "fsdp"), None, None),
    )
    out_specs = (
        P(("rep", "fsdp"), None, None),
        P(("rep", "fsdp"), None, None),
        P(("rep", "fsdp"), None, None),
        P(("rep", "fsdp"), None, None),
        P("fsdp", None),
        P("fsdp"),
        P("fsdp", None),
        P("fsdp"),
        P("fsdp"),
        P("fsdp"),
        P("fsdp", None),
        P("fsdp", None),
        P("fsdp"),
        P("fsdp", None),
        P("fsdp"),
        P("fsdp"),
        P("fsdp"),
    )
    return jax.shard_map(
        functools.partial(on_device, tuple(mesh.shape[a] for a in mesh.axis_names)),
        mesh=mesh,
        in_specs=in_specs,
        out_specs=out_specs,
        check_vma=False,
    )
```

```python
import functools
import math

import jax
import jax.numpy as jnp
import numpy as np
from jax import lax
from jax.experimental import pallas as pl
from jax.experimental.pallas import tpu as pltpu
from jax.sharding import PartitionSpec as P

HEADS = 12
HEAD = 64
BUCKETS = 32
MAX_DIST = 128
LANE = 128
NEAR = 512
ROWS = 16
TABLE_ROW = 12
MASKED = -1e30
LOG2E = 1.4426950408889634
LN2 = 0.6931471805599453
F32 = jnp.float32
BF16 = jnp.bfloat16
MESH = pl.DeviceIdType.MESH
VMEM_BYTES = 60 * 2**20
eps_norm = 1e-05
inv_root_tau = 0.3989422804014327


def bucket_of(offset):
    half_count = BUCKETS // 2
    result = (offset < 0).astype(np.int64) * half_count
    distance = np.abs(offset)
    exact_count = half_count // 2
    fraction = np.log(np.maximum(distance, 1) / exact_count) / np.log(MAX_DIST / exact_count)
    beyond = exact_count + (fraction * (half_count - exact_count)).astype(np.int64)
    beyond = np.minimum(beyond, half_count - 1)
    result = result + np.where(distance < exact_count, distance, beyond)
    return result.astype(np.int32)


def nt(a, b):
    return lax.dot_general(a, b, (((1,), (1,)), ((), ())), preferred_element_type=F32)


def nn(a, b):
    return lax.dot_general(a, b, (((1,), (0,)), ((), ())), preferred_element_type=F32)


def signed_places():
    places = np.arange(NEAR)
    return np.where(places < NEAR - LANE, places, places - NEAR)


def near_onehot(sign):
    offset = sign * (signed_places() - LANE)
    return (bucket_of(offset)[None, :] == np.arange(BUCKETS)[:, None]).astype(np.float32)


def skewed(row, width):
    wide = jnp.broadcast_to(row, (LANE, NEAR))
    return pltpu.roll(wide, 0, 1, stride=1, stride_axis=0)[:, :width]


def tile_bias(near, far_pos, far_neg, seq_len, sign):
    blocks = seq_len // LANE
    rows = []
    for rb in range(blocks):
        parts = []
        for cb in range(blocks):
            e = cb - rb
            if abs(e) <= 1:
                parts.append(near[:, (e + 1) * LANE : (e + 2) * LANE])
            else:
                parts.append(jnp.broadcast_to(far_pos if e * sign > 0 else far_neg, (LANE, LANE)))
        rows.append(jnp.concatenate(parts, 1))
    return rows


def head_lanes(shape, t):
    lane = lax.broadcasted_iota(jnp.int32, shape, 1)
    return (lane >= t * HEAD) & (lane < (t + 1) * HEAD)


def flip(v, m):
    a, b = v // 2, v % 2
    if m & 2:
        a = 1 - a
    if m & 1:
        b = 1 - b
    return a * 2 + b


def table_onehot(sign, shards):
    per_shard = BUCKETS // shards
    result = np.zeros((shards * ROWS, NEAR + LANE), np.float32)
    near = near_onehot(sign)
    for bucket in range(BUCKETS):
        row = bucket // per_shard * ROWS + TABLE_ROW + bucket % per_shard
        result[row, :NEAR] = near[bucket]
        result[row, NEAR] = bucket == BUCKETS // 2 - 1
        result[row, NEAR + 1] = bucket == BUCKETS - 1
    return jnp.asarray(result, BF16)


class Links:
    def __init__(self, send, recv):
        self.send, self.recv = send, recv
        self.r = lax.axis_index("rep")
        self.f = lax.axis_index("fsdp")
        self.y, self.x = self.r // 2, self.r % 2
        self.z, self.c = self.f // 2, self.f % 2
        self.xr, self.yr = flip(self.r, 1), flip(self.r, 2)
        self.sib = self.z * 2 + 1 - self.c

    def along(self, s):
        return ((self.z + s) % 4) * 2 + self.c

    def copy(self, at, src, dst, rep, fsdp):
        return pltpu.make_async_remote_copy(
            src_ref=src, dst_ref=dst, send_sem=self.send.at[at], recv_sem=self.recv.at[at],
            device_id={"rep": rep, "fsdp": fsdp}, device_id_type=MESH)

    def barrier(self):
        sem = pltpu.get_barrier_semaphore()
        peers = [(self.r, self.along(s)) for s in (1, 2, 3)]
        peers += [(self.xr, self.f), (self.yr, self.f), (self.r, self.sib)]
        for rep, fsdp in peers:
            pl.semaphore_signal(sem, inc=1, device_id={"rep": rep, "fsdp": fsdp}, device_id_type=MESH)
        pl.semaphore_wait(sem, len(peers))


def quarter_of(ref, rows, cols, owner, q, part=None):
    pr, pc = rows // 2, cols // 2
    r0, c0 = owner * rows + (q // 2) * pr, (q % 2) * pc
    if part is not None:
        if pr % 32 == 0:
            r0, pr = r0 + part * (pr // 2), pr // 2
        else:
            first = (pc // LANE + 1) // 2 * LANE
            c0, pc = (c0, first) if part == 0 else (c0 + first, pc - first)
    return ref.at[pl.ds(pl.multiple_of(r0, 16), pr), pl.ds(pl.multiple_of(c0, LANE), pc)]


class Gather(Links):
    SLOTS = 12

    def __init__(self, shapes, shards, fulls, send, recv):
        super().__init__(send, recv)
        self.shapes, self.shards, self.fulls = shapes, shards, fulls

    def z_send(self, w, s):
        rows, cols = self.shapes[w]
        src = quarter_of(self.shards[w], rows, cols, 0, self.r)
        dst = quarter_of(self.fulls[w], rows, cols, self.f, self.r)
        return self.copy((w, s, 0), src, dst, self.r, self.along(s))

    def hop(self, w, s, slot, q, rep, fsdp, part=None):
        rows, cols = self.shapes[w]
        place = quarter_of(self.fulls[w], rows, cols, self.along(4 - s), q, part)
        return self.copy((w, s, slot), place, place, rep, fsdp)

    def own_place(self, w):
        rows = self.shapes[w][0]
        return self.fulls[w].at[pl.ds(pl.multiple_of(self.f * rows, 16), rows), :]

    def own_sib(self, w):
        return self.copy((w, 0, 0), self.shards[w], self.own_place(w), self.r, self.sib)

    def own_here(self, w):
        return pltpu.make_async_copy(self.shards[w], self.own_place(w), self.send.at[w, 0, 1])

    def h_x(self, w, s):
        return self.hop(w, s, 1, self.r, self.xr, self.f)

    def h_y(self, w, s):
        return self.hop(w, s, 2, self.r, self.yr, self.f)

    def h_dy(self, w, s):
        return self.hop(w, s, 3, self.xr, self.yr, self.f, 0)

    def h_dx(self, w, s):
        return self.hop(w, s, 4, self.yr, self.xr, self.f, 1)

    def h_sib(self, w, s, m):
        return self.hop(w, s, 5 + m, flip(self.r, m), self.r, self.sib)

    def start(self, w):
        for s in (1, 2, 3):
            self.z_send(w, s).start()
        self.own_sib(w).start()
        self.own_here(w).start()

    def relay_z(self, w, s):
        self.z_send(w, s).wait_recv()
        self.h_x(w, s).start()
        self.h_y(w, s).start()
        self.h_sib(w, s, 0).start()

    def relay_xy(self, w, s):
        self.h_x(w, s).wait_recv()
        self.h_dy(w, s).start()
        self.h_sib(w, s, 1).start()
        self.h_y(w, s).wait_recv()
        self.h_dx(w, s).start()
        self.h_sib(w, s, 2).start()

    def relay_diag(self, w, s):
        self.h_dy(w, s).wait_recv()
        self.h_dx(w, s).wait_recv()
        self.h_sib(w, s, 3).start()

    def arrive(self, w):
        for s in (1, 2, 3):
            for m in range(4):
                self.h_sib(w, s, m).wait_recv()
        self.own_sib(w).wait_recv()
        self.own_here(w).wait()

    def drain(self, w):
        for s in (1, 2, 3):
            for d in (self.z_send(w, s), self.h_x(w, s), self.h_y(w, s), self.h_dy(w, s), self.h_dx(w, s)):
                d.wait_send()
            for m in range(4):
                self.h_sib(w, s, m).wait_send()
        self.own_sib(w).wait_send()

    def small_place(self, owner):
        return self.small_full.at[pl.ds(pl.multiple_of(owner * ROWS, ROWS), ROWS), :]

    def small_copies(self):
        w = len(self.shapes)
        far = [self.copy((w, s, 0), self.small_shard, self.small_place(self.f), self.r, self.along(s)) for s in (1, 2, 3)]
        own = self.copy((w, 0, 0), self.small_shard, self.small_place(self.f), self.r, self.sib)
        here = pltpu.make_async_copy(self.small_shard, self.small_place(self.f), self.send.at[w, 0, 1])
        sib = []
        for s in (1, 2, 3):
            place = self.small_place(self.along(4 - s))
            sib.append(self.copy((w, s, 1), place, place, self.r, self.sib))
        return far, own, here, sib


class Reduce(Links):
    SLOTS = 8

    def __init__(self, shapes, grads, outs, bufs, send, recv):
        super().__init__(send, recv)
        self.shapes, self.grads, self.outs, self.bufs = shapes, grads, outs, bufs

    @staticmethod
    def scratch(shapes):
        out = []
        for rows, cols in shapes:
            out += [
                pltpu.VMEM((4, rows, cols), BF16),
                pltpu.VMEM((4, rows, cols), BF16),
                pltpu.VMEM((2, rows, cols // 2), BF16),
                pltpu.VMEM((2, rows // 2, cols), BF16),
                pltpu.VMEM((4, rows // 2, cols // 2), BF16),
                pltpu.VMEM((3, rows // 2, cols // 2), BF16),
                pltpu.VMEM((rows // 2, cols // 2), BF16),
            ]
        return out

    def shard(self, w, s, core):
        rows = self.shapes[w][0]
        at = pl.multiple_of((((self.z + s) % 4) * 2 + core) * rows, 16)
        return self.grads[w].at[pl.ds(at, rows), :]

    def half_rows(self, w, bit):
        h = self.shapes[w][0] // 2
        return pl.ds(pl.multiple_of(bit * h, 16), h)

    def half_cols(self, w, bit):
        h = self.shapes[w][1] // 2
        return pl.ds(pl.multiple_of(bit * h, 128), h)

    def core_copy(self, w, s):
        return self.copy((w, s, 0), self.shard(w, s, 1 - self.c), self.bufs[w][1].at[s], self.r, self.sib)

    def core_load(self, w, s):
        return pltpu.make_async_copy(self.shard(w, s, self.c), self.bufs[w][0].at[s], self.send.at[w, s, 7])

    def start(self, w, s):
        self.core_copy(w, s).start()
        self.core_load(w, s).start()

    def x_first(self, s):
        return s % 2 == 1

    def first_copy(self, w, s):
        own, hx, hy = self.bufs[w][0], self.bufs[w][2], self.bufs[w][3]
        if self.x_first(s):
            return self.copy((w, s, 1), own.at[s, :, self.half_cols(w, 1 - self.x)], hx.at[s // 2], self.xr, self.f)
        return self.copy((w, s, 1), own.at[s, self.half_rows(w, 1 - self.y), :], hy.at[s // 2], self.yr, self.f)

    def add_core(self, w, s):
        self.core_copy(w, s).wait_recv()
        self.core_load(w, s).wait()
        own, got = self.bufs[w][0], self.bufs[w][1]
        own[s] = own[s] + got[s]
        self.first_copy(w, s).start()

    def second_copy(self, w, s):
        own, quarter = self.bufs[w][0], self.bufs[w][4]
        if self.x_first(s):
            src = own.at[s, self.half_rows(w, 1 - self.y), self.half_cols(w, self.x)]
            return self.copy((w, s, 2), src, quarter.at[s], self.yr, self.f)
        src = own.at[s, self.half_rows(w, self.y), self.half_cols(w, 1 - self.x)]
        return self.copy((w, s, 2), src, quarter.at[s], self.xr, self.f)

    def add_first(self, w, s):
        self.first_copy(w, s).wait_recv()
        own, hx, hy = self.bufs[w][0], self.bufs[w][2], self.bufs[w][3]
        if self.x_first(s):
            at = (s, slice(None), self.half_cols(w, self.x))
            own[at] = own[at] + hx[s // 2]
        else:
            at = (s, self.half_rows(w, self.y), slice(None))
            own[at] = own[at] + hy[s // 2]
        self.second_copy(w, s).start()

    def far_copy(self, w, s):
        own, far = self.bufs[w][0], self.bufs[w][5]
        src = own.at[s, self.half_rows(w, self.y), self.half_cols(w, self.x)]
        return self.copy((w, s, 3), src, far.at[s - 1], self.r, self.along(s))

    def add_second(self, w, s):
        self.second_copy(w, s).wait_recv()
        own, quarter = self.bufs[w][0], self.bufs[w][4]
        at = (s, self.half_rows(w, self.y), self.half_cols(w, self.x))
        own[at] = own[at] + quarter[s]
        if s > 0:
            self.far_copy(w, s).start()

    def place(self, w, q, part=None):
        rows, cols = self.shapes[w]
        h = rows // 2
        r0, n = (q // 2) * h, h
        if part is not None:
            n = h // 32 * 16 if part == 0 else h - h // 32 * 16
            r0 = r0 if part == 0 else r0 + h // 32 * 16
        return self.outs[w].at[pl.ds(pl.multiple_of(r0, 16), n), self.half_cols(w, q % 2)]

    def out_local(self, w):
        return pltpu.make_async_copy(self.bufs[w][6], self.place(w, self.r), self.send.at[w, 0, 3])

    def out_x(self, w):
        return self.copy((w, 0, 4), self.bufs[w][6], self.place(w, self.r), self.xr, self.f)

    def out_y(self, w):
        return self.copy((w, 0, 5), self.bufs[w][6], self.place(w, self.r), self.yr, self.f)

    def out_dy(self, w):
        p = self.place(w, flip(self.r, 1), 0)
        return self.copy((w, 1, 4), p, p, self.yr, self.f)

    def out_dx(self, w):
        p = self.place(w, flip(self.r, 2), 1)
        return self.copy((w, 1, 5), p, p, self.xr, self.f)

    def total(self, w):
        own, far, done = self.bufs[w][0], self.bufs[w][5], self.bufs[w][6]
        for s in (1, 2, 3):
            self.far_copy(w, s).wait_recv()
        at = (0, self.half_rows(w, self.y), self.half_cols(w, self.x))
        done[...] = (own[at].astype(F32) + far[0].astype(F32) + far[1].astype(F32) + far[2].astype(F32)).astype(BF16)
        self.out_x(w).start()
        self.out_y(w).start()
        self.out_local(w).start()

    def relay(self, w):
        self.out_x(w).wait_recv()
        self.out_dy(w).start()
        self.out_y(w).wait_recv()
        self.out_dx(w).start()

    def finish(self, w):
        for s in range(4):
            self.core_copy(w, s).wait_send()
            self.first_copy(w, s).wait_send()
            self.second_copy(w, s).wait_send()
            if s:
                self.far_copy(w, s).wait_send()
        self.out_local(w).wait()
        self.out_x(w).wait_send()
        self.out_y(w).wait_send()
        for d in (self.out_dy(w), self.out_dx(w)):
            d.wait_send()
            d.wait_recv()


def plan(red, n, order):
    items = [(w, s) for w in order for s in (1, 2, 3, 0)]
    ticks = []
    m = len(items)
    for k in range(m + 4):
        acts = []
        if k < m:
            acts.append(functools.partial(red.add_core, *items[k]))
        if 0 <= k - 2 < m:
            acts.append(functools.partial(red.add_first, *items[k - 2]))
        if 0 <= k - 4 < m:
            w, s = items[k - 4]
            acts.append(functools.partial(red.add_second, w, s))
            if s == 0:
                j = order.index(w)
                if j > 0:
                    acts.append(functools.partial(red.total, order[j - 1]))
                if j > 1:
                    acts.append(functools.partial(red.relay, order[j - 2]))
        ticks.append(acts)
    tail = [functools.partial(red.total, order[-1])]
    if n > 1:
        tail.append(functools.partial(red.relay, order[-2]))
    tail.append(functools.partial(red.relay, order[-1]))
    ticks.append(tail)
    ticks.append([functools.partial(red.finish, w) for w in order])
    return items, ticks


def spread_rows(small, row, step, count, unit):
    width = count * unit
    lane = lax.broadcasted_iota(jnp.int32, (8, width), 1)
    total = jnp.zeros((8, width), F32)
    for k in range(count):
        one = jnp.broadcast_to(small[row[k] : row[k] + 1, :], (8, LANE))
        wide = jnp.concatenate([one, jnp.zeros((8, width - LANE), F32)], 1)
        wide = jnp.where(lane < unit, wide, 0.0)
        total = total + (pltpu.roll(wide, k * unit, 1) if k else wide)
    return total[0:1]


def fill_mask(mask_ref, ord_ref, limit, s, seq_len, turned):
    blocks = seq_len // LANE
    own = ord_ref[pl.ds(s, 1), :].astype(F32)
    cols = jnp.broadcast_to(own, (LANE, seq_len)).T
    for rb in range(blocks):
        col = cols[rb * LANE : (rb + 1) * LANE, :]
        rank = jnp.concatenate([col] * blocks, 1)
        place = lax.broadcasted_iota(jnp.int32, (LANE, seq_len), 0 if turned else 1)
        if turned:
            place = place + rb * LANE
        order = (rank <= own) if turned else (own <= rank)
        ok = (place < limit) & ((place == 0) | order)
        mask_ref[s, rb * LANE : (rb + 1) * LANE, :] = jnp.where(ok, 0.0, MASKED)


def fill_near(near_ref, small, onehot_ref):
    near_ref[...] = lax.dot_general(small, onehot_ref[...], (((0,), (0,)), ((), ())), preferred_element_type=F32) * LOG2E


def attention_step(hp, s, proj, mask_ref, near_ref, put_out, put_total):
    query_c, keys, value, query_g = proj
    seq_len = keys.shape[0]
    blocks = seq_len // LANE
    values = jnp.concatenate([value, jnp.ones((seq_len, LANE), BF16)], 1)
    lane = lax.broadcasted_iota(jnp.int32, (seq_len, LANE), 1)
    diag_r = lax.broadcasted_iota(jnp.int32, (LANE, LANE), 0)
    diag_c = lax.broadcasted_iota(jnp.int32, (LANE, LANE), 1)
    outs = [[], []]
    totals = [jnp.zeros((seq_len, LANE), F32), jnp.zeros((seq_len, LANE), F32)]
    for t in range(2):
        head = hp * 2 + t
        sel = head_lanes((seq_len, LANE), t)
        head_row = near_ref[pl.ds(head, 1), :]
        near = skewed(head_row[:, :NEAR], 3 * LANE)
        bias = tile_bias(near, head_row[:, NEAR : NEAR + 1], head_row[:, NEAR + 1 : NEAR + 2], seq_len, -1)
        for stream in range(2):
            query = jnp.where(sel, query_g if stream else query_c, jnp.zeros((), BF16))
            raw = nt(query, keys)
            probs = []
            maxes = []
            for rb in range(blocks):
                part = raw[rb * LANE : (rb + 1) * LANE, :] + (bias[rb] + mask_ref[s, rb * LANE : (rb + 1) * LANE, :])
                if stream == 1:
                    hit = diag_r == diag_c
                    if rb == 0:
                        hit = hit & (diag_c != 0)
                    pieces = []
                    if rb > 0:
                        pieces.append(part[:, : rb * LANE])
                    pieces.append(jnp.where(hit, MASKED, part[:, rb * LANE : (rb + 1) * LANE]))
                    if rb < blocks - 1:
                        pieces.append(part[:, (rb + 1) * LANE :])
                    part = jnp.concatenate(pieces, 1)
                top = jnp.max(part, 1, keepdims=True)
                probs.append(jnp.exp2(part - top).astype(BF16))
                maxes.append(jnp.broadcast_to(top, (LANE, LANE)))
            mixed = nn(jnp.concatenate(probs, 0), values)
            total = mixed[:, LANE:]
            outs[stream].append(mixed[:, :LANE] / total)
            log_total = jnp.concatenate(maxes, 0) + jnp.log2(total)
            hi = log_total.astype(BF16).astype(F32)
            totals[stream] = jnp.where(lane == head, -hi, jnp.where(lane == head + HEAD, hi - log_total, totals[stream]))
    first = head_lanes((seq_len, LANE), 0)
    mine = (lane == hp * 2) | (lane == hp * 2 + 1) | (lane == hp * 2 + HEAD) | (lane == hp * 2 + 1 + HEAD)
    for stream in range(2):
        put_out(stream, jnp.where(first, outs[stream][0], outs[stream][1]).astype(BF16))
        put_total(stream, totals[stream].astype(BF16), mine)


def forward_kernel(shapes, linked, len_ref, content_ref, query_ref, ord_ref, onehot_ref, *refs):
    n = len(shapes)
    if linked:
        shards, small_shard, refs = refs[:n], refs[n], refs[n + 1 :]
        full_refs, refs = refs[: n - 1], refs[n - 1 :]
        joined_out, small_out, refs = refs[0], refs[1], refs[2:]
    else:
        joined_in, small_in, refs = refs[0], refs[1], refs[2:]
    mixed_ref, total_ref, proj_out, joined_ref, small_ref, proj_ref, mask_ref, near_ref, own_sem = refs[:9]
    hp = pl.program_id(0)
    s = pl.program_id(1)
    step = hp * pl.num_programs(1) + s
    steps = (HEADS // 2) * total_ref.shape[1]
    seqs = total_ref.shape[1]
    seq_len = total_ref.shape[2]
    row_count, width = content_ref.shape
    if linked:
        send, recv = refs[9:]
        net = Gather(shapes, shards, (joined_ref,) + tuple(full_refs), send, recv)
        net.small_shard, net.small_full = small_shard, small_ref
    proj_copy = pltpu.make_async_copy(proj_ref, proj_out, own_sem.at[0])

    @pl.when(step == 0)
    def _():
        if linked:
            net.barrier()
            far, own, here, sib = net.small_copies()
            for d in far + [own, here]:
                d.start()
            for w in range(n):
                net.start(w)
            for s0 in range(seqs):
                fill_mask(mask_ref, ord_ref, len_ref[s0], s0, seq_len, False)
            for d, e in zip(far, sib):
                d.wait_recv()
                e.start()
            for k in (1, 2, 3):
                net.relay_z(0, k)
            for k in (1, 2, 3):
                net.relay_xy(0, k)
            for k in (1, 2, 3):
                net.relay_z(1, k)
            for k in (1, 2, 3):
                net.relay_diag(0, k)
            for k in (1, 2, 3):
                net.relay_z(2, k)
            for d in far:
                d.wait_send()
            for d in [own] + sib:
                d.wait_send()
                d.wait_recv()
            here.wait()
            net.arrive(0)
            pltpu.make_async_copy(joined_ref, joined_out, own_sem.at[1]).start()
            pltpu.make_async_copy(small_ref, small_out, own_sem.at[2]).start()
        else:
            fetch = (pltpu.make_async_copy(joined_in, joined_ref, own_sem.at[1]), pltpu.make_async_copy(small_in, small_ref, own_sem.at[2]))
            for d in fetch:
                d.start()
            for s0 in range(seqs):
                fill_mask(mask_ref, ord_ref, len_ref[s0], s0, seq_len, False)
            for d in fetch:
                d.wait()
        fill_near(near_ref, small_ref[...], onehot_ref)
        small = small_ref[...].astype(F32)
        shards_all = small.shape[0] // ROWS
        unit = width // shards_all
        half = shards_all // 2
        shift_q = spread_rows(small, [k // 2 * ROWS + k % 2 for k in range(2 * half)], 0, 2 * half, unit)
        shift_v = spread_rows(small, [(half + k // 2) * ROWS + k % 2 for k in range(2 * half)], 0, 2 * half, unit)
        scale = LOG2E / math.sqrt(HEAD)
        chunk = 256

        @pl.loop(0, row_count // chunk)
        def _(i):
            rows = pl.ds(pl.multiple_of(i * chunk, chunk), chunk)
            rows_c = content_ref[rows, :]
            proj_ref[rows, 0:width] = ((nn(rows_c, joined_ref[:, 0:width]) + shift_q) * scale).astype(BF16)
            proj_ref[rows, width : 2 * width] = nn(rows_c, joined_ref[:, width : 2 * width]).astype(BF16)
            proj_ref[rows, 2 * width : 3 * width] = (nn(rows_c, joined_ref[:, 2 * width : 3 * width]) + shift_v).astype(BF16)
            proj_ref[rows, 3 * width : 4 * width] = ((nn(query_ref[rows, :], joined_ref[:, 0:width]) + shift_q) * scale).astype(BF16)

        proj_copy.start()

    if linked:
        agenda = {
            1: [(net.relay_xy, 1, (1, 2, 3))],
            3: [(net.relay_z, 3, (1, 2, 3))],
            4: [(net.relay_xy, 2, (1,))],
            5: [(net.relay_xy, 2, (2,)), (net.relay_diag, 1, (1, 2, 3))],
            6: [(net.relay_xy, 2, (3,))],
            8: [(net.relay_diag, 2, (1, 2)), (net.relay_xy, 3, (1,))],
            9: [(net.relay_diag, 2, (3,)), (net.relay_xy, 3, (2,))],
            10: [(net.relay_xy, 3, (3,))],
        }
        for at, acts in agenda.items():

            @pl.when(step == min(at, steps - 1))
            def _():
                for act, w, ks in acts:
                    for k in ks:
                        act(w, k)

    here_rows = pl.ds(pl.multiple_of(s * seq_len, seq_len), seq_len)
    column = lambda k: pl.ds(pl.multiple_of(k * width + hp * LANE, LANE), LANE)
    proj = [proj_ref[here_rows, column(k)] for k in range(4)]

    def put_out(stream, value):
        mixed_ref[stream] = value

    def put_total(stream, value, mine):
        @pl.when(hp == 0)
        def _():
            total_ref[stream, s] = value

        @pl.when(hp > 0)
        def _():
            total_ref[stream, s] = jnp.where(mine, value, total_ref[stream, s])

    attention_step(hp, s, proj, mask_ref, near_ref, put_out, put_total)

    @pl.when(step == steps - 1)
    def _():
        proj_copy.wait()
        if linked:
            pltpu.make_async_copy(joined_ref, joined_out, own_sem.at[1]).wait()
            pltpu.make_async_copy(small_ref, small_out, own_sem.at[2]).wait()
            for k in (1, 2, 3):
                net.relay_diag(3, k)
            for w in range(n):
                if w:
                    net.arrive(w)
                net.drain(w)


def forward_attention(linked, content_rows, query_rows, lengths, order, weights, small):
    row_count, width = content_rows.shape
    seqs, seq_len = order.shape
    pairs = width // LANE
    shards = 8 if linked else small.shape[0] // ROWS
    onehot = table_onehot(-1, shards)
    shapes = [w.shape for w in weights] if linked else []
    n = len(shapes)
    anywhere = pl.BlockSpec(memory_space=pl.ANY)
    inside = pl.BlockSpec(memory_space=pltpu.VMEM)
    block3 = pl.BlockSpec((2, seq_len, LANE), lambda h, s: (0, s, h))
    joined_shape = (width, 3 * width)
    small_shape = (shards * ROWS, LANE)
    out_specs, out_shape = [], []
    if linked:
        out_specs += [anywhere] * (n + 1)
        out_shape += [jax.ShapeDtypeStruct((8 * a, b), BF16) for a, b in shapes[1:]]
        out_shape += [jax.ShapeDtypeStruct(joined_shape, BF16), jax.ShapeDtypeStruct(small_shape, BF16)]
    out_specs += [block3, pl.BlockSpec((2, seqs, seq_len, LANE), lambda h, s: (0, 0, 0, 0)), anywhere]
    out_shape += [
        jax.ShapeDtypeStruct((2, row_count, width), BF16),
        jax.ShapeDtypeStruct((2, seqs, seq_len, LANE), BF16),
        jax.ShapeDtypeStruct((row_count, 4 * width), BF16),
    ]
    scratch = [
        pltpu.VMEM(joined_shape, BF16),
        pltpu.VMEM(small_shape, BF16),
        pltpu.VMEM((row_count, 4 * width), BF16),
        pltpu.VMEM((seqs, seq_len, seq_len), F32),
        pltpu.VMEM((LANE, NEAR + LANE), F32),
        pltpu.SemaphoreType.DMA((3,)),
    ]
    if linked:
        scratch += [pltpu.SemaphoreType.DMA((n + 1, 4, Gather.SLOTS)), pltpu.SemaphoreType.DMA((n + 1, 4, Gather.SLOTS))]
    flops = 2 * row_count * width * 4 * width + 8 * row_count * seq_len * width
    return pl.pallas_call(
        functools.partial(forward_kernel, shapes, linked),
        grid=(pairs, seqs),
        in_specs=[pl.BlockSpec(memory_space=pltpu.SMEM), inside, inside, inside, inside] + [anywhere] * (n + 1 if linked else 2),
        out_specs=out_specs,
        out_shape=out_shape,
        scratch_shapes=scratch,
        cost_estimate=pl.CostEstimate(flops=flops, bytes_accessed=30 * 2**20, transcendentals=4 * row_count * seq_len * HEADS),
        compiler_params=pltpu.CompilerParams(
            dimension_semantics=("arbitrary", "arbitrary"), vmem_limit_bytes=VMEM_BYTES,
            **(dict(collective_id=0, has_side_effects=True) if linked else {})),
        name="attention_forward",
    )(lengths, content_rows, query_rows, order, onehot, *(list(weights) + [small]))


def backward_kernel(shapes, linked, len_ref, q_ref, k_ref, v_ref, g_ref, dc_ref, dg_ref, oc_ref, og_ref, tot_ref, ord_ref, small_ref, onehot_ref, *refs):
    n = len(shapes)
    grads, refs = refs[:n], refs[n:]
    outs, refs = refs[:n], refs[n:]
    grad_ref, sums_ref, mask_ref, acc_ref, near_ref = refs[:5]
    refs = refs[5:]
    hp = pl.program_id(0)
    s = pl.program_id(1)
    last = pl.num_programs(1) - 1
    step = hp * pl.num_programs(1) + s
    seq_len = q_ref.shape[0]
    blocks = seq_len // LANE
    half = seq_len // 2
    steps = (HEADS // 2) * ord_ref.shape[0]
    if linked:
        bufs = [refs[7 * w : 7 * w + 7] for w in range(n)]
        send, recv = refs[7 * n :]
        net = Reduce(shapes, grads, outs, bufs, send, recv)
        items, ticks = plan(net, n, list(range(n)))

        @pl.when(step == 0)
        def _():
            net.barrier()
            for w, k in items:
                net.start(w, k)

        tail = ticks[-2:]
        ticks = ticks[:-2]
        for at in range(1, steps):
            acts = [a for i, t in enumerate(ticks) if 1 + i * (steps - 1) // len(ticks) == at for a in t]

            @pl.when(step == at)
            def _():
                for act in acts:
                    act()

    @pl.when(hp == 0)
    def _():
        fill_mask(mask_ref, ord_ref, len_ref[s], s, seq_len, True)

    @pl.when(step == 0)
    def _():
        fill_near(near_ref, small_ref[...], onehot_ref)

    lane = lax.broadcasted_iota(jnp.int32, (seq_len, LANE), 1)
    ones = jnp.ones((seq_len, LANE), BF16)
    zero = jnp.zeros((), BF16)
    keys = k_ref[...]
    keys_wide = jnp.concatenate([keys, ones], 1)
    values_wide = jnp.concatenate([v_ref[...], ones], 1)
    keys_turned = keys.astype(F32).T.astype(BF16)
    lane_r = lax.broadcasted_iota(jnp.int32, (LANE, LANE), 0)
    lane_c = lax.broadcasted_iota(jnp.int32, (LANE, LANE), 1)
    pick = (lane_r // HEAD == lane_c).astype(BF16)
    grad_keys = None
    grad_values = None
    grad_query = [[], []]
    streams = []
    for src, grad, out, tot in ((q_ref, dc_ref, oc_ref, tot_ref[0, 0]), (g_ref, dg_ref, og_ref, tot_ref[1, 0])):
        g = grad[...]
        delta = nn((g.astype(F32) * out[...].astype(F32)).astype(BF16), pick)
        streams.append((src[...], g, -delta, tot))
    for t in range(2):
        head = hp * 2 + t
        sel = head_lanes((seq_len, LANE), t)
        head_row = near_ref[pl.ds(head, 1), :]
        near = skewed(head_row[:, :NEAR], 3 * LANE)
        bias = tile_bias(near, head_row[:, NEAR : NEAR + 1], head_row[:, NEAR + 1 : NEAR + 2], seq_len, 1)
        for c0 in range(0, seq_len, half):
            both = None
            for stream in range(2):
                q, g, delta, tot = streams[stream]
                q = jnp.where(sel, q, zero)[c0 : c0 + half]
                g = jnp.where(sel, g, zero)[c0 : c0 + half]
                d = delta[c0 : c0 + half]
                ln = lane[c0 : c0 + half]
                tt = jnp.where((ln == head) | (ln == head + HEAD), tot[c0 : c0 + half], zero)
                dd = jnp.where(ln == t, d, 0.0)
                dhi = dd.astype(BF16)
                dlo = pltpu.roll(dd - dhi.astype(F32), HEAD, 1).astype(BF16)
                raw = nt(keys_wide, jnp.concatenate([q, tt], 1))
                dpr = nt(values_wide, jnp.concatenate([g, dhi + dlo], 1))
                probs, grads = [], []
                for rb in range(blocks):
                    sl = slice(rb * LANE, (rb + 1) * LANE)
                    part = raw[sl] + (bias[rb][:, c0 : c0 + half] + mask_ref[s, sl, c0 : c0 + half])
                    r0 = rb * LANE
                    if stream == 1 and c0 <= r0 < c0 + half:
                        hit = lane_r == lane_c
                        if rb == 0:
                            hit = hit & (lane_r != 0)
                        x0 = r0 - c0
                        diag = jnp.where(hit, MASKED, part[:, x0 : x0 + LANE])
                        pieces = []
                        if x0 > 0:
                            pieces.append(part[:, :x0])
                        pieces.append(diag)
                        if x0 + LANE < half:
                            pieces.append(part[:, x0 + LANE :])
                        part = jnp.concatenate(pieces, 1)
                    p = jnp.exp2(part)
                    probs.append(p.astype(BF16))
                    grads.append(p * dpr[sl])
                low = [x.astype(BF16) for x in grads]
                prob = jnp.concatenate(probs, 0)
                gl = jnp.concatenate(low, 0)
                gv = nn(prob, g)
                gk = nn(gl, q)
                grad_values = gv if grad_values is None else grad_values + gv
                grad_keys = gk if grad_keys is None else grad_keys + gk
                grad_query[stream].append(nn(keys_turned[t * HEAD : (t + 1) * HEAD], gl))
                both = grads if both is None else [a + b for a, b in zip(both, grads)]
            sums = {}
            for rb in range(blocks):
                for cb in range(half // LANE):
                    e = cb + c0 // LANE - rb
                    e = max(-2, min(2, e))
                    x = both[rb][:, cb * LANE : (cb + 1) * LANE]
                    sums[e] = x if e not in sums else sums[e] + x
            for e, x in sums.items():
                lanes = slice((e + 2) * LANE, (e + 3) * LANE)
                fresh = c0 == 0
                if fresh:
                    @pl.when(s == 0)
                    def _():
                        acc_ref[t, :, lanes] = x

                    @pl.when(s > 0)
                    def _():
                        acc_ref[t, :, lanes] = acc_ref[t, :, lanes] + x
                else:
                    acc_ref[t, :, lanes] = acc_ref[t, :, lanes] + x
            if c0 == 0:
                for e in range(-2, 3):
                    if e not in sums:
                        @pl.when(s == 0)
                        def _():
                            acc_ref[t, :, (e + 2) * LANE : (e + 3) * LANE] = jnp.zeros((LANE, LANE), F32)
    count = seq_len // half
    scale = 1.0 / math.sqrt(HEAD)
    for stream, ref in ((0, 0), (1, 3)):
        pieces = grad_query[stream]
        top = jnp.concatenate(pieces[:count], 1)
        bot = jnp.concatenate(pieces[count:], 1)
        grad_ref[ref] = (jnp.concatenate([top, bot], 0) * scale).T.astype(BF16)
    grad_ref[1] = (grad_keys * LN2).astype(BF16)
    grad_ref[2] = grad_values.astype(BF16)

    @pl.when(s == last)
    def _():
        for t in range(2):
            near = jnp.concatenate([acc_ref[t, :, LANE : 4 * LANE], jnp.zeros((LANE, LANE), F32)], 1)
            mirror = (lane_r + lane_c == LANE - 1).astype(F32)
            flipped = lax.dot_general(mirror, near, (((1,), (0,)), ((), ())), precision=lax.Precision.HIGHEST, preferred_element_type=F32)
            turned = pltpu.roll(flipped, 0, 1, stride=1, stride_axis=0)
            row = jnp.sum(turned, 0, keepdims=True)
            below = jnp.sum(acc_ref[t, :, :LANE], 0, keepdims=True)
            above = jnp.sum(acc_ref[t, :, 4 * LANE :], 0, keepdims=True)
            sums_ref[pl.ds(hp * 2 + t, 1), :] = jnp.concatenate([row, below, above], 1)

    if linked:

        @pl.when(step == steps - 1)
        def _():
            for acts in tail:
                for act in acts:
                    act()


def backward_attention(linked, proj, grad_mixed, mixed, totals, lengths, order, small, weight_grads):
    rows, width = grad_mixed.shape
    seqs, seq_len = order.shape
    pairs = width // LANE
    onehot = table_onehot(1, small.shape[0] // ROWS)
    shapes = [(g.shape[0] // 8, g.shape[1]) for g in weight_grads]
    n = len(shapes)
    block = lambda off: pl.BlockSpec((seq_len, LANE), lambda h, s, off=off: (s, off + h))
    low = pl.BlockSpec((seq_len, LANE), lambda h, s: (seqs + s, h))
    anywhere = pl.BlockSpec(memory_space=pl.ANY)
    inside = pl.BlockSpec(memory_space=pltpu.VMEM)
    sums_shape = (2 * pairs, NEAR + 2 * LANE)
    scratch = [
        pltpu.VMEM((seqs, seq_len, seq_len), F32),
        pltpu.VMEM((2, LANE, 5 * LANE), F32),
        pltpu.VMEM((LANE, NEAR + LANE), F32),
    ]
    if linked:
        scratch += Reduce.scratch(shapes)
        scratch += [pltpu.SemaphoreType.DMA((n, 4, Reduce.SLOTS)), pltpu.SemaphoreType.DMA((n, 4, Reduce.SLOTS))]
    outs = pl.pallas_call(
        functools.partial(backward_kernel, shapes, linked),
        grid=(pairs, seqs),
        in_specs=[
            pl.BlockSpec(memory_space=pltpu.SMEM),
            block(0), block(pairs), block(2 * pairs), block(3 * pairs),
            block(0), low, block(0), low,
            pl.BlockSpec((2, 1, seq_len, LANE), lambda h, s: (0, s, 0, 0)),
            inside, inside, inside,
        ] + [anywhere] * n,
        out_specs=[anywhere] * n + [pl.BlockSpec((4, seq_len, LANE), lambda h, s: (0, s, h)), pl.BlockSpec(sums_shape, lambda h, s: (0, 0))],
        out_shape=[jax.ShapeDtypeStruct(a, BF16) for a in shapes] + [jax.ShapeDtypeStruct((4, rows // 2, width), BF16), jax.ShapeDtypeStruct(sums_shape, F32)],
        scratch_shapes=scratch,
        cost_estimate=pl.CostEstimate(flops=20 * rows * seq_len * width, bytes_accessed=30 * 2**20, transcendentals=2 * rows * seq_len * HEADS),
        compiler_params=pltpu.CompilerParams(
            dimension_semantics=("arbitrary", "arbitrary"), vmem_limit_bytes=VMEM_BYTES,
            **(dict(collective_id=1, has_side_effects=True) if linked else {})),
        name="attention_backward",
    )(lengths, proj, proj, proj, proj, grad_mixed, grad_mixed, mixed, mixed, totals, order, small, onehot, *weight_grads)
    sums = outs[n + 1]
    fold = np.zeros((sums_shape[1], BUCKETS), np.float32)
    fold[:NEAR] = np.roll(near_onehot(1).T, LANE - 1, 0)
    fold[NEAR : NEAR + LANE, BUCKETS - 1] = 1
    fold[NEAR + LANE :, BUCKETS // 2 - 1] = 1
    grad_table = jnp.dot(sums, jnp.asarray(fold), precision=lax.Precision.HIGHEST).T
    return outs[:n], outs[n], grad_table


def small_reduce(net, w, part, out, bufs):
    own, core, across_x, across_y, far = bufs
    rows = 4 * ROWS
    mine = part.at[pl.ds(pl.multiple_of(net.c * rows, rows), rows), :]
    other = part.at[pl.ds(pl.multiple_of((1 - net.c) * rows, rows), rows), :]
    load = pltpu.make_async_copy(mine, own.at[0], net.send.at[w, 0, 7])
    to_core = net.copy((w, 0, 0), other, core, net.r, net.sib)
    to_x = net.copy((w, 0, 1), own.at[1], across_x, net.xr, net.f)
    to_y = net.copy((w, 0, 2), own.at[2], across_y, net.yr, net.f)
    z_rows = lambda s: pl.ds(pl.multiple_of((net.z + s) % 4 * ROWS, ROWS), ROWS)
    to_far = [net.copy((w, s, 3), own.at[3, z_rows(s), :], far.at[s - 1], net.r, net.along(s)) for s in (1, 2, 3)]

    def first():
        load.start()
        to_core.start()

    def second():
        load.wait()
        to_core.wait_recv()
        own[1] = own[0] + core[...]
        to_x.start()

    def third():
        to_x.wait_recv()
        own[2] = own[1] + across_x[...]
        to_y.start()

    def fourth():
        to_y.wait_recv()
        own[3] = own[2] + across_y[...]
        for d in to_far:
            d.start()

    def fifth():
        for d in to_far:
            d.wait_recv()
        out[...] = own[3, z_rows(0), :] + far[0] + far[1] + far[2]
        for d in [to_core, to_x, to_y] + to_far:
            d.wait_send()

    return first, second, third, fourth, fifth


def reduce_kernel(shapes, n, *refs):
    grads, small_part, refs = refs[:n], refs[n], refs[n + 1 :]
    outs, small_out, refs = refs[:n], refs[n], refs[n + 1 :]
    bufs = [refs[7 * w : 7 * w + 7] for w in range(n)]
    small_bufs, (send, recv) = refs[7 * n : 7 * n + 5], refs[7 * n + 5 :]
    net = Reduce(shapes, grads, outs, bufs, send, recv)
    first, second, third, fourth, fifth = small_reduce(net, n, small_part, small_out, small_bufs)
    net.barrier()
    items, ticks = plan(net, n, list(range(n)))
    first()
    for w, k in items:
        net.start(w, k)
    extra = {1: second, 4: third, 6: fourth}
    for i, acts in enumerate(ticks):
        for act in acts:
            act()
        if i in extra:
            extra[i]()
    fifth()


def reduce_rest(weight_grads, small_grads):
    n = len(weight_grads)
    shapes = [(g.shape[0] // 8, g.shape[1]) for g in weight_grads]
    anywhere = pl.BlockSpec(memory_space=pl.ANY)
    inside = pl.BlockSpec(memory_space=pltpu.VMEM)
    rows = 4 * ROWS
    scratch = Reduce.scratch(shapes)
    scratch += [pltpu.VMEM((4, rows, LANE), F32)] + [pltpu.VMEM((rows, LANE), F32)] * 3 + [pltpu.VMEM((3, ROWS, LANE), F32)]
    scratch += [pltpu.SemaphoreType.DMA((n + 1, 4, Reduce.SLOTS)), pltpu.SemaphoreType.DMA((n + 1, 4, Reduce.SLOTS))]
    return pl.pallas_call(
        functools.partial(reduce_kernel, shapes, n),
        out_shape=[jax.ShapeDtypeStruct(a, BF16) for a in shapes] + [jax.ShapeDtypeStruct((ROWS, LANE), F32)],
        in_specs=[anywhere] * (n + 1),
        out_specs=[anywhere] * n + [inside],
        scratch_shapes=scratch,
        compiler_params=pltpu.CompilerParams(collective_id=2, has_side_effects=True, vmem_limit_bytes=VMEM_BYTES),
        name="reduce_rest",
    )(*weight_grads, small_grads)


ERF_P = 0.3275911 * 0.7071067811865476
ERF_A = (0.254829592 * 0.5, -0.284496736 * 0.5, 1.421413741 * 0.5, -1.453152027 * 0.5, 1.061405429 * 0.5)


def gelu_pair(z):
    bell = jnp.exp2(z * z * (-0.5 * LOG2E))
    t = 1.0 / (1.0 + ERF_P * jnp.abs(z))
    tail = ERF_A[4]
    for a in ERF_A[3::-1]:
        tail = tail * t + a
    tail = tail * t * bell
    share = jnp.where(z < 0.0, tail, 1.0 - tail)
    return z * share, share + z * bell * inv_root_tau


def norm_rows(summed):
    row_mean = jnp.mean(summed, -1, keepdims=True)
    centered = summed - row_mean
    inverse = lax.rsqrt(jnp.mean(centered * centered, -1, keepdims=True) + eps_norm)
    return centered * inverse, inverse


def norm_rows_back(scaled, normed, inverse):
    return inverse * (scaled - jnp.mean(scaled, -1, keepdims=True) - normed * jnp.mean(scaled * normed, -1, keepdims=True))


def fold8(value):
    rows, cols = value.shape
    return jnp.sum(value.reshape(rows // 8, 8, cols), 0)


def ffn_kernel(chunk, len_ref, mixed_ref, content_ref, query_ref, ccot_ref, qcot_ref, small_ref, wo_hbm, win_hbm, wout_hbm,
               cout_ref, qout_ref, hid_ref, dz_ref, first_ref, dffn_ref, dbranch_ref, dmixed_ref, sums_ref, wide_sums_ref,
               wo_ref, win_ref, wout_ref, vec_ref, shift_ref, slope_ref, acc_ref, wide_acc_ref, sem):
    i = pl.program_id(0)
    n = pl.num_programs(0)
    rows, width = mixed_ref.shape
    hidden = win_ref.shape[1]
    loads = [pltpu.make_async_copy(a, b, sem.at[k]) for k, (a, b) in enumerate(((wo_hbm, wo_ref), (win_hbm, win_ref), (wout_hbm, wout_ref)))]

    @pl.when(i == 0)
    def _():
        for d in loads:
            d.start()
        small = small_ref[...].astype(F32)
        shards = small.shape[0] // ROWS
        unit = width // shards
        for k in range(2, 8):
            vec_ref[k : k + 1, :] = spread_rows(small, [f * ROWS + k for f in range(shards)], 0, shards, unit)
        count = hidden // unit
        shift_ref[0:1, :] = spread_rows(small, [k // 4 * ROWS + 8 + k % 4 for k in range(count)], 0, count, unit)
        acc_ref[...] = jnp.zeros_like(acc_ref)
        wide_acc_ref[...] = jnp.zeros_like(wide_acc_ref)
        for d in loads:
            d.wait()

    first_stream = i < n // 2
    vec = lambda k: vec_ref[k : k + 1, :]

    def add_sum(k, value):
        acc_ref[k] = acc_ref[k] + fold8(value)

    residual = jnp.where(first_stream, content_ref[...], query_ref[...]).astype(F32)
    branch = nn(mixed_ref[...], wo_ref[...]) + vec(2)
    normed_one, inverse_one = norm_rows(residual + branch)
    first_low = (normed_one * vec(3) + vec(4)).astype(BF16)
    first_ref[...] = first_low
    for c in range(0, hidden, chunk):
        cols = slice(c, c + chunk)
        value, slope = gelu_pair(nn(first_low, win_ref[:, cols]) + shift_ref[0:1, cols])
        hid_ref[:, cols] = value.astype(BF16)
        slope_ref[:, cols] = slope.astype(BF16)
    ffn = nn(hid_ref[...], wout_ref[...]) + vec(5)
    normed_two, inverse_two = norm_rows(first_low.astype(F32) + ffn)
    final = (normed_two * vec(6) + vec(7)).astype(BF16)

    @pl.when(first_stream)
    def _():
        cout_ref[...] = final

    @pl.when(jnp.logical_not(first_stream))
    def _():
        qout_ref[...] = final

    per_stream = n // 2
    at = jnp.where(first_stream, i, i - per_stream) * rows
    seq_len = per_stream * rows // len_ref.shape[0]
    seq = at // seq_len
    place = at - seq * seq_len + lax.broadcasted_iota(jnp.int32, (rows, 1), 0)
    upstream = jnp.where(first_stream, ccot_ref[...], qcot_ref[...]).astype(F32)
    upstream = jnp.where(place < len_ref[seq], upstream, 0.0)
    add_sum(5, upstream * normed_two)
    add_sum(6, upstream)
    grad_two = norm_rows_back(upstream * vec(6), normed_two, inverse_two)
    grad_ffn = grad_two.astype(BF16)
    dffn_ref[...] = grad_ffn
    add_sum(4, grad_ffn.astype(F32))
    for c in range(0, hidden, chunk):
        cols = slice(c, c + chunk)
        grad = nt(grad_ffn, wout_ref[cols, :]) * slope_ref[:, cols].astype(F32)
        wide_acc_ref[:, cols] = wide_acc_ref[:, cols] + fold8(grad)
        dz_ref[:, cols] = grad.astype(BF16)
    grad_first = grad_two + nt(dz_ref[...], win_ref[...])
    add_sum(2, grad_first * normed_one)
    add_sum(3, grad_first)
    grad_branch = norm_rows_back(grad_first * vec(3), normed_one, inverse_one).astype(BF16)
    dbranch_ref[...] = grad_branch
    add_sum(1, grad_branch.astype(F32))
    dmixed_ref[...] = nt(grad_branch, wo_ref[...]).astype(BF16)

    @pl.when(i == n - 1)
    def _():
        for k in range(8):
            sums_ref[k : k + 1, :] = jnp.sum(acc_ref[k], 0, keepdims=True)
        wide_sums_ref[...] = jnp.sum(wide_acc_ref[...], 0, keepdims=True)


def ffn_stage(mixed, content_rows, query_rows, content_cot, query_cot, lengths, small, out_proj, in_proj, out_ffn, rows=256, chunk=768):
    total, width = mixed.shape
    hidden = in_proj.shape[1]
    n = total // rows
    half = n // 2
    anywhere = pl.BlockSpec(memory_space=pl.ANY)
    row_block = lambda cols: pl.BlockSpec((rows, cols), lambda i: (i, 0))
    low = pl.BlockSpec((rows, width), lambda i: (jnp.minimum(i, half - 1), 0))
    high = pl.BlockSpec((rows, width), lambda i: (jnp.maximum(i - half, 0), 0))
    whole = lambda shape: pl.BlockSpec(shape, lambda i: (0,) * len(shape))
    shape = jax.ShapeDtypeStruct
    return pl.pallas_call(
        functools.partial(ffn_kernel, chunk),
        grid=(n,),
        in_specs=[pl.BlockSpec(memory_space=pltpu.SMEM), row_block(width), low, high, low, high, whole(small.shape)] + [anywhere] * 3,
        out_specs=[low, high, row_block(hidden), row_block(hidden)] + [row_block(width)] * 4 + [whole((8, width)), whole((1, hidden))],
        out_shape=[shape((total // 2, width), BF16)] * 2 + [shape((total, hidden), BF16)] * 2 + [shape((total, width), BF16)] * 4
        + [shape((8, width), F32), shape((1, hidden), F32)],
        scratch_shapes=[
            pltpu.VMEM((width, width), BF16),
            pltpu.VMEM((width, hidden), BF16),
            pltpu.VMEM((hidden, width), BF16),
            pltpu.VMEM((8, width), F32),
            pltpu.VMEM((8, hidden), F32),
            pltpu.VMEM((rows, hidden), BF16),
            pltpu.VMEM((8, 8, width), F32),
            pltpu.VMEM((8, hidden), F32),
            pltpu.SemaphoreType.DMA((3,)),
        ],
        cost_estimate=pl.CostEstimate(flops=4 * total * width * (2 * hidden + width), bytes_accessed=60 * 2**20, transcendentals=2 * total * hidden),
        compiler_params=pltpu.CompilerParams(dimension_semantics=("arbitrary",), vmem_limit_bytes=VMEM_BYTES),
        name="ffn_stage",
    )(lengths, mixed, content_rows, query_rows, content_cot, query_cot, small, out_proj, in_proj, out_ffn)


def rows_inner(left_op, right_op):
    return lax.dot_general(
        left_op, right_op, (((0,), (0,)), ((), ())), preferred_element_type=jnp.float32
    )


def times_transpose(left_op, right_op):
    return lax.dot_general(
        left_op, right_op, (((1,), (1,)), ((), ())), preferred_element_type=jnp.float32
    )


def pack_small(groups, shards):
    rows = []
    for g in groups:
        g = g.reshape(shards, -1, g.shape[-1]) if g.ndim > 1 else g
        rows.append(g)
    wide = [jnp.pad(g, ((0, 0), (0, 0), (0, LANE - g.shape[2]))) for g in rows]
    joined = jnp.concatenate(wide, 1)
    joined = jnp.pad(joined, ((0, 0), (0, ROWS - joined.shape[1]), (0, 0)))
    return joined.reshape(shards * ROWS, LANE)


def on_device(axes, content_stream, query_stream, lengths, factor_order, qkv_weight, qv_bias, out_weight, out_bias, norm1_gain, norm1_bias, rel_table, ffn_in_weight, ffn_in_bias, ffn_out_weight, ffn_out_bias, norm2_gain, norm2_bias, content_cot, query_cot):
    linked = axes == (4, 8)
    shards = axes[1]
    seq_count, seq_len, width = content_stream.shape
    row_count = seq_count * seq_len
    unit = width // shards
    small_args = (qv_bias, out_bias, norm1_gain, norm1_bias, ffn_out_bias, norm2_gain, norm2_bias, ffn_in_bias)
    small = pack_small([p.reshape(1, -1, unit) for p in small_args] + [rel_table[None]], 1).astype(BF16)
    weights = [w.astype(BF16) for w in (qkv_weight, out_weight, ffn_in_weight, ffn_out_weight)]
    content_rows = content_stream.reshape(row_count, width)
    query_rows = query_stream.reshape(row_count, width)
    if linked:
        out_proj, in_proj, out_ffn, joined_proj, small, mixed, totals, proj = forward_attention(
            True, content_rows, query_rows, lengths, factor_order, weights, small)
    else:
        gather = lambda a: lax.all_gather(a, "fsdp", axis=0, tiled=True)
        joined_proj, out_proj, in_proj, out_ffn = [gather(w) for w in weights]
        small = gather(small)
        mixed, totals, proj = forward_attention(False, content_rows, query_rows, lengths, factor_order, [joined_proj], small)
    mixed_rows = mixed.reshape(2 * row_count, width)
    flat_cot = lambda a: a.reshape(row_count, width)
    content_out, query_out, hidden_low, grad_hidden, first_low, grad_ffn, grad_branch, grad_mixed, sums, wide_sums = ffn_stage(
        mixed_rows, content_rows, query_rows, flat_cot(content_cot), flat_cot(query_cot), lengths, small, out_proj, in_proj, out_ffn)
    grad_out_ffn = rows_inner(hidden_low, grad_ffn).astype(BF16)
    grad_in_proj = rows_inner(first_low, grad_hidden).astype(BF16)
    grad_out_proj = rows_inner(mixed_rows, grad_branch).astype(BF16)
    ready = [grad_in_proj, grad_out_ffn, grad_out_proj] if linked else []
    early, grads, grad_table = backward_attention(linked, proj, grad_mixed, mixed_rows, totals, lengths, factor_order, small, ready)
    grad_q = rows_inner(content_rows, grads[0]) + rows_inner(query_rows, grads[3])
    grad_joined = jnp.concatenate([grad_q, rows_inner(content_rows, grads[1]), rows_inner(content_rows, grads[2])], 1).astype(BF16)
    low_sums = jnp.sum(grads.astype(F32), 1)
    grad_proj_shift = jnp.concatenate([low_sums[0] + low_sums[3], low_sums[2]])
    rows_of = lambda g: g.reshape(shards, -1, unit) if g.ndim == 1 or g.shape[0] == 1 else g.reshape(-1, shards, unit).transpose(1, 0, 2)
    packed = pack_small([rows_of(grad_proj_shift), rows_of(sums[1:7]), rows_of(wide_sums), grad_table.reshape(shards, -1, HEADS)], shards)
    if linked:
        packed = packed.reshape(4, 2, ROWS, LANE).transpose(1, 0, 2, 3).reshape(8 * ROWS, LANE)
        sum_joined, mine = reduce_rest([grad_joined], packed)
        sum_in, sum_out, sum_proj = early
    else:
        scatter = lambda a: lax.psum(lax.psum_scatter(a, "fsdp", scatter_dimension=0, tiled=True), "rep")
        sum_joined, sum_in, sum_out, sum_proj = [scatter(a) for a in (grad_joined, grad_in_proj, grad_out_ffn, grad_out_proj)]
        mine = scatter(packed)
    sum_joined, sum_in, sum_out, sum_proj = [a.astype(F32) for a in (sum_joined, sum_in, sum_out, sum_proj)]
    content_grad_rows = grad_branch[:row_count].astype(F32) + (
        times_transpose(grads[0], joined_proj[:, :width])
        + times_transpose(grads[1], joined_proj[:, width : 2 * width])
        + times_transpose(grads[2], joined_proj[:, 2 * width :])
    )
    query_grad_rows = grad_branch[row_count:].astype(F32) + times_transpose(grads[3], joined_proj[:, :width])
    vec = lambda k: mine[k, :unit]
    block_shape = (seq_count, seq_len, width)
    return (
        content_out.reshape(block_shape),
        query_out.reshape(block_shape),
        content_grad_rows.reshape(block_shape).astype(BF16),
        query_grad_rows.reshape(block_shape).astype(BF16),
        sum_joined,
        mine[0:2, :unit].reshape(-1),
        sum_proj,
        vec(2),
        vec(3),
        vec(4),
        mine[TABLE_ROW : TABLE_ROW + rel_table.shape[0], :HEADS],
        sum_in,
        mine[8:12, :unit].reshape(-1),
        sum_out,
        vec(5),
        vec(6),
        vec(7),
    )


def solution(mesh):
    in_specs = (
        P(("rep", "fsdp"), None, None),
        P(("rep", "fsdp"), None, None),
        P(("rep", "fsdp")),
        P(("rep", "fsdp"), None),
        P("fsdp", None),
        P("fsdp"),
        P("fsdp", None),
        P("fsdp"),
        P("fsdp"),
        P("fsdp"),
        P("fsdp", None),
        P("fsdp", None),
        P("fsdp"),
        P("fsdp", None),
        P("fsdp"),
        P("fsdp"),
        P("fsdp"),
        P(("rep", "fsdp"), None, None),
        P(("rep", "fsdp"), None, None),
    )
    out_specs = (
        P(("rep", "fsdp"), None, None),
        P(("rep", "fsdp"), None, None),
        P(("rep", "fsdp"), None, None),
        P(("rep", "fsdp"), None, None),
        P("fsdp", None),
        P("fsdp"),
        P("fsdp", None),
        P("fsdp"),
        P("fsdp"),
        P("fsdp"),
        P("fsdp", None),
        P("fsdp", None),
        P("fsdp"),
        P("fsdp", None),
        P("fsdp"),
        P("fsdp"),
        P("fsdp"),
    )
    return jax.shard_map(
        functools.partial(on_device, tuple(mesh.shape[a] for a in mesh.axis_names)),
        mesh=mesh,
        in_specs=in_specs,
        out_specs=out_specs,
        check_vma=False,
    )
```

```python
import functools
import math

import jax
import jax.numpy as jnp
import numpy as np
from jax import lax
from jax.experimental import pallas as pl
from jax.experimental.pallas import tpu as pltpu
from jax.sharding import PartitionSpec as P

HEADS = 12
HEAD = 64
BUCKETS = 32
MAX_DIST = 128
LANE = 128
NEAR = 512
ROWS = 16
TABLE_ROW = 12
MASKED = -1e30
LOG2E = 1.4426950408889634
LN2 = 0.6931471805599453
F32 = jnp.float32
BF16 = jnp.bfloat16
MESH = pl.DeviceIdType.MESH
VMEM_BYTES = 60 * 2**20
eps_norm = 1e-05
inv_root_tau = 0.3989422804014327


def bucket_of(offset):
    half_count = BUCKETS // 2
    result = (offset < 0).astype(np.int64) * half_count
    distance = np.abs(offset)
    exact_count = half_count // 2
    fraction = np.log(np.maximum(distance, 1) / exact_count) / np.log(MAX_DIST / exact_count)
    beyond = exact_count + (fraction * (half_count - exact_count)).astype(np.int64)
    beyond = np.minimum(beyond, half_count - 1)
    result = result + np.where(distance < exact_count, distance, beyond)
    return result.astype(np.int32)


def nt(a, b):
    return lax.dot_general(a, b, (((1,), (1,)), ((), ())), preferred_element_type=F32)


def nn(a, b):
    return lax.dot_general(a, b, (((1,), (0,)), ((), ())), preferred_element_type=F32)


def signed_places():
    places = np.arange(NEAR)
    return np.where(places < NEAR - LANE, places, places - NEAR)


def near_onehot(sign):
    offset = sign * (signed_places() - LANE)
    return (bucket_of(offset)[None, :] == np.arange(BUCKETS)[:, None]).astype(np.float32)


def skewed(row, width):
    wide = jnp.broadcast_to(row, (LANE, NEAR))
    return pltpu.roll(wide, 0, 1, stride=1, stride_axis=0)[:, :width]


def tile_bias(near, far_pos, far_neg, seq_len, sign):
    blocks = seq_len // LANE
    rows = []
    for rb in range(blocks):
        parts = []
        for cb in range(blocks):
            e = cb - rb
            if abs(e) <= 1:
                parts.append(near[:, (e + 1) * LANE : (e + 2) * LANE])
            else:
                parts.append(jnp.broadcast_to(far_pos if e * sign > 0 else far_neg, (LANE, LANE)))
        rows.append(jnp.concatenate(parts, 1))
    return rows


def head_lanes(shape, t):
    lane = lax.broadcasted_iota(jnp.int32, shape, 1)
    return (lane >= t * HEAD) & (lane < (t + 1) * HEAD)


def flip(v, m):
    a, b = v // 2, v % 2
    if m & 2:
        a = 1 - a
    if m & 1:
        b = 1 - b
    return a * 2 + b


def table_onehot(sign, shards):
    per_shard = BUCKETS // shards
    result = np.zeros((shards * ROWS, NEAR + LANE), np.float32)
    near = near_onehot(sign)
    for bucket in range(BUCKETS):
        row = bucket // per_shard * ROWS + TABLE_ROW + bucket % per_shard
        result[row, :NEAR] = near[bucket]
        result[row, NEAR] = bucket == BUCKETS // 2 - 1
        result[row, NEAR + 1] = bucket == BUCKETS - 1
    return jnp.asarray(result, BF16)


class Links:
    def __init__(self, send, recv):
        self.send, self.recv = send, recv
        self.r = lax.axis_index("rep")
        self.f = lax.axis_index("fsdp")
        self.y, self.x = self.r // 2, self.r % 2
        self.z, self.c = self.f // 2, self.f % 2
        self.xr, self.yr = flip(self.r, 1), flip(self.r, 2)
        self.sib = self.z * 2 + 1 - self.c

    def along(self, s):
        return ((self.z + s) % 4) * 2 + self.c

    def copy(self, at, src, dst, rep, fsdp):
        return pltpu.make_async_remote_copy(
            src_ref=src, dst_ref=dst, send_sem=self.send.at[at], recv_sem=self.recv.at[at],
            device_id={"rep": rep, "fsdp": fsdp}, device_id_type=MESH)

    def barrier(self):
        sem = pltpu.get_barrier_semaphore()
        peers = [(self.r, self.along(s)) for s in (1, 2, 3)]
        peers += [(self.xr, self.f), (self.yr, self.f), (self.r, self.sib)]
        for rep, fsdp in peers:
            pl.semaphore_signal(sem, inc=1, device_id={"rep": rep, "fsdp": fsdp}, device_id_type=MESH)
        pl.semaphore_wait(sem, len(peers))


def quarter_of(ref, rows, cols, owner, q, part=None):
    pr, pc = rows // 2, cols // 2
    r0, c0 = owner * rows + (q // 2) * pr, (q % 2) * pc
    if part is not None:
        if pr % 32 == 0:
            r0, pr = r0 + part * (pr // 2), pr // 2
        else:
            first = (pc // LANE + 1) // 2 * LANE
            c0, pc = (c0, first) if part == 0 else (c0 + first, pc - first)
    return ref.at[pl.ds(pl.multiple_of(r0, 16), pr), pl.ds(pl.multiple_of(c0, LANE), pc)]


class Gather(Links):
    SLOTS = 12

    def __init__(self, shapes, shards, fulls, send, recv):
        super().__init__(send, recv)
        self.shapes, self.shards, self.fulls = shapes, shards, fulls

    def z_send(self, w, s):
        rows, cols = self.shapes[w]
        src = quarter_of(self.shards[w], rows, cols, 0, self.r)
        dst = quarter_of(self.fulls[w], rows, cols, self.f, self.r)
        return self.copy((w, s, 0), src, dst, self.r, self.along(s))

    def hop(self, w, s, slot, q, rep, fsdp, part=None):
        rows, cols = self.shapes[w]
        place = quarter_of(self.fulls[w], rows, cols, self.along(4 - s), q, part)
        return self.copy((w, s, slot), place, place, rep, fsdp)

    def own_place(self, w):
        rows = self.shapes[w][0]
        return self.fulls[w].at[pl.ds(pl.multiple_of(self.f * rows, 16), rows), :]

    def own_sib(self, w):
        return self.copy((w, 0, 0), self.shards[w], self.own_place(w), self.r, self.sib)

    def own_here(self, w):
        return pltpu.make_async_copy(self.shards[w], self.own_place(w), self.send.at[w, 0, 1])

    def h_x(self, w, s):
        return self.hop(w, s, 1, self.r, self.xr, self.f)

    def h_y(self, w, s):
        return self.hop(w, s, 2, self.r, self.yr, self.f)

    def h_dy(self, w, s):
        return self.hop(w, s, 3, self.xr, self.yr, self.f, 0)

    def h_dx(self, w, s):
        return self.hop(w, s, 4, self.yr, self.xr, self.f, 1)

    def h_sib(self, w, s, m):
        return self.hop(w, s, 5 + m, flip(self.r, m), self.r, self.sib)

    def start(self, w):
        for s in (1, 2, 3):
            self.z_send(w, s).start()
        self.own_sib(w).start()
        self.own_here(w).start()

    def relay_z(self, w, s):
        self.z_send(w, s).wait_recv()
        self.h_x(w, s).start()
        self.h_y(w, s).start()
        self.h_sib(w, s, 0).start()

    def relay_xy(self, w, s):
        self.h_x(w, s).wait_recv()
        self.h_dy(w, s).start()
        self.h_sib(w, s, 1).start()
        self.h_y(w, s).wait_recv()
        self.h_dx(w, s).start()
        self.h_sib(w, s, 2).start()

    def relay_diag(self, w, s):
        self.h_dy(w, s).wait_recv()
        self.h_dx(w, s).wait_recv()
        self.h_sib(w, s, 3).start()

    def arrive(self, w):
        for s in (1, 2, 3):
            for m in range(4):
                self.h_sib(w, s, m).wait_recv()
        self.own_sib(w).wait_recv()
        self.own_here(w).wait()

    def drain(self, w):
        for s in (1, 2, 3):
            for d in (self.z_send(w, s), self.h_x(w, s), self.h_y(w, s), self.h_dy(w, s), self.h_dx(w, s)):
                d.wait_send()
            for m in range(4):
                self.h_sib(w, s, m).wait_send()
        self.own_sib(w).wait_send()

    def small_place(self, owner):
        return self.small_full.at[pl.ds(pl.multiple_of(owner * ROWS, ROWS), ROWS), :]

    def small_copies(self):
        w = len(self.shapes)
        far = [self.copy((w, s, 0), self.small_shard, self.small_place(self.f), self.r, self.along(s)) for s in (1, 2, 3)]
        own = self.copy((w, 0, 0), self.small_shard, self.small_place(self.f), self.r, self.sib)
        here = pltpu.make_async_copy(self.small_shard, self.small_place(self.f), self.send.at[w, 0, 1])
        sib = []
        for s in (1, 2, 3):
            place = self.small_place(self.along(4 - s))
            sib.append(self.copy((w, s, 1), place, place, self.r, self.sib))
        return far, own, here, sib


class Reduce(Links):
    SLOTS = 8

    def __init__(self, shapes, grads, outs, bufs, send, recv):
        super().__init__(send, recv)
        self.shapes, self.grads, self.outs, self.bufs = shapes, grads, outs, bufs

    @staticmethod
    def scratch(shapes):
        out = []
        for rows, cols in shapes:
            out += [
                pltpu.VMEM((4, rows, cols), BF16),
                pltpu.VMEM((4, rows, cols), BF16),
                pltpu.VMEM((2, rows, cols // 2), BF16),
                pltpu.VMEM((2, rows // 2, cols), BF16),
                pltpu.VMEM((4, rows // 2, cols // 2), BF16),
                pltpu.VMEM((3, rows // 2, cols // 2), BF16),
                pltpu.VMEM((rows // 2, cols // 2), BF16),
            ]
        return out

    def shard(self, w, s, core):
        rows = self.shapes[w][0]
        at = pl.multiple_of((((self.z + s) % 4) * 2 + core) * rows, 16)
        return self.grads[w].at[pl.ds(at, rows), :]

    def half_rows(self, w, bit):
        h = self.shapes[w][0] // 2
        return pl.ds(pl.multiple_of(bit * h, 16), h)

    def half_cols(self, w, bit):
        h = self.shapes[w][1] // 2
        return pl.ds(pl.multiple_of(bit * h, 128), h)

    def core_copy(self, w, s):
        return self.copy((w, s, 0), self.shard(w, s, 1 - self.c), self.bufs[w][1].at[s], self.r, self.sib)

    def core_load(self, w, s):
        return pltpu.make_async_copy(self.shard(w, s, self.c), self.bufs[w][0].at[s], self.send.at[w, s, 7])

    def start(self, w, s):
        self.core_copy(w, s).start()
        self.core_load(w, s).start()

    def x_first(self, s):
        return s % 2 == 1

    def first_copy(self, w, s):
        own, hx, hy = self.bufs[w][0], self.bufs[w][2], self.bufs[w][3]
        if self.x_first(s):
            return self.copy((w, s, 1), own.at[s, :, self.half_cols(w, 1 - self.x)], hx.at[s // 2], self.xr, self.f)
        return self.copy((w, s, 1), own.at[s, self.half_rows(w, 1 - self.y), :], hy.at[s // 2], self.yr, self.f)

    def add_core(self, w, s):
        self.core_copy(w, s).wait_recv()
        self.core_load(w, s).wait()
        own, got = self.bufs[w][0], self.bufs[w][1]
        own[s] = own[s] + got[s]
        self.first_copy(w, s).start()

    def second_copy(self, w, s):
        own, quarter = self.bufs[w][0], self.bufs[w][4]
        if self.x_first(s):
            src = own.at[s, self.half_rows(w, 1 - self.y), self.half_cols(w, self.x)]
            return self.copy((w, s, 2), src, quarter.at[s], self.yr, self.f)
        src = own.at[s, self.half_rows(w, self.y), self.half_cols(w, 1 - self.x)]
        return self.copy((w, s, 2), src, quarter.at[s], self.xr, self.f)

    def add_first(self, w, s):
        self.first_copy(w, s).wait_recv()
        own, hx, hy = self.bufs[w][0], self.bufs[w][2], self.bufs[w][3]
        if self.x_first(s):
            at = (s, slice(None), self.half_cols(w, self.x))
            own[at] = own[at] + hx[s // 2]
        else:
            at = (s, self.half_rows(w, self.y), slice(None))
            own[at] = own[at] + hy[s // 2]
        self.second_copy(w, s).start()

    def far_copy(self, w, s):
        own, far = self.bufs[w][0], self.bufs[w][5]
        src = own.at[s, self.half_rows(w, self.y), self.half_cols(w, self.x)]
        return self.copy((w, s, 3), src, far.at[s - 1], self.r, self.along(s))

    def add_second(self, w, s):
        self.second_copy(w, s).wait_recv()
        own, quarter = self.bufs[w][0], self.bufs[w][4]
        at = (s, self.half_rows(w, self.y), self.half_cols(w, self.x))
        own[at] = own[at] + quarter[s]
        if s > 0:
            self.far_copy(w, s).start()

    def place(self, w, q, part=None):
        rows, cols = self.shapes[w]
        h = rows // 2
        r0, n = (q // 2) * h, h
        if part is not None:
            n = h // 32 * 16 if part == 0 else h - h // 32 * 16
            r0 = r0 if part == 0 else r0 + h // 32 * 16
        return self.outs[w].at[pl.ds(pl.multiple_of(r0, 16), n), self.half_cols(w, q % 2)]

    def out_local(self, w):
        return pltpu.make_async_copy(self.bufs[w][6], self.place(w, self.r), self.send.at[w, 0, 3])

    def out_x(self, w):
        return self.copy((w, 0, 4), self.bufs[w][6], self.place(w, self.r), self.xr, self.f)

    def out_y(self, w):
        return self.copy((w, 0, 5), self.bufs[w][6], self.place(w, self.r), self.yr, self.f)

    def out_dy(self, w):
        p = self.place(w, flip(self.r, 1), 0)
        return self.copy((w, 1, 4), p, p, self.yr, self.f)

    def out_dx(self, w):
        p = self.place(w, flip(self.r, 2), 1)
        return self.copy((w, 1, 5), p, p, self.xr, self.f)

    def total(self, w):
        own, far, done = self.bufs[w][0], self.bufs[w][5], self.bufs[w][6]
        for s in (1, 2, 3):
            self.far_copy(w, s).wait_recv()
        at = (0, self.half_rows(w, self.y), self.half_cols(w, self.x))
        done[...] = (own[at].astype(F32) + far[0].astype(F32) + far[1].astype(F32) + far[2].astype(F32)).astype(BF16)
        self.out_x(w).start()
        self.out_y(w).start()
        self.out_local(w).start()

    def relay(self, w):
        self.out_x(w).wait_recv()
        self.out_dy(w).start()
        self.out_y(w).wait_recv()
        self.out_dx(w).start()

    def finish(self, w):
        for s in range(4):
            self.core_copy(w, s).wait_send()
            self.first_copy(w, s).wait_send()
            self.second_copy(w, s).wait_send()
            if s:
                self.far_copy(w, s).wait_send()
        self.out_local(w).wait()
        self.out_x(w).wait_send()
        self.out_y(w).wait_send()
        for d in (self.out_dy(w), self.out_dx(w)):
            d.wait_send()
            d.wait_recv()


def plan(red, n, order):
    items = [(w, s) for w in order for s in (1, 2, 3, 0)]
    ticks = []
    m = len(items)
    for k in range(m + 4):
        acts = []
        if k < m:
            acts.append(functools.partial(red.add_core, *items[k]))
        if 0 <= k - 2 < m:
            acts.append(functools.partial(red.add_first, *items[k - 2]))
        if 0 <= k - 4 < m:
            w, s = items[k - 4]
            acts.append(functools.partial(red.add_second, w, s))
            if s == 0:
                j = order.index(w)
                if j > 0:
                    acts.append(functools.partial(red.total, order[j - 1]))
                if j > 1:
                    acts.append(functools.partial(red.relay, order[j - 2]))
        ticks.append(acts)
    tail = [functools.partial(red.total, order[-1])]
    if n > 1:
        tail.append(functools.partial(red.relay, order[-2]))
    tail.append(functools.partial(red.relay, order[-1]))
    ticks.append(tail)
    ticks.append([functools.partial(red.finish, w) for w in order])
    return items, ticks


def spread_rows(small, row, step, count, unit):
    width = count * unit
    lane = lax.broadcasted_iota(jnp.int32, (8, width), 1)
    total = jnp.zeros((8, width), F32)
    for k in range(count):
        one = jnp.broadcast_to(small[row[k] : row[k] + 1, :], (8, LANE))
        wide = jnp.concatenate([one, jnp.zeros((8, width - LANE), F32)], 1)
        wide = jnp.where(lane < unit, wide, 0.0)
        total = total + (pltpu.roll(wide, k * unit, 1) if k else wide)
    return total[0:1]


def fill_mask(mask_ref, ord_ref, limit, s, seq_len, turned):
    blocks = seq_len // LANE
    own = ord_ref[pl.ds(s, 1), :].astype(F32)
    cols = jnp.broadcast_to(own, (LANE, seq_len)).T
    for rb in range(blocks):
        col = cols[rb * LANE : (rb + 1) * LANE, :]
        rank = jnp.concatenate([col] * blocks, 1)
        place = lax.broadcasted_iota(jnp.int32, (LANE, seq_len), 0 if turned else 1)
        if turned:
            place = place + rb * LANE
        order = (rank <= own) if turned else (own <= rank)
        ok = (place < limit) & ((place == 0) | order)
        mask_ref[s, rb * LANE : (rb + 1) * LANE, :] = jnp.where(ok, 0.0, MASKED)


def fill_near(near_ref, small, onehot_ref):
    near_ref[...] = lax.dot_general(small, onehot_ref[...], (((0,), (0,)), ((), ())), preferred_element_type=F32) * LOG2E


def attention_step(hp, s, proj, mask_ref, near_ref, put_out, put_total):
    query_c, keys, value, query_g = proj
    seq_len = keys.shape[0]
    blocks = seq_len // LANE
    values = jnp.concatenate([value, jnp.ones((seq_len, LANE), BF16)], 1)
    lane = lax.broadcasted_iota(jnp.int32, (seq_len, LANE), 1)
    diag_r = lax.broadcasted_iota(jnp.int32, (LANE, LANE), 0)
    diag_c = lax.broadcasted_iota(jnp.int32, (LANE, LANE), 1)
    outs = [[], []]
    totals = [jnp.zeros((seq_len, LANE), F32), jnp.zeros((seq_len, LANE), F32)]
    for t in range(2):
        head = hp * 2 + t
        sel = head_lanes((seq_len, LANE), t)
        head_row = near_ref[pl.ds(head, 1), :]
        near = skewed(head_row[:, :NEAR], 3 * LANE)
        bias = tile_bias(near, head_row[:, NEAR : NEAR + 1], head_row[:, NEAR + 1 : NEAR + 2], seq_len, -1)
        for stream in range(2):
            query = jnp.where(sel, query_g if stream else query_c, jnp.zeros((), BF16))
            raw = nt(query, keys)
            probs = []
            maxes = []
            for rb in range(blocks):
                part = raw[rb * LANE : (rb + 1) * LANE, :] + (bias[rb] + mask_ref[s, rb * LANE : (rb + 1) * LANE, :])
                if stream == 1:
                    hit = diag_r == diag_c
                    if rb == 0:
                        hit = hit & (diag_c != 0)
                    pieces = []
                    if rb > 0:
                        pieces.append(part[:, : rb * LANE])
                    pieces.append(jnp.where(hit, MASKED, part[:, rb * LANE : (rb + 1) * LANE]))
                    if rb < blocks - 1:
                        pieces.append(part[:, (rb + 1) * LANE :])
                    part = jnp.concatenate(pieces, 1)
                top = jnp.max(part, 1, keepdims=True)
                probs.append(jnp.exp2(part - top).astype(BF16))
                maxes.append(jnp.broadcast_to(top, (LANE, LANE)))
            mixed = nn(jnp.concatenate(probs, 0), values)
            total = mixed[:, LANE:]
            outs[stream].append(mixed[:, :LANE] / total)
            log_total = jnp.concatenate(maxes, 0) + jnp.log2(total)
            hi = log_total.astype(BF16).astype(F32)
            totals[stream] = jnp.where(lane == head, -hi, jnp.where(lane == head + HEAD, hi - log_total, totals[stream]))
    first = head_lanes((seq_len, LANE), 0)
    mine = (lane == hp * 2) | (lane == hp * 2 + 1) | (lane == hp * 2 + HEAD) | (lane == hp * 2 + 1 + HEAD)
    for stream in range(2):
        put_out(stream, jnp.where(first, outs[stream][0], outs[stream][1]).astype(BF16))
        put_total(stream, totals[stream].astype(BF16), mine)


def forward_kernel(shapes, linked, len_ref, content_ref, query_ref, ord_ref, onehot_ref, *refs):
    n = len(shapes)
    if linked:
        shards, small_shard, refs = refs[:n], refs[n], refs[n + 1 :]
        full_refs, refs = refs[: n - 1], refs[n - 1 :]
        joined_out, small_out, refs = refs[0], refs[1], refs[2:]
    else:
        joined_in, small_in, refs = refs[0], refs[1], refs[2:]
    mixed_ref, total_ref, proj_out, joined_ref, small_ref, proj_ref, mask_ref, near_ref, own_sem = refs[:9]
    hp = pl.program_id(0)
    s = pl.program_id(1)
    step = hp * pl.num_programs(1) + s
    steps = (HEADS // 2) * total_ref.shape[1]
    seqs = total_ref.shape[1]
    seq_len = total_ref.shape[2]
    row_count, width = content_ref.shape
    if linked:
        send, recv = refs[9:]
        net = Gather(shapes, shards, (joined_ref,) + tuple(full_refs), send, recv)
        net.small_shard, net.small_full = small_shard, small_ref
    proj_copy = pltpu.make_async_copy(proj_ref, proj_out, own_sem.at[0])

    @pl.when(step == 0)
    def _():
        if linked:
            net.barrier()
            far, own, here, sib = net.small_copies()
            for d in far + [own, here]:
                d.start()
            for w in range(n):
                net.start(w)
            for s0 in range(seqs):
                fill_mask(mask_ref, ord_ref, len_ref[s0], s0, seq_len, False)
            for d, e in zip(far, sib):
                d.wait_recv()
                e.start()
            for k in (1, 2, 3):
                net.relay_z(0, k)
            for k in (1, 2, 3):
                net.relay_xy(0, k)
            for k in (1, 2, 3):
                net.relay_z(1, k)
            for k in (1, 2, 3):
                net.relay_diag(0, k)
            for k in (1, 2, 3):
                net.relay_z(2, k)
            for d in far:
                d.wait_send()
            for d in [own] + sib:
                d.wait_send()
                d.wait_recv()
            here.wait()
            net.arrive(0)
            pltpu.make_async_copy(joined_ref, joined_out, own_sem.at[1]).start()
            pltpu.make_async_copy(small_ref, small_out, own_sem.at[2]).start()
        else:
            fetch = (pltpu.make_async_copy(joined_in, joined_ref, own_sem.at[1]), pltpu.make_async_copy(small_in, small_ref, own_sem.at[2]))
            for d in fetch:
                d.start()
            for s0 in range(seqs):
                fill_mask(mask_ref, ord_ref, len_ref[s0], s0, seq_len, False)
            for d in fetch:
                d.wait()
        fill_near(near_ref, small_ref[...], onehot_ref)
        small = small_ref[...].astype(F32)
        shards_all = small.shape[0] // ROWS
        unit = width // shards_all
        half = shards_all // 2
        shift_q = spread_rows(small, [k // 2 * ROWS + k % 2 for k in range(2 * half)], 0, 2 * half, unit)
        shift_v = spread_rows(small, [(half + k // 2) * ROWS + k % 2 for k in range(2 * half)], 0, 2 * half, unit)
        scale = LOG2E / math.sqrt(HEAD)
        chunk = 256

        @pl.loop(0, row_count // chunk)
        def _(i):
            rows = pl.ds(pl.multiple_of(i * chunk, chunk), chunk)
            rows_c = content_ref[rows, :]
            proj_ref[rows, 0:width] = ((nn(rows_c, joined_ref[:, 0:width]) + shift_q) * scale).astype(BF16)
            proj_ref[rows, width : 2 * width] = nn(rows_c, joined_ref[:, width : 2 * width]).astype(BF16)
            proj_ref[rows, 2 * width : 3 * width] = (nn(rows_c, joined_ref[:, 2 * width : 3 * width]) + shift_v).astype(BF16)
            proj_ref[rows, 3 * width : 4 * width] = ((nn(query_ref[rows, :], joined_ref[:, 0:width]) + shift_q) * scale).astype(BF16)

        proj_copy.start()

    if linked:
        agenda = {
            1: [(net.relay_xy, 1, (1, 2, 3))],
            3: [(net.relay_z, 3, (1, 2, 3))],
            4: [(net.relay_xy, 2, (1,))],
            5: [(net.relay_xy, 2, (2,)), (net.relay_diag, 1, (1, 2, 3))],
            6: [(net.relay_xy, 2, (3,))],
            8: [(net.relay_diag, 2, (1, 2)), (net.relay_xy, 3, (1,))],
            9: [(net.relay_diag, 2, (3,)), (net.relay_xy, 3, (2,))],
            10: [(net.relay_xy, 3, (3,))],
        }
        for at, acts in agenda.items():

            @pl.when(step == min(at, steps - 1))
            def _():
                for act, w, ks in acts:
                    for k in ks:
                        act(w, k)

    here_rows = pl.ds(pl.multiple_of(s * seq_len, seq_len), seq_len)
    column = lambda k: pl.ds(pl.multiple_of(k * width + hp * LANE, LANE), LANE)
    proj = [proj_ref[here_rows, column(k)] for k in range(4)]

    def put_out(stream, value):
        mixed_ref[stream] = value

    def put_total(stream, value, mine):
        @pl.when(hp == 0)
        def _():
            total_ref[stream, s] = value

        @pl.when(hp > 0)
        def _():
            total_ref[stream, s] = jnp.where(mine, value, total_ref[stream, s])

    attention_step(hp, s, proj, mask_ref, near_ref, put_out, put_total)

    @pl.when(step == steps - 1)
    def _():
        proj_copy.wait()
        if linked:
            pltpu.make_async_copy(joined_ref, joined_out, own_sem.at[1]).wait()
            pltpu.make_async_copy(small_ref, small_out, own_sem.at[2]).wait()
            for k in (1, 2, 3):
                net.relay_diag(3, k)
            for w in range(n):
                if w:
                    net.arrive(w)
                net.drain(w)


def forward_attention(linked, content_rows, query_rows, lengths, order, weights, small):
    row_count, width = content_rows.shape
    seqs, seq_len = order.shape
    pairs = width // LANE
    shards = 8 if linked else small.shape[0] // ROWS
    onehot = table_onehot(-1, shards)
    shapes = [w.shape for w in weights] if linked else []
    n = len(shapes)
    anywhere = pl.BlockSpec(memory_space=pl.ANY)
    inside = pl.BlockSpec(memory_space=pltpu.VMEM)
    block3 = pl.BlockSpec((2, seq_len, LANE), lambda h, s: (0, s, h))
    joined_shape = (width, 3 * width)
    small_shape = (shards * ROWS, LANE)
    out_specs, out_shape = [], []
    if linked:
        out_specs += [anywhere] * (n + 1)
        out_shape += [jax.ShapeDtypeStruct((8 * a, b), BF16) for a, b in shapes[1:]]
        out_shape += [jax.ShapeDtypeStruct(joined_shape, BF16), jax.ShapeDtypeStruct(small_shape, BF16)]
    out_specs += [block3, pl.BlockSpec((2, seqs, seq_len, LANE), lambda h, s: (0, 0, 0, 0)), anywhere]
    out_shape += [
        jax.ShapeDtypeStruct((2, row_count, width), BF16),
        jax.ShapeDtypeStruct((2, seqs, seq_len, LANE), BF16),
        jax.ShapeDtypeStruct((row_count, 4 * width), BF16),
    ]
    scratch = [
        pltpu.VMEM(joined_shape, BF16),
        pltpu.VMEM(small_shape, BF16),
        pltpu.VMEM((row_count, 4 * width), BF16),
        pltpu.VMEM((seqs, seq_len, seq_len), F32),
        pltpu.VMEM((LANE, NEAR + LANE), F32),
        pltpu.SemaphoreType.DMA((3,)),
    ]
    if linked:
        scratch += [pltpu.SemaphoreType.DMA((n + 1, 4, Gather.SLOTS)), pltpu.SemaphoreType.DMA((n + 1, 4, Gather.SLOTS))]
    flops = 2 * row_count * width * 4 * width + 8 * row_count * seq_len * width
    return pl.pallas_call(
        functools.partial(forward_kernel, shapes, linked),
        grid=(pairs, seqs),
        in_specs=[pl.BlockSpec(memory_space=pltpu.SMEM), inside, inside, inside, inside] + [anywhere] * (n + 1 if linked else 2),
        out_specs=out_specs,
        out_shape=out_shape,
        scratch_shapes=scratch,
        cost_estimate=pl.CostEstimate(flops=flops, bytes_accessed=30 * 2**20, transcendentals=4 * row_count * seq_len * HEADS),
        compiler_params=pltpu.CompilerParams(
            dimension_semantics=("arbitrary", "arbitrary"), vmem_limit_bytes=VMEM_BYTES,
            **(dict(collective_id=0, has_side_effects=True) if linked else {})),
        name="attention_forward",
    )(lengths, content_rows, query_rows, order, onehot, *(list(weights) + [small]))


def backward_kernel(shapes, linked, len_ref, q_ref, k_ref, v_ref, g_ref, dc_ref, dg_ref, oc_ref, og_ref, tot_ref, ord_ref, small_ref, onehot_ref, *refs):
    n = len(shapes)
    grads, refs = refs[:n], refs[n:]
    outs, refs = refs[:n], refs[n:]
    grad_ref, lows_ref, sums_ref, mask_ref, acc_ref, near_ref = refs[:6]
    refs = refs[6:]
    hp = pl.program_id(0)
    s = pl.program_id(1)
    last = pl.num_programs(1) - 1
    step = hp * pl.num_programs(1) + s
    seq_len = q_ref.shape[0]
    blocks = seq_len // LANE
    half = seq_len // 2
    steps = (HEADS // 2) * ord_ref.shape[0]
    if linked:
        bufs = [refs[7 * w : 7 * w + 7] for w in range(n)]
        send, recv = refs[7 * n :]
        net = Reduce(shapes, grads, outs, bufs, send, recv)
        items, ticks = plan(net, n, list(range(n)))

        @pl.when(step == 0)
        def _():
            net.barrier()
            for w, k in items:
                net.start(w, k)

        tail = ticks[-2:]
        ticks = ticks[:-2]
        for at in range(1, steps):
            acts = [a for i, t in enumerate(ticks) if 1 + i * (steps - 1) // len(ticks) == at for a in t]

            @pl.when(step == at)
            def _():
                for act in acts:
                    act()

    @pl.when(hp == 0)
    def _():
        fill_mask(mask_ref, ord_ref, len_ref[s], s, seq_len, True)

    @pl.when(step == 0)
    def _():
        fill_near(near_ref, small_ref[...], onehot_ref)

    lane = lax.broadcasted_iota(jnp.int32, (seq_len, LANE), 1)
    ones = jnp.ones((seq_len, LANE), BF16)
    zero = jnp.zeros((), BF16)
    keys = k_ref[...]
    keys_wide = jnp.concatenate([keys, ones], 1)
    values_wide = jnp.concatenate([v_ref[...], ones], 1)
    keys_turned = keys.astype(F32).T.astype(BF16)
    lane_r = lax.broadcasted_iota(jnp.int32, (LANE, LANE), 0)
    lane_c = lax.broadcasted_iota(jnp.int32, (LANE, LANE), 1)
    pick = (lane_r // HEAD == lane_c).astype(BF16)
    grad_keys = None
    grad_values = None
    grad_query = [[], []]
    streams = []
    for src, grad, out, tot in ((q_ref, dc_ref, oc_ref, tot_ref[0, 0]), (g_ref, dg_ref, og_ref, tot_ref[1, 0])):
        g = grad[...]
        delta = nn((g.astype(F32) * out[...].astype(F32)).astype(BF16), pick)
        streams.append((src[...], g, -delta, tot))
    for t in range(2):
        head = hp * 2 + t
        sel = head_lanes((seq_len, LANE), t)
        head_row = near_ref[pl.ds(head, 1), :]
        near = skewed(head_row[:, :NEAR], 3 * LANE)
        bias = tile_bias(near, head_row[:, NEAR : NEAR + 1], head_row[:, NEAR + 1 : NEAR + 2], seq_len, 1)
        for c0 in range(0, seq_len, half):
            both = None
            for stream in range(2):
                q, g, delta, tot = streams[stream]
                q = jnp.where(sel, q, zero)[c0 : c0 + half]
                g = jnp.where(sel, g, zero)[c0 : c0 + half]
                d = delta[c0 : c0 + half]
                ln = lane[c0 : c0 + half]
                tt = jnp.where((ln == head) | (ln == head + HEAD), tot[c0 : c0 + half], zero)
                dd = jnp.where(ln == t, d, 0.0)
                dhi = dd.astype(BF16)
                dlo = pltpu.roll(dd - dhi.astype(F32), HEAD, 1).astype(BF16)
                raw = nt(keys_wide, jnp.concatenate([q, tt], 1))
                dpr = nt(values_wide, jnp.concatenate([g, dhi + dlo], 1))
                probs, grads = [], []
                for rb in range(blocks):
                    sl = slice(rb * LANE, (rb + 1) * LANE)
                    part = raw[sl] + (bias[rb][:, c0 : c0 + half] + mask_ref[s, sl, c0 : c0 + half])
                    r0 = rb * LANE
                    if stream == 1 and c0 <= r0 < c0 + half:
                        hit = lane_r == lane_c
                        if rb == 0:
                            hit = hit & (lane_r != 0)
                        x0 = r0 - c0
                        diag = jnp.where(hit, MASKED, part[:, x0 : x0 + LANE])
                        pieces = []
                        if x0 > 0:
                            pieces.append(part[:, :x0])
                        pieces.append(diag)
                        if x0 + LANE < half:
                            pieces.append(part[:, x0 + LANE :])
                        part = jnp.concatenate(pieces, 1)
                    p = jnp.exp2(part)
                    probs.append(p.astype(BF16))
                    grads.append(p * dpr[sl])
                low = [x.astype(BF16) for x in grads]
                prob = jnp.concatenate(probs, 0)
                gl = jnp.concatenate(low, 0)
                gv = nn(prob, g)
                gk = nn(gl, q)
                grad_values = gv if grad_values is None else grad_values + gv
                grad_keys = gk if grad_keys is None else grad_keys + gk
                grad_query[stream].append(nn(keys_turned[t * HEAD : (t + 1) * HEAD], gl))
                both = grads if both is None else [a + b for a, b in zip(both, grads)]
            sums = {}
            for rb in range(blocks):
                for cb in range(half // LANE):
                    e = cb + c0 // LANE - rb
                    e = max(-2, min(2, e))
                    x = both[rb][:, cb * LANE : (cb + 1) * LANE]
                    sums[e] = x if e not in sums else sums[e] + x
            for e, x in sums.items():
                lanes = slice((e + 2) * LANE, (e + 3) * LANE)
                fresh = c0 == 0
                if fresh:
                    @pl.when(s == 0)
                    def _():
                        acc_ref[t, :, lanes] = x

                    @pl.when(s > 0)
                    def _():
                        acc_ref[t, :, lanes] = acc_ref[t, :, lanes] + x
                else:
                    acc_ref[t, :, lanes] = acc_ref[t, :, lanes] + x
            if c0 == 0:
                for e in range(-2, 3):
                    if e not in sums:
                        @pl.when(s == 0)
                        def _():
                            acc_ref[t, :, (e + 2) * LANE : (e + 3) * LANE] = jnp.zeros((LANE, LANE), F32)
    count = seq_len // half
    scale = 1.0 / math.sqrt(HEAD)

    @pl.when(s == 0)
    def _():
        lows_ref[...] = jnp.zeros_like(lows_ref)

    def put_grad(k, value):
        grad_ref[k] = value
        lows_ref[k] = lows_ref[k] + fold8(value.astype(F32))

    for stream, ref in ((0, 0), (1, 3)):
        pieces = grad_query[stream]
        top = jnp.concatenate(pieces[:count], 1)
        bot = jnp.concatenate(pieces[count:], 1)
        put_grad(ref, (jnp.concatenate([top, bot], 0) * scale).T.astype(BF16))
    put_grad(1, (grad_keys * LN2).astype(BF16))
    put_grad(2, grad_values.astype(BF16))

    @pl.when(s == last)
    def _():
        for t in range(2):
            near = jnp.concatenate([acc_ref[t, :, LANE : 4 * LANE], jnp.zeros((LANE, LANE), F32)], 1)
            mirror = (lane_r + lane_c == LANE - 1).astype(F32)
            flipped = lax.dot_general(mirror, near, (((1,), (0,)), ((), ())), precision=lax.Precision.HIGHEST, preferred_element_type=F32)
            turned = pltpu.roll(flipped, 0, 1, stride=1, stride_axis=0)
            row = jnp.sum(turned, 0, keepdims=True)
            below = jnp.sum(acc_ref[t, :, :LANE], 0, keepdims=True)
            above = jnp.sum(acc_ref[t, :, 4 * LANE :], 0, keepdims=True)
            sums_ref[pl.ds(hp * 2 + t, 1), :] = jnp.concatenate([row, below, above], 1)

    if linked:

        @pl.when(step == steps - 1)
        def _():
            for acts in tail:
                for act in acts:
                    act()


def backward_attention(linked, proj, grad_mixed, mixed, totals, lengths, order, small, weight_grads):
    rows, width = grad_mixed.shape
    seqs, seq_len = order.shape
    pairs = width // LANE
    onehot = table_onehot(1, small.shape[0] // ROWS)
    shapes = [(g.shape[0] // 8, g.shape[1]) for g in weight_grads]
    n = len(shapes)
    block = lambda off: pl.BlockSpec((seq_len, LANE), lambda h, s, off=off: (s, off + h))
    low = pl.BlockSpec((seq_len, LANE), lambda h, s: (seqs + s, h))
    anywhere = pl.BlockSpec(memory_space=pl.ANY)
    inside = pl.BlockSpec(memory_space=pltpu.VMEM)
    sums_shape = (2 * pairs, NEAR + 2 * LANE)
    scratch = [
        pltpu.VMEM((seqs, seq_len, seq_len), F32),
        pltpu.VMEM((2, LANE, 5 * LANE), F32),
        pltpu.VMEM((LANE, NEAR + LANE), F32),
    ]
    if linked:
        scratch += Reduce.scratch(shapes)
        scratch += [pltpu.SemaphoreType.DMA((n, 4, Reduce.SLOTS)), pltpu.SemaphoreType.DMA((n, 4, Reduce.SLOTS))]
    outs = pl.pallas_call(
        functools.partial(backward_kernel, shapes, linked),
        grid=(pairs, seqs),
        in_specs=[
            pl.BlockSpec(memory_space=pltpu.SMEM),
            block(0), block(pairs), block(2 * pairs), block(3 * pairs),
            block(0), low, block(0), low,
            pl.BlockSpec((2, 1, seq_len, LANE), lambda h, s: (0, s, 0, 0)),
            inside, inside, inside,
        ] + [anywhere] * n,
        out_specs=[anywhere] * n + [pl.BlockSpec((4, seq_len, LANE), lambda h, s: (0, s, h)), pl.BlockSpec((4, 8, LANE), lambda h, s: (0, 0, h)), pl.BlockSpec(sums_shape, lambda h, s: (0, 0))],
        out_shape=[jax.ShapeDtypeStruct(a, BF16) for a in shapes] + [jax.ShapeDtypeStruct((4, rows // 2, width), BF16), jax.ShapeDtypeStruct((4, 8, width), F32), jax.ShapeDtypeStruct(sums_shape, F32)],
        scratch_shapes=scratch,
        cost_estimate=pl.CostEstimate(flops=20 * rows * seq_len * width, bytes_accessed=30 * 2**20, transcendentals=2 * rows * seq_len * HEADS),
        compiler_params=pltpu.CompilerParams(
            dimension_semantics=("arbitrary", "arbitrary"), vmem_limit_bytes=VMEM_BYTES,
            **(dict(collective_id=1, has_side_effects=True) if linked else {})),
        name="attention_backward",
    )(lengths, proj, proj, proj, proj, grad_mixed, grad_mixed, mixed, mixed, totals, order, small, onehot, *weight_grads)
    sums = outs[n + 2]
    fold = np.zeros((sums_shape[1], BUCKETS), np.float32)
    fold[:NEAR] = np.roll(near_onehot(1).T, LANE - 1, 0)
    fold[NEAR : NEAR + LANE, BUCKETS - 1] = 1
    fold[NEAR + LANE :, BUCKETS // 2 - 1] = 1
    grad_table = jnp.dot(sums, jnp.asarray(fold), precision=lax.Precision.HIGHEST).T
    return outs[:n], outs[n], jnp.sum(outs[n + 1], 1), grad_table


def small_reduce(net, w, part, out, bufs):
    own, core, across_x, across_y, far = bufs
    rows = 4 * ROWS
    mine = part.at[pl.ds(pl.multiple_of(net.c * rows, rows), rows), :]
    other = part.at[pl.ds(pl.multiple_of((1 - net.c) * rows, rows), rows), :]
    load = pltpu.make_async_copy(mine, own.at[0], net.send.at[w, 0, 7])
    to_core = net.copy((w, 0, 0), other, core, net.r, net.sib)
    to_x = net.copy((w, 0, 1), own.at[1], across_x, net.xr, net.f)
    to_y = net.copy((w, 0, 2), own.at[2], across_y, net.yr, net.f)
    z_rows = lambda s: pl.ds(pl.multiple_of((net.z + s) % 4 * ROWS, ROWS), ROWS)
    to_far = [net.copy((w, s, 3), own.at[3, z_rows(s), :], far.at[s - 1], net.r, net.along(s)) for s in (1, 2, 3)]

    def first():
        load.start()
        to_core.start()

    def second():
        load.wait()
        to_core.wait_recv()
        own[1] = own[0] + core[...]
        to_x.start()

    def third():
        to_x.wait_recv()
        own[2] = own[1] + across_x[...]
        to_y.start()

    def fourth():
        to_y.wait_recv()
        own[3] = own[2] + across_y[...]
        for d in to_far:
            d.start()

    def fifth():
        for d in to_far:
            d.wait_recv()
        out[...] = own[3, z_rows(0), :] + far[0] + far[1] + far[2]
        for d in [to_core, to_x, to_y] + to_far:
            d.wait_send()

    return first, second, third, fourth, fifth


def input_grads(rows, grads, joined, branch):
    width = branch.shape[1]
    total = grads.shape[1]
    low = pl.ds(pl.multiple_of(total + rows.start, 256), rows.size)
    content = branch[rows, :].astype(F32)
    for k in range(3):
        content = content + nt(grads[k, rows, :], joined[:, k * width : (k + 1) * width])
    query = branch[low, :].astype(F32) + nt(grads[3, rows, :], joined[:, :width])
    return content.astype(BF16), query.astype(BF16)


def reduce_kernel(shapes, n, *refs):
    grads, small_part, sources, refs = refs[:n], refs[n], refs[n + 1 : n + 4], refs[n + 4 :]
    outs, small_out, stream_outs, refs = refs[:n], refs[n], refs[n + 1 : n + 3], refs[n + 3 :]
    held, results, own_sem, refs = refs[:3], refs[3:5], refs[5], refs[6:]
    bufs = [refs[7 * w : 7 * w + 7] for w in range(n)]
    small_bufs, (send, recv) = refs[7 * n : 7 * n + 5], refs[7 * n + 5 :]
    net = Reduce(shapes, grads, outs, bufs, send, recv)
    first, second, third, fourth, fifth = small_reduce(net, n, small_part, small_out, small_bufs)
    fetch = [pltpu.make_async_copy(a, b, own_sem.at[k]) for k, (a, b) in enumerate(zip(sources, held))]
    store = [pltpu.make_async_copy(a, b, own_sem.at[3 + k]) for k, (a, b) in enumerate(zip(results, stream_outs))]
    net.barrier()
    items, ticks = plan(net, n, list(range(n)))
    first()
    for w, k in items:
        net.start(w, k)
    for d in fetch:
        d.start()
    for d in fetch:
        d.wait()
    pieces = 4
    chunk = results[0].shape[0] // pieces
    extra = {1: second, 4: third, 6: fourth}
    for i, acts in enumerate(ticks):
        for act in acts:
            act()
        if i in extra:
            extra[i]()
        if 3 <= i < 3 + pieces:
            rows = pl.ds((i - 3) * chunk, chunk)
            content, query = input_grads(rows, *held)
            results[0][rows, :] = content
            results[1][rows, :] = query
        if i == 2 + pieces:
            for d in store:
                d.start()
    fifth()
    for d in store:
        d.wait()


def reduce_rest(weight_grads, small_grads, grads, joined, branch):
    n = len(weight_grads)
    shapes = [(g.shape[0] // 8, g.shape[1]) for g in weight_grads]
    anywhere = pl.BlockSpec(memory_space=pl.ANY)
    inside = pl.BlockSpec(memory_space=pltpu.VMEM)
    rows = 4 * ROWS
    stream = grads.shape[1:]
    scratch = [pltpu.VMEM(a.shape, BF16) for a in (grads, joined, branch)] + [pltpu.VMEM(stream, BF16)] * 2 + [pltpu.SemaphoreType.DMA((5,))]
    scratch += Reduce.scratch(shapes)
    scratch += [pltpu.VMEM((4, rows, LANE), F32)] + [pltpu.VMEM((rows, LANE), F32)] * 3 + [pltpu.VMEM((3, ROWS, LANE), F32)]
    scratch += [pltpu.SemaphoreType.DMA((n + 1, 4, Reduce.SLOTS)), pltpu.SemaphoreType.DMA((n + 1, 4, Reduce.SLOTS))]
    return pl.pallas_call(
        functools.partial(reduce_kernel, shapes, n),
        out_shape=[jax.ShapeDtypeStruct(a, BF16) for a in shapes] + [jax.ShapeDtypeStruct((ROWS, LANE), F32)] + [jax.ShapeDtypeStruct(stream, BF16)] * 2,
        in_specs=[anywhere] * (n + 4),
        out_specs=[anywhere] * n + [inside] + [anywhere] * 2,
        scratch_shapes=scratch,
        compiler_params=pltpu.CompilerParams(collective_id=2, has_side_effects=True, vmem_limit_bytes=VMEM_BYTES),
        name="reduce_rest",
    )(*weight_grads, small_grads, grads, joined, branch)


def prepare_kernel(unit, places, *refs):
    count = len(places)
    vectors, table, weights, refs = refs[:count], refs[count], refs[count + 1 : count + 5], refs[count + 5 :]
    small_ref, outs, wide_ref, part_ref = refs[0], refs[1:5], refs[5], refs[6]
    part_ref[...] = jnp.zeros_like(part_ref)
    lane = lax.broadcasted_iota(jnp.int32, (8, LANE), 1)
    for (row, chunks), ref in zip(places, vectors):
        if chunks == 1:
            part_ref[row : row + 1, :unit] = ref[...][None, :]
            continue
        size = chunks * unit
        wide = wide_ref.shape[1]
        wide_ref[0:1, :size] = ref[...][None, :]
        value = jnp.broadcast_to(wide_ref[0:1, :], (8, wide))
        for k in range(chunks):
            turned = pltpu.roll(value, wide - k * unit, 1) if k else value
            part_ref[row + k : row + k + 1, :] = jnp.where(lane < unit, turned[:, :LANE], 0.0)[0:1]
    part_ref[TABLE_ROW : TABLE_ROW + table.shape[0], : table.shape[1]] = table[...]
    small_ref[...] = part_ref[...].astype(BF16)
    for a, b in zip(weights, outs):
        b[...] = a[...].astype(BF16)


def prepare(vectors, table, weights, unit):
    places, row = [], 0
    for v in vectors:
        places.append((row, v.shape[0] // unit))
        row += v.shape[0] // unit
    widest = max(v.shape[0] for v in vectors)
    widest = (widest + LANE - 1) // LANE * LANE
    outs = pl.pallas_call(
        functools.partial(prepare_kernel, unit, places),
        out_shape=[jax.ShapeDtypeStruct((ROWS, LANE), BF16)] + [jax.ShapeDtypeStruct(w.shape, BF16) for w in weights],
        scratch_shapes=[pltpu.VMEM((8, widest), F32), pltpu.VMEM((ROWS, LANE), F32)],
        compiler_params=pltpu.CompilerParams(vmem_limit_bytes=VMEM_BYTES),
        name="prepare",
    )(*vectors, table, *weights)
    return outs[0], outs[1:]


ERF_P = 0.3275911 * 0.7071067811865476
ERF_A = (0.254829592 * 0.5, -0.284496736 * 0.5, 1.421413741 * 0.5, -1.453152027 * 0.5, 1.061405429 * 0.5)


def gelu_pair(z):
    bell = jnp.exp2(z * z * (-0.5 * LOG2E))
    t = 1.0 / (1.0 + ERF_P * jnp.abs(z))
    tail = ERF_A[4]
    for a in ERF_A[3::-1]:
        tail = tail * t + a
    tail = tail * t * bell
    share = jnp.where(z < 0.0, tail, 1.0 - tail)
    return z * share, share + z * bell * inv_root_tau


def norm_rows(summed):
    row_mean = jnp.mean(summed, -1, keepdims=True)
    centered = summed - row_mean
    inverse = lax.rsqrt(jnp.mean(centered * centered, -1, keepdims=True) + eps_norm)
    return centered * inverse, inverse


def norm_rows_back(scaled, normed, inverse):
    return inverse * (scaled - jnp.mean(scaled, -1, keepdims=True) - normed * jnp.mean(scaled * normed, -1, keepdims=True))


def fold8(value):
    rows, cols = value.shape
    return jnp.sum(value.reshape(rows // 8, 8, cols), 0)


def ffn_kernel(chunk, len_ref, mixed_ref, content_ref, query_ref, ccot_ref, qcot_ref, small_ref, wo_hbm, win_hbm, wout_hbm,
               cout_ref, qout_ref, hid_ref, dz_ref, first_ref, dffn_ref, dbranch_ref, dmixed_ref, sums_ref, wide_sums_ref,
               wo_ref, win_ref, wout_ref, vec_ref, shift_ref, slope_ref, acc_ref, wide_acc_ref, sem):
    i = pl.program_id(0)
    n = pl.num_programs(0)
    rows, width = mixed_ref.shape
    hidden = win_ref.shape[1]
    loads = [pltpu.make_async_copy(a, b, sem.at[k]) for k, (a, b) in enumerate(((wo_hbm, wo_ref), (win_hbm, win_ref), (wout_hbm, wout_ref)))]

    @pl.when(i == 0)
    def _():
        for d in loads:
            d.start()
        small = small_ref[...].astype(F32)
        shards = small.shape[0] // ROWS
        unit = width // shards
        for k in range(2, 8):
            vec_ref[k : k + 1, :] = spread_rows(small, [f * ROWS + k for f in range(shards)], 0, shards, unit)
        count = hidden // unit
        shift_ref[0:1, :] = spread_rows(small, [k // 4 * ROWS + 8 + k % 4 for k in range(count)], 0, count, unit)
        acc_ref[...] = jnp.zeros_like(acc_ref)
        wide_acc_ref[...] = jnp.zeros_like(wide_acc_ref)
        for d in loads:
            d.wait()

    first_stream = i < n // 2
    vec = lambda k: vec_ref[k : k + 1, :]

    def add_sum(k, value):
        acc_ref[k] = acc_ref[k] + fold8(value)

    residual = jnp.where(first_stream, content_ref[...], query_ref[...]).astype(F32)
    branch = nn(mixed_ref[...], wo_ref[...]) + vec(2)
    normed_one, inverse_one = norm_rows(residual + branch)
    first_low = (normed_one * vec(3) + vec(4)).astype(BF16)
    first_ref[...] = first_low
    for c in range(0, hidden, chunk):
        cols = slice(c, c + chunk)
        value, slope = gelu_pair(nn(first_low, win_ref[:, cols]) + shift_ref[0:1, cols])
        hid_ref[:, cols] = value.astype(BF16)
        slope_ref[:, cols] = slope.astype(BF16)
    ffn = nn(hid_ref[...], wout_ref[...]) + vec(5)
    normed_two, inverse_two = norm_rows(first_low.astype(F32) + ffn)
    final = (normed_two * vec(6) + vec(7)).astype(BF16)

    @pl.when(first_stream)
    def _():
        cout_ref[...] = final

    @pl.when(jnp.logical_not(first_stream))
    def _():
        qout_ref[...] = final

    per_stream = n // 2
    at = jnp.where(first_stream, i, i - per_stream) * rows
    seq_len = per_stream * rows // len_ref.shape[0]
    seq = at // seq_len
    place = at - seq * seq_len + lax.broadcasted_iota(jnp.int32, (rows, 1), 0)
    upstream = jnp.where(first_stream, ccot_ref[...], qcot_ref[...]).astype(F32)
    upstream = jnp.where(place < len_ref[seq], upstream, 0.0)
    add_sum(5, upstream * normed_two)
    add_sum(6, upstream)
    grad_two = norm_rows_back(upstream * vec(6), normed_two, inverse_two)
    grad_ffn = grad_two.astype(BF16)
    dffn_ref[...] = grad_ffn
    add_sum(4, grad_ffn.astype(F32))
    for c in range(0, hidden, chunk):
        cols = slice(c, c + chunk)
        grad = nt(grad_ffn, wout_ref[cols, :]) * slope_ref[:, cols].astype(F32)
        wide_acc_ref[:, cols] = wide_acc_ref[:, cols] + fold8(grad)
        dz_ref[:, cols] = grad.astype(BF16)
    grad_first = grad_two + nt(dz_ref[...], win_ref[...])
    add_sum(2, grad_first * normed_one)
    add_sum(3, grad_first)
    grad_branch = norm_rows_back(grad_first * vec(3), normed_one, inverse_one).astype(BF16)
    dbranch_ref[...] = grad_branch
    add_sum(1, grad_branch.astype(F32))
    dmixed_ref[...] = nt(grad_branch, wo_ref[...]).astype(BF16)

    @pl.when(i == n - 1)
    def _():
        for k in range(8):
            sums_ref[k : k + 1, :] = jnp.sum(acc_ref[k], 0, keepdims=True)
        wide_sums_ref[...] = jnp.sum(wide_acc_ref[...], 0, keepdims=True)


def ffn_stage(mixed, content_rows, query_rows, content_cot, query_cot, lengths, small, out_proj, in_proj, out_ffn, rows=512, chunk=768):
    total, width = mixed.shape
    hidden = in_proj.shape[1]
    n = total // rows
    half = n // 2
    anywhere = pl.BlockSpec(memory_space=pl.ANY)
    row_block = lambda cols: pl.BlockSpec((rows, cols), lambda i: (i, 0))
    low = pl.BlockSpec((rows, width), lambda i: (jnp.minimum(i, half - 1), 0))
    high = pl.BlockSpec((rows, width), lambda i: (jnp.maximum(i - half, 0), 0))
    whole = lambda shape: pl.BlockSpec(shape, lambda i: (0,) * len(shape))
    shape = jax.ShapeDtypeStruct
    return pl.pallas_call(
        functools.partial(ffn_kernel, chunk),
        grid=(n,),
        in_specs=[pl.BlockSpec(memory_space=pltpu.SMEM), row_block(width), low, high, low, high, whole(small.shape)] + [anywhere] * 3,
        out_specs=[low, high, row_block(hidden), row_block(hidden)] + [row_block(width)] * 4 + [whole((8, width)), whole((1, hidden))],
        out_shape=[shape((total // 2, width), BF16)] * 2 + [shape((total, hidden), BF16)] * 2 + [shape((total, width), BF16)] * 4
        + [shape((8, width), F32), shape((1, hidden), F32)],
        scratch_shapes=[
            pltpu.VMEM((width, width), BF16),
            pltpu.VMEM((width, hidden), BF16),
            pltpu.VMEM((hidden, width), BF16),
            pltpu.VMEM((8, width), F32),
            pltpu.VMEM((8, hidden), F32),
            pltpu.VMEM((rows, hidden), BF16),
            pltpu.VMEM((8, 8, width), F32),
            pltpu.VMEM((8, hidden), F32),
            pltpu.SemaphoreType.DMA((3,)),
        ],
        cost_estimate=pl.CostEstimate(flops=4 * total * width * (2 * hidden + width), bytes_accessed=60 * 2**20, transcendentals=2 * total * hidden),
        compiler_params=pltpu.CompilerParams(dimension_semantics=("arbitrary",), vmem_limit_bytes=VMEM_BYTES),
        name="ffn_stage",
    )(lengths, mixed, content_rows, query_rows, content_cot, query_cot, small, out_proj, in_proj, out_ffn)


def rows_inner(left_op, right_op):
    return lax.dot_general(
        left_op, right_op, (((0,), (0,)), ((), ())), preferred_element_type=jnp.float32
    )


def times_transpose(left_op, right_op):
    return lax.dot_general(
        left_op, right_op, (((1,), (1,)), ((), ())), preferred_element_type=jnp.float32
    )


def pack_small(groups, shards):
    rows = []
    for g in groups:
        g = g.reshape(shards, -1, g.shape[-1]) if g.ndim > 1 else g
        rows.append(g)
    wide = [jnp.pad(g, ((0, 0), (0, 0), (0, LANE - g.shape[2]))) for g in rows]
    joined = jnp.concatenate(wide, 1)
    joined = jnp.pad(joined, ((0, 0), (0, ROWS - joined.shape[1]), (0, 0)))
    return joined.reshape(shards * ROWS, LANE)


def on_device(axes, content_stream, query_stream, lengths, factor_order, qkv_weight, qv_bias, out_weight, out_bias, norm1_gain, norm1_bias, rel_table, ffn_in_weight, ffn_in_bias, ffn_out_weight, ffn_out_bias, norm2_gain, norm2_bias, content_cot, query_cot):
    linked = axes == (4, 8)
    shards = axes[1]
    seq_count, seq_len, width = content_stream.shape
    row_count = seq_count * seq_len
    unit = width // shards
    small_args = (qv_bias, out_bias, norm1_gain, norm1_bias, ffn_out_bias, norm2_gain, norm2_bias, ffn_in_bias)
    weights = (qkv_weight, out_weight, ffn_in_weight, ffn_out_weight)
    if linked:
        small, weights = prepare(small_args, rel_table, weights, unit)
    else:
        small = pack_small([p.reshape(1, -1, unit) for p in small_args] + [rel_table[None]], 1).astype(BF16)
        weights = [w.astype(BF16) for w in weights]
    content_rows = content_stream.reshape(row_count, width)
    query_rows = query_stream.reshape(row_count, width)
    if linked:
        out_proj, in_proj, out_ffn, joined_proj, small, mixed, totals, proj = forward_attention(
            True, content_rows, query_rows, lengths, factor_order, weights, small)
    else:
        gather = lambda a: lax.all_gather(a, "fsdp", axis=0, tiled=True)
        joined_proj, out_proj, in_proj, out_ffn = [gather(w) for w in weights]
        small = gather(small)
        mixed, totals, proj = forward_attention(False, content_rows, query_rows, lengths, factor_order, [joined_proj], small)
    mixed_rows = mixed.reshape(2 * row_count, width)
    flat_cot = lambda a: a.reshape(row_count, width)
    content_out, query_out, hidden_low, grad_hidden, first_low, grad_ffn, grad_branch, grad_mixed, sums, wide_sums = ffn_stage(
        mixed_rows, content_rows, query_rows, flat_cot(content_cot), flat_cot(query_cot), lengths, small, out_proj, in_proj, out_ffn)
    grad_out_ffn = rows_inner(hidden_low, grad_ffn).astype(BF16)
    grad_in_proj = rows_inner(first_low, grad_hidden).astype(BF16)
    grad_out_proj = rows_inner(mixed_rows, grad_branch).astype(BF16)
    ready = [grad_in_proj, grad_out_ffn, grad_out_proj] if linked else []
    early, grads, low_sums, grad_table = backward_attention(linked, proj, grad_mixed, mixed_rows, totals, lengths, factor_order, small, ready)
    grad_q = rows_inner(content_rows, grads[0]) + rows_inner(query_rows, grads[3])
    grad_joined = jnp.concatenate([grad_q, rows_inner(content_rows, grads[1]), rows_inner(content_rows, grads[2])], 1).astype(BF16)
    grad_proj_shift = jnp.concatenate([low_sums[0] + low_sums[3], low_sums[2]])
    rows_of = lambda g: g.reshape(shards, -1, unit) if g.ndim == 1 or g.shape[0] == 1 else g.reshape(-1, shards, unit).transpose(1, 0, 2)
    packed = pack_small([rows_of(grad_proj_shift), rows_of(sums[1:7]), rows_of(wide_sums), grad_table.reshape(shards, -1, HEADS)], shards)
    if linked:
        packed = packed.reshape(4, 2, ROWS, LANE).transpose(1, 0, 2, 3).reshape(8 * ROWS, LANE)
        sum_joined, mine, content_grad_rows, query_grad_rows = reduce_rest([grad_joined], packed, grads, joined_proj, grad_branch)
        sum_in, sum_out, sum_proj = early
    else:
        scatter = lambda a: lax.psum(lax.psum_scatter(a, "fsdp", scatter_dimension=0, tiled=True), "rep")
        sum_joined, sum_in, sum_out, sum_proj = [scatter(a) for a in (grad_joined, grad_in_proj, grad_out_ffn, grad_out_proj)]
        mine = scatter(packed)
        content_grad_rows = grad_branch[:row_count].astype(F32) + (
            times_transpose(grads[0], joined_proj[:, :width])
            + times_transpose(grads[1], joined_proj[:, width : 2 * width])
            + times_transpose(grads[2], joined_proj[:, 2 * width :])
        )
        query_grad_rows = grad_branch[row_count:].astype(F32) + times_transpose(grads[3], joined_proj[:, :width])
    sum_joined, sum_in, sum_out, sum_proj = [a.astype(F32) for a in (sum_joined, sum_in, sum_out, sum_proj)]
    vec = lambda k: mine[k, :unit]
    block_shape = (seq_count, seq_len, width)
    return (
        content_out.reshape(block_shape),
        query_out.reshape(block_shape),
        content_grad_rows.reshape(block_shape).astype(BF16),
        query_grad_rows.reshape(block_shape).astype(BF16),
        sum_joined,
        mine[0:2, :unit].reshape(-1),
        sum_proj,
        vec(2),
        vec(3),
        vec(4),
        mine[TABLE_ROW : TABLE_ROW + rel_table.shape[0], :HEADS],
        sum_in,
        mine[8:12, :unit].reshape(-1),
        sum_out,
        vec(5),
        vec(6),
        vec(7),
    )


def solution(mesh):
    in_specs = (
        P(("rep", "fsdp"), None, None),
        P(("rep", "fsdp"), None, None),
        P(("rep", "fsdp")),
        P(("rep", "fsdp"), None),
        P("fsdp", None),
        P("fsdp"),
        P("fsdp", None),
        P("fsdp"),
        P("fsdp"),
        P("fsdp"),
        P("fsdp", None),
        P("fsdp", None),
        P("fsdp"),
        P("fsdp", None),
        P("fsdp"),
        P("fsdp"),
        P("fsdp"),
        P(("rep", "fsdp"), None, None),
        P(("rep", "fsdp"), None, None),
    )
    out_specs = (
        P(("rep", "fsdp"), None, None),
        P(("rep", "fsdp"), None, None),
        P(("rep", "fsdp"), None, None),
        P(("rep", "fsdp"), None, None),
        P("fsdp", None),
        P("fsdp"),
        P("fsdp", None),
        P("fsdp"),
        P("fsdp"),
        P("fsdp"),
        P("fsdp", None),
        P("fsdp", None),
        P("fsdp"),
        P("fsdp", None),
        P("fsdp"),
        P("fsdp"),
        P("fsdp"),
    )
    return jax.shard_map(
        functools.partial(on_device, tuple(mesh.shape[a] for a in mesh.axis_names)),
        mesh=mesh,
        in_specs=in_specs,
        out_specs=out_specs,
        check_vma=False,
    )
```

```python
import functools
import math

import jax
import jax.numpy as jnp
import numpy as np
from jax import lax
from jax.experimental import pallas as pl
from jax.experimental.pallas import tpu as pltpu
from jax.sharding import PartitionSpec as P

HEADS = 12
HEAD = 64
BUCKETS = 32
MAX_DIST = 128
LANE = 128
NEAR = 512
ROWS = 16
TABLE_ROW = 12
MASKED = -1e30
LOG2E = 1.4426950408889634
LN2 = 0.6931471805599453
F32 = jnp.float32
BF16 = jnp.bfloat16
MESH = pl.DeviceIdType.MESH
VMEM_BYTES = 60 * 2**20
eps_norm = 1e-05
inv_root_tau = 0.3989422804014327


def bucket_of(offset):
    half_count = BUCKETS // 2
    result = (offset < 0).astype(np.int64) * half_count
    distance = np.abs(offset)
    exact_count = half_count // 2
    fraction = np.log(np.maximum(distance, 1) / exact_count) / np.log(MAX_DIST / exact_count)
    beyond = exact_count + (fraction * (half_count - exact_count)).astype(np.int64)
    beyond = np.minimum(beyond, half_count - 1)
    result = result + np.where(distance < exact_count, distance, beyond)
    return result.astype(np.int32)


def nt(a, b):
    return lax.dot_general(a, b, (((1,), (1,)), ((), ())), preferred_element_type=F32)


def nn(a, b):
    return lax.dot_general(a, b, (((1,), (0,)), ((), ())), preferred_element_type=F32)


def signed_places():
    places = np.arange(NEAR)
    return np.where(places < NEAR - LANE, places, places - NEAR)


def near_onehot(sign):
    offset = sign * (signed_places() - LANE)
    return (bucket_of(offset)[None, :] == np.arange(BUCKETS)[:, None]).astype(np.float32)


def skewed(row, width):
    wide = jnp.broadcast_to(row, (LANE, NEAR))
    return pltpu.roll(wide, 0, 1, stride=1, stride_axis=0)[:, :width]


def tile_bias(near, far_pos, far_neg, seq_len, sign):
    blocks = seq_len // LANE
    rows = []
    for rb in range(blocks):
        parts = []
        for cb in range(blocks):
            e = cb - rb
            if abs(e) <= 1:
                parts.append(near[:, (e + 1) * LANE : (e + 2) * LANE])
            else:
                parts.append(jnp.broadcast_to(far_pos if e * sign > 0 else far_neg, (LANE, LANE)))
        rows.append(jnp.concatenate(parts, 1))
    return rows


def head_lanes(shape, t):
    lane = lax.broadcasted_iota(jnp.int32, shape, 1)
    return (lane >= t * HEAD) & (lane < (t + 1) * HEAD)


def flip(v, m):
    a, b = v // 2, v % 2
    if m & 2:
        a = 1 - a
    if m & 1:
        b = 1 - b
    return a * 2 + b


def table_onehot(sign, shards):
    per_shard = BUCKETS // shards
    result = np.zeros((shards * ROWS, NEAR + LANE), np.float32)
    near = near_onehot(sign)
    for bucket in range(BUCKETS):
        row = bucket // per_shard * ROWS + TABLE_ROW + bucket % per_shard
        result[row, :NEAR] = near[bucket]
        result[row, NEAR] = bucket == BUCKETS // 2 - 1
        result[row, NEAR + 1] = bucket == BUCKETS - 1
    return jnp.asarray(result, BF16)


class Links:
    def __init__(self, send, recv):
        self.send, self.recv = send, recv
        self.r = lax.axis_index("rep")
        self.f = lax.axis_index("fsdp")
        self.y, self.x = self.r // 2, self.r % 2
        self.z, self.c = self.f // 2, self.f % 2
        self.xr, self.yr = flip(self.r, 1), flip(self.r, 2)
        self.sib = self.z * 2 + 1 - self.c

    def along(self, s):
        return ((self.z + s) % 4) * 2 + self.c

    def copy(self, at, src, dst, rep, fsdp):
        return pltpu.make_async_remote_copy(
            src_ref=src, dst_ref=dst, send_sem=self.send.at[at], recv_sem=self.recv.at[at],
            device_id={"rep": rep, "fsdp": fsdp}, device_id_type=MESH)

    def barrier(self):
        sem = pltpu.get_barrier_semaphore()
        peers = [(self.r, self.along(s)) for s in (1, 2, 3)]
        peers += [(self.xr, self.f), (self.yr, self.f), (self.r, self.sib)]
        for rep, fsdp in peers:
            pl.semaphore_signal(sem, inc=1, device_id={"rep": rep, "fsdp": fsdp}, device_id_type=MESH)
        pl.semaphore_wait(sem, len(peers))


def quarter_of(ref, rows, cols, owner, q, part=None):
    pr, pc = rows // 2, cols // 2
    r0, c0 = owner * rows + (q // 2) * pr, (q % 2) * pc
    if part is not None:
        if pr % 32 == 0:
            r0, pr = r0 + part * (pr // 2), pr // 2
        else:
            first = (pc // LANE + 1) // 2 * LANE
            c0, pc = (c0, first) if part == 0 else (c0 + first, pc - first)
    return ref.at[pl.ds(pl.multiple_of(r0, 16), pr), pl.ds(pl.multiple_of(c0, LANE), pc)]


class Gather(Links):
    SLOTS = 12

    def __init__(self, shapes, shards, fulls, send, recv):
        super().__init__(send, recv)
        self.shapes, self.shards, self.fulls = shapes, shards, fulls

    def z_send(self, w, s):
        rows, cols = self.shapes[w]
        src = quarter_of(self.shards[w], rows, cols, 0, self.r)
        dst = quarter_of(self.fulls[w], rows, cols, self.f, self.r)
        return self.copy((w, s, 0), src, dst, self.r, self.along(s))

    def hop(self, w, s, slot, q, rep, fsdp, part=None):
        rows, cols = self.shapes[w]
        place = quarter_of(self.fulls[w], rows, cols, self.along(4 - s), q, part)
        return self.copy((w, s, slot), place, place, rep, fsdp)

    def own_place(self, w):
        rows = self.shapes[w][0]
        return self.fulls[w].at[pl.ds(pl.multiple_of(self.f * rows, 16), rows), :]

    def own_sib(self, w):
        return self.copy((w, 0, 0), self.shards[w], self.own_place(w), self.r, self.sib)

    def own_here(self, w):
        return pltpu.make_async_copy(self.shards[w], self.own_place(w), self.send.at[w, 0, 1])

    def h_x(self, w, s):
        return self.hop(w, s, 1, self.r, self.xr, self.f)

    def h_y(self, w, s):
        return self.hop(w, s, 2, self.r, self.yr, self.f)

    def h_dy(self, w, s):
        return self.hop(w, s, 3, self.xr, self.yr, self.f, 0)

    def h_dx(self, w, s):
        return self.hop(w, s, 4, self.yr, self.xr, self.f, 1)

    def h_sib(self, w, s, m):
        return self.hop(w, s, 5 + m, flip(self.r, m), self.r, self.sib)

    def start(self, w):
        for s in (1, 2, 3):
            self.z_send(w, s).start()
        self.own_sib(w).start()
        self.own_here(w).start()

    def relay_z(self, w, s):
        self.z_send(w, s).wait_recv()
        self.h_x(w, s).start()
        self.h_y(w, s).start()
        self.h_sib(w, s, 0).start()

    def relay_xy(self, w, s):
        self.h_x(w, s).wait_recv()
        self.h_dy(w, s).start()
        self.h_sib(w, s, 1).start()
        self.h_y(w, s).wait_recv()
        self.h_dx(w, s).start()
        self.h_sib(w, s, 2).start()

    def relay_diag(self, w, s):
        self.h_dy(w, s).wait_recv()
        self.h_dx(w, s).wait_recv()
        self.h_sib(w, s, 3).start()

    def arrive(self, w):
        for s in (1, 2, 3):
            for m in range(4):
                self.h_sib(w, s, m).wait_recv()
        self.own_sib(w).wait_recv()
        self.own_here(w).wait()

    def drain(self, w):
        for s in (1, 2, 3):
            for d in (self.z_send(w, s), self.h_x(w, s), self.h_y(w, s), self.h_dy(w, s), self.h_dx(w, s)):
                d.wait_send()
            for m in range(4):
                self.h_sib(w, s, m).wait_send()
        self.own_sib(w).wait_send()

    def small_place(self, owner):
        return self.small_full.at[pl.ds(pl.multiple_of(owner * ROWS, ROWS), ROWS), :]

    def small_copies(self):
        w = len(self.shapes)
        far = [self.copy((w, s, 0), self.small_shard, self.small_place(self.f), self.r, self.along(s)) for s in (1, 2, 3)]
        own = self.copy((w, 0, 0), self.small_shard, self.small_place(self.f), self.r, self.sib)
        here = pltpu.make_async_copy(self.small_shard, self.small_place(self.f), self.send.at[w, 0, 1])
        sib = []
        for s in (1, 2, 3):
            place = self.small_place(self.along(4 - s))
            sib.append(self.copy((w, s, 1), place, place, self.r, self.sib))
        return far, own, here, sib


class Reduce(Links):
    SLOTS = 8

    def __init__(self, shapes, grads, outs, bufs, send, recv):
        super().__init__(send, recv)
        self.shapes, self.grads, self.outs, self.bufs = shapes, grads, outs, bufs

    @staticmethod
    def scratch(shapes):
        out = []
        for rows, cols in shapes:
            out += [
                pltpu.VMEM((4, rows, cols), BF16),
                pltpu.VMEM((4, rows, cols), BF16),
                pltpu.VMEM((2, rows, cols // 2), BF16),
                pltpu.VMEM((2, rows // 2, cols), BF16),
                pltpu.VMEM((4, rows // 2, cols // 2), BF16),
                pltpu.VMEM((3, rows // 2, cols // 2), BF16),
                pltpu.VMEM((rows // 2, cols // 2), BF16),
            ]
        return out

    def shard(self, w, s, core):
        rows = self.shapes[w][0]
        at = pl.multiple_of((((self.z + s) % 4) * 2 + core) * rows, 16)
        return self.grads[w].at[pl.ds(at, rows), :]

    def half_rows(self, w, bit):
        h = self.shapes[w][0] // 2
        return pl.ds(pl.multiple_of(bit * h, 16), h)

    def half_cols(self, w, bit):
        h = self.shapes[w][1] // 2
        return pl.ds(pl.multiple_of(bit * h, 128), h)

    def core_copy(self, w, s):
        return self.copy((w, s, 0), self.shard(w, s, 1 - self.c), self.bufs[w][1].at[s], self.r, self.sib)

    def core_load(self, w, s):
        return pltpu.make_async_copy(self.shard(w, s, self.c), self.bufs[w][0].at[s], self.send.at[w, s, 7])

    def start(self, w, s):
        self.core_copy(w, s).start()
        self.core_load(w, s).start()

    def x_first(self, s):
        return s % 2 == 1

    def first_copy(self, w, s):
        own, hx, hy = self.bufs[w][0], self.bufs[w][2], self.bufs[w][3]
        if self.x_first(s):
            return self.copy((w, s, 1), own.at[s, :, self.half_cols(w, 1 - self.x)], hx.at[s // 2], self.xr, self.f)
        return self.copy((w, s, 1), own.at[s, self.half_rows(w, 1 - self.y), :], hy.at[s // 2], self.yr, self.f)

    def add_core(self, w, s):
        self.core_copy(w, s).wait_recv()
        self.core_load(w, s).wait()
        own, got = self.bufs[w][0], self.bufs[w][1]
        own[s] = own[s] + got[s]
        self.first_copy(w, s).start()

    def second_copy(self, w, s):
        own, quarter = self.bufs[w][0], self.bufs[w][4]
        if self.x_first(s):
            src = own.at[s, self.half_rows(w, 1 - self.y), self.half_cols(w, self.x)]
            return self.copy((w, s, 2), src, quarter.at[s], self.yr, self.f)
        src = own.at[s, self.half_rows(w, self.y), self.half_cols(w, 1 - self.x)]
        return self.copy((w, s, 2), src, quarter.at[s], self.xr, self.f)

    def add_first(self, w, s):
        self.first_copy(w, s).wait_recv()
        own, hx, hy = self.bufs[w][0], self.bufs[w][2], self.bufs[w][3]
        if self.x_first(s):
            at = (s, slice(None), self.half_cols(w, self.x))
            own[at] = own[at] + hx[s // 2]
        else:
            at = (s, self.half_rows(w, self.y), slice(None))
            own[at] = own[at] + hy[s // 2]
        self.second_copy(w, s).start()

    def far_copy(self, w, s):
        own, far = self.bufs[w][0], self.bufs[w][5]
        src = own.at[s, self.half_rows(w, self.y), self.half_cols(w, self.x)]
        return self.copy((w, s, 3), src, far.at[s - 1], self.r, self.along(s))

    def add_second(self, w, s):
        self.second_copy(w, s).wait_recv()
        own, quarter = self.bufs[w][0], self.bufs[w][4]
        at = (s, self.half_rows(w, self.y), self.half_cols(w, self.x))
        own[at] = own[at] + quarter[s]
        if s > 0:
            self.far_copy(w, s).start()

    def place(self, w, q, part=None):
        rows, cols = self.shapes[w]
        h = rows // 2
        r0, n = (q // 2) * h, h
        if part is not None:
            n = h // 32 * 16 if part == 0 else h - h // 32 * 16
            r0 = r0 if part == 0 else r0 + h // 32 * 16
        return self.outs[w].at[pl.ds(pl.multiple_of(r0, 16), n), self.half_cols(w, q % 2)]

    def out_local(self, w):
        return pltpu.make_async_copy(self.bufs[w][6], self.place(w, self.r), self.send.at[w, 0, 3])

    def out_x(self, w):
        return self.copy((w, 0, 4), self.bufs[w][6], self.place(w, self.r), self.xr, self.f)

    def out_y(self, w):
        return self.copy((w, 0, 5), self.bufs[w][6], self.place(w, self.r), self.yr, self.f)

    def out_dy(self, w):
        p = self.place(w, flip(self.r, 1), 0)
        return self.copy((w, 1, 4), p, p, self.yr, self.f)

    def out_dx(self, w):
        p = self.place(w, flip(self.r, 2), 1)
        return self.copy((w, 1, 5), p, p, self.xr, self.f)

    def total(self, w):
        own, far, done = self.bufs[w][0], self.bufs[w][5], self.bufs[w][6]
        for s in (1, 2, 3):
            self.far_copy(w, s).wait_recv()
        at = (0, self.half_rows(w, self.y), self.half_cols(w, self.x))
        done[...] = (own[at].astype(F32) + far[0].astype(F32) + far[1].astype(F32) + far[2].astype(F32)).astype(BF16)
        self.out_x(w).start()
        self.out_y(w).start()
        self.out_local(w).start()

    def relay(self, w):
        self.out_x(w).wait_recv()
        self.out_dy(w).start()
        self.out_y(w).wait_recv()
        self.out_dx(w).start()

    def finish(self, w):
        for s in range(4):
            self.core_copy(w, s).wait_send()
            self.first_copy(w, s).wait_send()
            self.second_copy(w, s).wait_send()
            if s:
                self.far_copy(w, s).wait_send()
        self.out_local(w).wait()
        self.out_x(w).wait_send()
        self.out_y(w).wait_send()
        for d in (self.out_dy(w), self.out_dx(w)):
            d.wait_send()
            d.wait_recv()


def plan(red, n, order):
    items = [(w, s) for w in order for s in (1, 2, 3, 0)]
    ticks = []
    m = len(items)
    for k in range(m + 4):
        acts = []
        if k < m:
            acts.append(functools.partial(red.add_core, *items[k]))
        if 0 <= k - 2 < m:
            acts.append(functools.partial(red.add_first, *items[k - 2]))
        if 0 <= k - 4 < m:
            w, s = items[k - 4]
            acts.append(functools.partial(red.add_second, w, s))
            if s == 0:
                j = order.index(w)
                if j > 0:
                    acts.append(functools.partial(red.total, order[j - 1]))
                if j > 1:
                    acts.append(functools.partial(red.relay, order[j - 2]))
        ticks.append(acts)
    tail = [functools.partial(red.total, order[-1])]
    if n > 1:
        tail.append(functools.partial(red.relay, order[-2]))
    tail.append(functools.partial(red.relay, order[-1]))
    ticks.append(tail)
    ticks.append([functools.partial(red.finish, w) for w in order])
    return items, ticks


def spread_rows(small, row, step, count, unit):
    width = count * unit
    lane = lax.broadcasted_iota(jnp.int32, (8, width), 1)
    total = jnp.zeros((8, width), F32)
    for k in range(count):
        one = jnp.broadcast_to(small[row[k] : row[k] + 1, :], (8, LANE))
        wide = jnp.concatenate([one, jnp.zeros((8, width - LANE), F32)], 1)
        wide = jnp.where(lane < unit, wide, 0.0)
        total = total + (pltpu.roll(wide, k * unit, 1) if k else wide)
    return total[0:1]


def fill_mask(mask_ref, ord_ref, limit, s, seq_len, turned):
    blocks = seq_len // LANE
    own = ord_ref[pl.ds(s, 1), :].astype(F32)
    cols = jnp.broadcast_to(own, (LANE, seq_len)).T
    for rb in range(blocks):
        col = cols[rb * LANE : (rb + 1) * LANE, :]
        rank = jnp.concatenate([col] * blocks, 1)
        place = lax.broadcasted_iota(jnp.int32, (LANE, seq_len), 0 if turned else 1)
        if turned:
            place = place + rb * LANE
        order = (rank <= own) if turned else (own <= rank)
        ok = (place < limit) & ((place == 0) | order)
        mask_ref[s, rb * LANE : (rb + 1) * LANE, :] = jnp.where(ok, 0.0, MASKED)


def fill_near(near_ref, small, onehot_ref):
    near_ref[...] = lax.dot_general(small, onehot_ref[...], (((0,), (0,)), ((), ())), preferred_element_type=F32) * LOG2E


def attention_step(hp, s, proj, mask_ref, near_ref, put_out, put_total):
    query_c, keys, value, query_g = proj
    seq_len = keys.shape[0]
    blocks = seq_len // LANE
    values = jnp.concatenate([value, jnp.ones((seq_len, LANE), BF16)], 1)
    lane = lax.broadcasted_iota(jnp.int32, (seq_len, LANE), 1)
    diag_r = lax.broadcasted_iota(jnp.int32, (LANE, LANE), 0)
    diag_c = lax.broadcasted_iota(jnp.int32, (LANE, LANE), 1)
    outs = [[], []]
    totals = [jnp.zeros((seq_len, LANE), F32), jnp.zeros((seq_len, LANE), F32)]
    for t in range(2):
        head = hp * 2 + t
        sel = head_lanes((seq_len, LANE), t)
        head_row = near_ref[pl.ds(head, 1), :]
        near = skewed(head_row[:, :NEAR], 3 * LANE)
        bias = tile_bias(near, head_row[:, NEAR : NEAR + 1], head_row[:, NEAR + 1 : NEAR + 2], seq_len, -1)
        for stream in range(2):
            query = jnp.where(sel, query_g if stream else query_c, jnp.zeros((), BF16))
            raw = nt(query, keys)
            probs = []
            maxes = []
            for rb in range(blocks):
                part = raw[rb * LANE : (rb + 1) * LANE, :] + (bias[rb] + mask_ref[s, rb * LANE : (rb + 1) * LANE, :])
                if stream == 1:
                    hit = diag_r == diag_c
                    if rb == 0:
                        hit = hit & (diag_c != 0)
                    pieces = []
                    if rb > 0:
                        pieces.append(part[:, : rb * LANE])
                    pieces.append(jnp.where(hit, MASKED, part[:, rb * LANE : (rb + 1) * LANE]))
                    if rb < blocks - 1:
                        pieces.append(part[:, (rb + 1) * LANE :])
                    part = jnp.concatenate(pieces, 1)
                top = jnp.max(part, 1, keepdims=True)
                probs.append(jnp.exp2(part - top).astype(BF16))
                maxes.append(jnp.broadcast_to(top, (LANE, LANE)))
            mixed = nn(jnp.concatenate(probs, 0), values)
            total = mixed[:, LANE:]
            outs[stream].append(mixed[:, :LANE] / total)
            log_total = jnp.concatenate(maxes, 0) + jnp.log2(total)
            hi = log_total.astype(BF16).astype(F32)
            totals[stream] = jnp.where(lane == head, -hi, jnp.where(lane == head + HEAD, hi - log_total, totals[stream]))
    first = head_lanes((seq_len, LANE), 0)
    mine = (lane == hp * 2) | (lane == hp * 2 + 1) | (lane == hp * 2 + HEAD) | (lane == hp * 2 + 1 + HEAD)
    for stream in range(2):
        put_out(stream, jnp.where(first, outs[stream][0], outs[stream][1]).astype(BF16))
        put_total(stream, totals[stream].astype(BF16), mine)


def forward_kernel(shapes, linked, len_ref, content_ref, query_ref, ord_ref, onehot_ref, *refs):
    n = len(shapes)
    if linked:
        shards, small_shard, refs = refs[:n], refs[n], refs[n + 1 :]
        full_refs, refs = refs[: n - 1], refs[n - 1 :]
        joined_out, small_out, refs = refs[0], refs[1], refs[2:]
    else:
        joined_in, small_in, refs = refs[0], refs[1], refs[2:]
    mixed_ref, total_ref, proj_out, joined_ref, small_ref, proj_ref, mask_ref, near_ref, own_sem = refs[:9]
    hp = pl.program_id(0)
    s = pl.program_id(1)
    step = hp * pl.num_programs(1) + s
    steps = (HEADS // 2) * total_ref.shape[1]
    seqs = total_ref.shape[1]
    seq_len = total_ref.shape[2]
    row_count, width = content_ref.shape
    if linked:
        send, recv = refs[9:]
        net = Gather(shapes, shards, (joined_ref,) + tuple(full_refs), send, recv)
        net.small_shard, net.small_full = small_shard, small_ref
    proj_copy = pltpu.make_async_copy(proj_ref, proj_out, own_sem.at[0])

    @pl.when(step == 0)
    def _():
        if linked:
            net.barrier()
            far, own, here, sib = net.small_copies()
            for d in far + [own, here]:
                d.start()
            for w in range(n):
                net.start(w)
            for s0 in range(seqs):
                fill_mask(mask_ref, ord_ref, len_ref[s0], s0, seq_len, False)
            for d, e in zip(far, sib):
                d.wait_recv()
                e.start()
            for k in (1, 2, 3):
                net.relay_z(0, k)
            for k in (1, 2, 3):
                net.relay_xy(0, k)
            for k in (1, 2, 3):
                net.relay_z(1, k)
            for k in (1, 2, 3):
                net.relay_diag(0, k)
            for k in (1, 2, 3):
                net.relay_z(2, k)
            for d in far:
                d.wait_send()
            for d in [own] + sib:
                d.wait_send()
                d.wait_recv()
            here.wait()
            net.arrive(0)
            pltpu.make_async_copy(joined_ref, joined_out, own_sem.at[1]).start()
            pltpu.make_async_copy(small_ref, small_out, own_sem.at[2]).start()
        else:
            fetch = (pltpu.make_async_copy(joined_in, joined_ref, own_sem.at[1]), pltpu.make_async_copy(small_in, small_ref, own_sem.at[2]))
            for d in fetch:
                d.start()
            for s0 in range(seqs):
                fill_mask(mask_ref, ord_ref, len_ref[s0], s0, seq_len, False)
            for d in fetch:
                d.wait()
        fill_near(near_ref, small_ref[...], onehot_ref)
        small = small_ref[...].astype(F32)
        shards_all = small.shape[0] // ROWS
        unit = width // shards_all
        half = shards_all // 2
        shift_q = spread_rows(small, [k // 2 * ROWS + k % 2 for k in range(2 * half)], 0, 2 * half, unit)
        shift_v = spread_rows(small, [(half + k // 2) * ROWS + k % 2 for k in range(2 * half)], 0, 2 * half, unit)
        scale = LOG2E / math.sqrt(HEAD)
        chunk = 256

        @pl.loop(0, row_count // chunk)
        def _(i):
            rows = pl.ds(pl.multiple_of(i * chunk, chunk), chunk)
            rows_c = content_ref[rows, :]
            proj_ref[rows, 0:width] = ((nn(rows_c, joined_ref[:, 0:width]) + shift_q) * scale).astype(BF16)
            proj_ref[rows, width : 2 * width] = nn(rows_c, joined_ref[:, width : 2 * width]).astype(BF16)
            proj_ref[rows, 2 * width : 3 * width] = (nn(rows_c, joined_ref[:, 2 * width : 3 * width]) + shift_v).astype(BF16)
            proj_ref[rows, 3 * width : 4 * width] = ((nn(query_ref[rows, :], joined_ref[:, 0:width]) + shift_q) * scale).astype(BF16)

        proj_copy.start()

    if linked:
        agenda = {
            1: [(net.relay_xy, 1, (1, 2, 3))],
            3: [(net.relay_z, 3, (1, 2, 3))],
            4: [(net.relay_xy, 2, (1,))],
            5: [(net.relay_xy, 2, (2,)), (net.relay_diag, 1, (1, 2, 3))],
            6: [(net.relay_xy, 2, (3,))],
            8: [(net.relay_diag, 2, (1, 2)), (net.relay_xy, 3, (1,))],
            9: [(net.relay_diag, 2, (3,)), (net.relay_xy, 3, (2,))],
            10: [(net.relay_xy, 3, (3,))],
        }
        for at, acts in agenda.items():

            @pl.when(step == min(at, steps - 1))
            def _():
                for act, w, ks in acts:
                    for k in ks:
                        act(w, k)

    here_rows = pl.ds(pl.multiple_of(s * seq_len, seq_len), seq_len)
    column = lambda k: pl.ds(pl.multiple_of(k * width + hp * LANE, LANE), LANE)
    proj = [proj_ref[here_rows, column(k)] for k in range(4)]

    def put_out(stream, value):
        mixed_ref[stream] = value

    def put_total(stream, value, mine):
        @pl.when(hp == 0)
        def _():
            total_ref[stream, s] = value

        @pl.when(hp > 0)
        def _():
            total_ref[stream, s] = jnp.where(mine, value, total_ref[stream, s])

    attention_step(hp, s, proj, mask_ref, near_ref, put_out, put_total)

    @pl.when(step == steps - 1)
    def _():
        proj_copy.wait()
        if linked:
            pltpu.make_async_copy(joined_ref, joined_out, own_sem.at[1]).wait()
            pltpu.make_async_copy(small_ref, small_out, own_sem.at[2]).wait()
            for k in (1, 2, 3):
                net.relay_diag(3, k)
            for w in range(n):
                if w:
                    net.arrive(w)
                net.drain(w)


def forward_attention(linked, content_rows, query_rows, lengths, order, weights, small):
    row_count, width = content_rows.shape
    seqs, seq_len = order.shape
    pairs = width // LANE
    shards = 8 if linked else small.shape[0] // ROWS
    onehot = table_onehot(-1, shards)
    shapes = [w.shape for w in weights] if linked else []
    n = len(shapes)
    anywhere = pl.BlockSpec(memory_space=pl.ANY)
    inside = pl.BlockSpec(memory_space=pltpu.VMEM)
    block3 = pl.BlockSpec((2, seq_len, LANE), lambda h, s: (0, s, h))
    joined_shape = (width, 3 * width)
    small_shape = (shards * ROWS, LANE)
    out_specs, out_shape = [], []
    if linked:
        out_specs += [anywhere] * (n + 1)
        out_shape += [jax.ShapeDtypeStruct((8 * a, b), BF16) for a, b in shapes[1:]]
        out_shape += [jax.ShapeDtypeStruct(joined_shape, BF16), jax.ShapeDtypeStruct(small_shape, BF16)]
    out_specs += [block3, pl.BlockSpec((2, seqs, seq_len, LANE), lambda h, s: (0, 0, 0, 0)), anywhere]
    out_shape += [
        jax.ShapeDtypeStruct((2, row_count, width), BF16),
        jax.ShapeDtypeStruct((2, seqs, seq_len, LANE), BF16),
        jax.ShapeDtypeStruct((row_count, 4 * width), BF16),
    ]
    scratch = [
        pltpu.VMEM(joined_shape, BF16),
        pltpu.VMEM(small_shape, BF16),
        pltpu.VMEM((row_count, 4 * width), BF16),
        pltpu.VMEM((seqs, seq_len, seq_len), F32),
        pltpu.VMEM((LANE, NEAR + LANE), F32),
        pltpu.SemaphoreType.DMA((3,)),
    ]
    if linked:
        scratch += [pltpu.SemaphoreType.DMA((n + 1, 4, Gather.SLOTS)), pltpu.SemaphoreType.DMA((n + 1, 4, Gather.SLOTS))]
    flops = 2 * row_count * width * 4 * width + 8 * row_count * seq_len * width
    return pl.pallas_call(
        functools.partial(forward_kernel, shapes, linked),
        grid=(pairs, seqs),
        in_specs=[pl.BlockSpec(memory_space=pltpu.SMEM), inside, inside, inside, inside] + [anywhere] * (n + 1 if linked else 2),
        out_specs=out_specs,
        out_shape=out_shape,
        scratch_shapes=scratch,
        cost_estimate=pl.CostEstimate(flops=flops, bytes_accessed=30 * 2**20, transcendentals=4 * row_count * seq_len * HEADS),
        compiler_params=pltpu.CompilerParams(
            dimension_semantics=("arbitrary", "arbitrary"), vmem_limit_bytes=VMEM_BYTES,
            **(dict(collective_id=0, has_side_effects=True) if linked else {})),
        name="attention_forward",
    )(lengths, content_rows, query_rows, order, onehot, *(list(weights) + [small]))


def backward_kernel(shapes, linked, len_ref, q_ref, k_ref, v_ref, g_ref, dc_ref, dg_ref, oc_ref, og_ref, tot_ref, ord_ref, small_ref, onehot_ref, *refs):
    n = len(shapes)
    grads, refs = refs[:n], refs[n:]
    outs, refs = refs[:n], refs[n:]
    grad_ref, lows_ref, sums_ref, mask_ref, acc_ref, near_ref = refs[:6]
    refs = refs[6:]
    hp = pl.program_id(0)
    s = pl.program_id(1)
    last = pl.num_programs(1) - 1
    step = hp * pl.num_programs(1) + s
    seq_len = q_ref.shape[0]
    blocks = seq_len // LANE
    half = seq_len // 2
    steps = (HEADS // 2) * ord_ref.shape[0]
    if linked:
        bufs = [refs[7 * w : 7 * w + 7] for w in range(n)]
        send, recv = refs[7 * n :]
        net = Reduce(shapes, grads, outs, bufs, send, recv)
        items, ticks = plan(net, n, list(range(n)))

        @pl.when(step == 0)
        def _():
            net.barrier()
            for w, k in items:
                net.start(w, k)

        tail = ticks[-2:]
        ticks = ticks[:-2]
        for at in range(1, steps):
            acts = [a for i, t in enumerate(ticks) if 1 + i * (steps - 1) // len(ticks) == at for a in t]

            @pl.when(step == at)
            def _():
                for act in acts:
                    act()

    @pl.when(hp == 0)
    def _():
        fill_mask(mask_ref, ord_ref, len_ref[s], s, seq_len, True)

    @pl.when(step == 0)
    def _():
        fill_near(near_ref, small_ref[...], onehot_ref)

    lane = lax.broadcasted_iota(jnp.int32, (seq_len, LANE), 1)
    ones = jnp.ones((seq_len, LANE), BF16)
    zero = jnp.zeros((), BF16)
    keys = k_ref[...]
    keys_wide = jnp.concatenate([keys, ones], 1)
    values_wide = jnp.concatenate([v_ref[...], ones], 1)
    keys_turned = keys.astype(F32).T.astype(BF16)
    lane_r = lax.broadcasted_iota(jnp.int32, (LANE, LANE), 0)
    lane_c = lax.broadcasted_iota(jnp.int32, (LANE, LANE), 1)
    pick = (lane_r // HEAD == lane_c).astype(BF16)
    grad_keys = None
    grad_values = None
    grad_query = [[], []]
    streams = []
    for src, grad, out, tot in ((q_ref, dc_ref, oc_ref, tot_ref[0, 0]), (g_ref, dg_ref, og_ref, tot_ref[1, 0])):
        g = grad[...]
        delta = nn((g.astype(F32) * out[...].astype(F32)).astype(BF16), pick)
        streams.append((src[...], g, -delta, tot))
    for t in range(2):
        head = hp * 2 + t
        sel = head_lanes((seq_len, LANE), t)
        head_row = near_ref[pl.ds(head, 1), :]
        near = skewed(head_row[:, :NEAR], 3 * LANE)
        bias = tile_bias(near, head_row[:, NEAR : NEAR + 1], head_row[:, NEAR + 1 : NEAR + 2], seq_len, 1)
        for c0 in range(0, seq_len, half):
            both = None
            for stream in range(2):
                q, g, delta, tot = streams[stream]
                q = jnp.where(sel, q, zero)[c0 : c0 + half]
                g = jnp.where(sel, g, zero)[c0 : c0 + half]
                d = delta[c0 : c0 + half]
                ln = lane[c0 : c0 + half]
                tt = jnp.where((ln == head) | (ln == head + HEAD), tot[c0 : c0 + half], zero)
                dd = jnp.where(ln == t, d, 0.0)
                dhi = dd.astype(BF16)
                dlo = pltpu.roll(dd - dhi.astype(F32), HEAD, 1).astype(BF16)
                raw = nt(keys_wide, jnp.concatenate([q, tt], 1))
                dpr = nt(values_wide, jnp.concatenate([g, dhi + dlo], 1))
                probs, grads = [], []
                for rb in range(blocks):
                    sl = slice(rb * LANE, (rb + 1) * LANE)
                    part = raw[sl] + (bias[rb][:, c0 : c0 + half] + mask_ref[s, sl, c0 : c0 + half])
                    r0 = rb * LANE
                    if stream == 1 and c0 <= r0 < c0 + half:
                        hit = lane_r == lane_c
                        if rb == 0:
                            hit = hit & (lane_r != 0)
                        x0 = r0 - c0
                        diag = jnp.where(hit, MASKED, part[:, x0 : x0 + LANE])
                        pieces = []
                        if x0 > 0:
                            pieces.append(part[:, :x0])
                        pieces.append(diag)
                        if x0 + LANE < half:
                            pieces.append(part[:, x0 + LANE :])
                        part = jnp.concatenate(pieces, 1)
                    p = jnp.exp2(part)
                    probs.append(p.astype(BF16))
                    grads.append(p * dpr[sl])
                low = [x.astype(BF16) for x in grads]
                prob = jnp.concatenate(probs, 0)
                gl = jnp.concatenate(low, 0)
                gv = nn(prob, g)
                gk = nn(gl, q)
                grad_values = gv if grad_values is None else grad_values + gv
                grad_keys = gk if grad_keys is None else grad_keys + gk
                grad_query[stream].append(nn(keys_turned[t * HEAD : (t + 1) * HEAD], gl))
                both = grads if both is None else [a + b for a, b in zip(both, grads)]
            sums = {}
            for rb in range(blocks):
                for cb in range(half // LANE):
                    e = cb + c0 // LANE - rb
                    e = max(-2, min(2, e))
                    x = both[rb][:, cb * LANE : (cb + 1) * LANE]
                    sums[e] = x if e not in sums else sums[e] + x
            for e, x in sums.items():
                lanes = slice((e + 2) * LANE, (e + 3) * LANE)
                fresh = c0 == 0
                if fresh:
                    @pl.when(s == 0)
                    def _():
                        acc_ref[t, :, lanes] = x

                    @pl.when(s > 0)
                    def _():
                        acc_ref[t, :, lanes] = acc_ref[t, :, lanes] + x
                else:
                    acc_ref[t, :, lanes] = acc_ref[t, :, lanes] + x
            if c0 == 0:
                for e in range(-2, 3):
                    if e not in sums:
                        @pl.when(s == 0)
                        def _():
                            acc_ref[t, :, (e + 2) * LANE : (e + 3) * LANE] = jnp.zeros((LANE, LANE), F32)
    count = seq_len // half
    scale = 1.0 / math.sqrt(HEAD)

    @pl.when(s == 0)
    def _():
        lows_ref[...] = jnp.zeros_like(lows_ref)

    def put_grad(k, value):
        grad_ref[k] = value
        lows_ref[k] = lows_ref[k] + fold8(value.astype(F32))

    for stream, ref in ((0, 0), (1, 3)):
        pieces = grad_query[stream]
        top = jnp.concatenate(pieces[:count], 1)
        bot = jnp.concatenate(pieces[count:], 1)
        put_grad(ref, (jnp.concatenate([top, bot], 0) * scale).T.astype(BF16))
    put_grad(1, (grad_keys * LN2).astype(BF16))
    put_grad(2, grad_values.astype(BF16))

    @pl.when(s == last)
    def _():
        for t in range(2):
            near = jnp.concatenate([acc_ref[t, :, LANE : 4 * LANE], jnp.zeros((LANE, LANE), F32)], 1)
            mirror = (lane_r + lane_c == LANE - 1).astype(F32)
            flipped = lax.dot_general(mirror, near, (((1,), (0,)), ((), ())), precision=lax.Precision.HIGHEST, preferred_element_type=F32)
            turned = pltpu.roll(flipped, 0, 1, stride=1, stride_axis=0)
            row = jnp.sum(turned, 0, keepdims=True)
            below = jnp.sum(acc_ref[t, :, :LANE], 0, keepdims=True)
            above = jnp.sum(acc_ref[t, :, 4 * LANE :], 0, keepdims=True)
            sums_ref[pl.ds(hp * 2 + t, 1), :] = jnp.concatenate([row, below, above], 1)

    if linked:

        @pl.when(step == steps - 1)
        def _():
            for acts in tail:
                for act in acts:
                    act()


def backward_attention(linked, proj, grad_mixed, mixed, totals, lengths, order, small, weight_grads):
    rows, width = grad_mixed.shape
    seqs, seq_len = order.shape
    pairs = width // LANE
    onehot = table_onehot(1, small.shape[0] // ROWS)
    shapes = [(g.shape[0] // 8, g.shape[1]) for g in weight_grads]
    n = len(shapes)
    block = lambda off: pl.BlockSpec((seq_len, LANE), lambda h, s, off=off: (s, off + h))
    low = pl.BlockSpec((seq_len, LANE), lambda h, s: (seqs + s, h))
    anywhere = pl.BlockSpec(memory_space=pl.ANY)
    inside = pl.BlockSpec(memory_space=pltpu.VMEM)
    sums_shape = (2 * pairs, NEAR + 2 * LANE)
    scratch = [
        pltpu.VMEM((seqs, seq_len, seq_len), F32),
        pltpu.VMEM((2, LANE, 5 * LANE), F32),
        pltpu.VMEM((LANE, NEAR + LANE), F32),
    ]
    if linked:
        scratch += Reduce.scratch(shapes)
        scratch += [pltpu.SemaphoreType.DMA((n, 4, Reduce.SLOTS)), pltpu.SemaphoreType.DMA((n, 4, Reduce.SLOTS))]
    outs = pl.pallas_call(
        functools.partial(backward_kernel, shapes, linked),
        grid=(pairs, seqs),
        in_specs=[
            pl.BlockSpec(memory_space=pltpu.SMEM),
            block(0), block(pairs), block(2 * pairs), block(3 * pairs),
            block(0), low, block(0), low,
            pl.BlockSpec((2, 1, seq_len, LANE), lambda h, s: (0, s, 0, 0)),
            inside, inside, inside,
        ] + [anywhere] * n,
        out_specs=[anywhere] * n + [pl.BlockSpec((4, seq_len, LANE), lambda h, s: (0, s, h)), pl.BlockSpec((4, 8, LANE), lambda h, s: (0, 0, h)), pl.BlockSpec(sums_shape, lambda h, s: (0, 0))],
        out_shape=[jax.ShapeDtypeStruct(a, BF16) for a in shapes] + [jax.ShapeDtypeStruct((4, rows // 2, width), BF16), jax.ShapeDtypeStruct((4, 8, width), F32), jax.ShapeDtypeStruct(sums_shape, F32)],
        scratch_shapes=scratch,
        cost_estimate=pl.CostEstimate(flops=20 * rows * seq_len * width, bytes_accessed=30 * 2**20, transcendentals=2 * rows * seq_len * HEADS),
        compiler_params=pltpu.CompilerParams(
            dimension_semantics=("arbitrary", "arbitrary"), vmem_limit_bytes=VMEM_BYTES,
            **(dict(collective_id=1, has_side_effects=True) if linked else {})),
        name="attention_backward",
    )(lengths, proj, proj, proj, proj, grad_mixed, grad_mixed, mixed, mixed, totals, order, small, onehot, *weight_grads)
    sums = outs[n + 2]
    fold = np.zeros((sums_shape[1], BUCKETS), np.float32)
    fold[:NEAR] = np.roll(near_onehot(1).T, LANE - 1, 0)
    fold[NEAR : NEAR + LANE, BUCKETS - 1] = 1
    fold[NEAR + LANE :, BUCKETS // 2 - 1] = 1
    grad_table = jnp.dot(sums, jnp.asarray(fold), precision=lax.Precision.HIGHEST).T
    return outs[:n], outs[n], jnp.sum(outs[n + 1], 1), grad_table


def small_reduce(net, w, part, out, bufs):
    own, core, across_x, across_y, far = bufs
    rows = 4 * ROWS
    mine = part.at[pl.ds(pl.multiple_of(net.c * rows, rows), rows), :]
    other = part.at[pl.ds(pl.multiple_of((1 - net.c) * rows, rows), rows), :]
    load = pltpu.make_async_copy(mine, own.at[0], net.send.at[w, 0, 7])
    to_core = net.copy((w, 0, 0), other, core, net.r, net.sib)
    to_x = net.copy((w, 0, 1), own.at[1], across_x, net.xr, net.f)
    to_y = net.copy((w, 0, 2), own.at[2], across_y, net.yr, net.f)
    z_rows = lambda s: pl.ds(pl.multiple_of((net.z + s) % 4 * ROWS, ROWS), ROWS)
    to_far = [net.copy((w, s, 3), own.at[3, z_rows(s), :], far.at[s - 1], net.r, net.along(s)) for s in (1, 2, 3)]

    def first():
        load.start()
        to_core.start()

    def second():
        load.wait()
        to_core.wait_recv()
        own[1] = own[0] + core[...]
        to_x.start()

    def third():
        to_x.wait_recv()
        own[2] = own[1] + across_x[...]
        to_y.start()

    def fourth():
        to_y.wait_recv()
        own[3] = own[2] + across_y[...]
        for d in to_far:
            d.start()

    def fifth():
        for d in to_far:
            d.wait_recv()
        out[...] = own[3, z_rows(0), :] + far[0] + far[1] + far[2]
        for d in [to_core, to_x, to_y] + to_far:
            d.wait_send()

    return first, second, third, fourth, fifth


def input_grads(rows, grads, joined, branch):
    width = branch.shape[1]
    total = grads.shape[1]
    low = pl.ds(pl.multiple_of(total + rows.start, 256), rows.size)
    content = branch[rows, :].astype(F32)
    for k in range(3):
        content = content + nt(grads[k, rows, :], joined[:, k * width : (k + 1) * width])
    query = branch[low, :].astype(F32) + nt(grads[3, rows, :], joined[:, :width])
    return content.astype(BF16), query.astype(BF16)


def reduce_kernel(shapes, n, *refs):
    grads, small_part, sources, refs = refs[:n], refs[n], refs[n + 1 : n + 4], refs[n + 4 :]
    outs, small_out, stream_outs, refs = refs[:n], refs[n], refs[n + 1 : n + 3], refs[n + 3 :]
    held, results, own_sem, refs = refs[:3], refs[3:5], refs[5], refs[6:]
    bufs = [refs[7 * w : 7 * w + 7] for w in range(n)]
    small_bufs, (send, recv) = refs[7 * n : 7 * n + 5], refs[7 * n + 5 :]
    net = Reduce(shapes, grads, outs, bufs, send, recv)
    first, second, third, fourth, fifth = small_reduce(net, n, small_part, small_out, small_bufs)
    fetch = [pltpu.make_async_copy(a, b, own_sem.at[k]) for k, (a, b) in enumerate(zip(sources, held))]
    store = [pltpu.make_async_copy(a, b, own_sem.at[3 + k]) for k, (a, b) in enumerate(zip(results, stream_outs))]
    net.barrier()
    items, ticks = plan(net, n, list(range(n)))
    first()
    for w, k in items:
        net.start(w, k)
    for d in fetch:
        d.start()
    for d in fetch:
        d.wait()
    pieces = 4
    chunk = results[0].shape[0] // pieces
    extra = {1: second, 4: third, 6: fourth}
    for i, acts in enumerate(ticks):
        for act in acts:
            act()
        if i in extra:
            extra[i]()
        if 3 <= i < 3 + pieces:
            rows = pl.ds((i - 3) * chunk, chunk)
            content, query = input_grads(rows, *held)
            results[0][rows, :] = content
            results[1][rows, :] = query
        if i == 2 + pieces:
            for d in store:
                d.start()
    fifth()
    for d in store:
        d.wait()


def reduce_rest(weight_grads, small_grads, grads, joined, branch):
    n = len(weight_grads)
    shapes = [(g.shape[0] // 8, g.shape[1]) for g in weight_grads]
    anywhere = pl.BlockSpec(memory_space=pl.ANY)
    inside = pl.BlockSpec(memory_space=pltpu.VMEM)
    rows = 4 * ROWS
    stream = grads.shape[1:]
    scratch = [pltpu.VMEM(a.shape, BF16) for a in (grads, joined, branch)] + [pltpu.VMEM(stream, BF16)] * 2 + [pltpu.SemaphoreType.DMA((5,))]
    scratch += Reduce.scratch(shapes)
    scratch += [pltpu.VMEM((4, rows, LANE), F32)] + [pltpu.VMEM((rows, LANE), F32)] * 3 + [pltpu.VMEM((3, ROWS, LANE), F32)]
    scratch += [pltpu.SemaphoreType.DMA((n + 1, 4, Reduce.SLOTS)), pltpu.SemaphoreType.DMA((n + 1, 4, Reduce.SLOTS))]
    return pl.pallas_call(
        functools.partial(reduce_kernel, shapes, n),
        out_shape=[jax.ShapeDtypeStruct(a, BF16) for a in shapes] + [jax.ShapeDtypeStruct((ROWS, LANE), F32)] + [jax.ShapeDtypeStruct(stream, BF16)] * 2,
        in_specs=[anywhere] * (n + 4),
        out_specs=[anywhere] * n + [inside] + [anywhere] * 2,
        scratch_shapes=scratch,
        compiler_params=pltpu.CompilerParams(collective_id=2, has_side_effects=True, vmem_limit_bytes=VMEM_BYTES),
        name="reduce_rest",
    )(*weight_grads, small_grads, grads, joined, branch)


def prepare_kernel(unit, places, *refs):
    count = len(places)
    vectors, table, weights, refs = refs[:count], refs[count], refs[count + 1 : count + 5], refs[count + 5 :]
    small_ref, outs, wide_ref, part_ref = refs[0], refs[1:5], refs[5], refs[6]
    part_ref[...] = jnp.zeros_like(part_ref)
    lane = lax.broadcasted_iota(jnp.int32, (8, LANE), 1)
    for (row, chunks), ref in zip(places, vectors):
        if chunks == 1:
            part_ref[row : row + 1, :unit] = ref[...][None, :]
            continue
        size = chunks * unit
        wide = wide_ref.shape[1]
        wide_ref[0:1, :size] = ref[...][None, :]
        value = jnp.broadcast_to(wide_ref[0:1, :], (8, wide))
        for k in range(chunks):
            turned = pltpu.roll(value, wide - k * unit, 1) if k else value
            part_ref[row + k : row + k + 1, :] = jnp.where(lane < unit, turned[:, :LANE], 0.0)[0:1]
    part_ref[TABLE_ROW : TABLE_ROW + table.shape[0], : table.shape[1]] = table[...]
    small_ref[...] = part_ref[...].astype(BF16)
    for a, b in zip(weights, outs):
        b[...] = a[...].astype(BF16)


def prepare(vectors, table, weights, unit):
    places, row = [], 0
    for v in vectors:
        places.append((row, v.shape[0] // unit))
        row += v.shape[0] // unit
    widest = max(v.shape[0] for v in vectors)
    widest = (widest + LANE - 1) // LANE * LANE
    outs = pl.pallas_call(
        functools.partial(prepare_kernel, unit, places),
        out_shape=[jax.ShapeDtypeStruct((ROWS, LANE), BF16)] + [jax.ShapeDtypeStruct(w.shape, BF16) for w in weights],
        scratch_shapes=[pltpu.VMEM((8, widest), F32), pltpu.VMEM((ROWS, LANE), F32)],
        compiler_params=pltpu.CompilerParams(vmem_limit_bytes=VMEM_BYTES),
        name="prepare",
    )(*vectors, table, *weights)
    return outs[0], outs[1:]


ERF_P = 0.3275911 * 0.7071067811865476
ERF_A = (0.254829592 * 0.5, -0.284496736 * 0.5, 1.421413741 * 0.5, -1.453152027 * 0.5, 1.061405429 * 0.5)


def gelu_pair(z):
    bell = jnp.exp2(z * z * (-0.5 * LOG2E))
    t = 1.0 / (1.0 + ERF_P * jnp.abs(z))
    tail = ERF_A[4]
    for a in ERF_A[3::-1]:
        tail = tail * t + a
    tail = tail * t * bell
    share = jnp.where(z < 0.0, tail, 1.0 - tail)
    return z * share, share + z * bell * inv_root_tau


def norm_rows(summed):
    row_mean = jnp.mean(summed, -1, keepdims=True)
    centered = summed - row_mean
    inverse = lax.rsqrt(jnp.mean(centered * centered, -1, keepdims=True) + eps_norm)
    return centered * inverse, inverse


def norm_rows_back(scaled, normed, inverse):
    return inverse * (scaled - jnp.mean(scaled, -1, keepdims=True) - normed * jnp.mean(scaled * normed, -1, keepdims=True))


def fold8(value):
    rows, cols = value.shape
    return jnp.sum(value.reshape(rows // 8, 8, cols), 0)


def ffn_kernel(chunk, len_ref, mixed_ref, content_ref, query_ref, ccot_ref, qcot_ref, small_ref, wo_hbm, win_hbm, wout_hbm,
               cout_ref, qout_ref, hid_ref, dz_ref, first_ref, dffn_ref, dbranch_ref, dmixed_ref, sums_ref, wide_sums_ref,
               wo_ref, win_ref, wout_ref, vec_ref, shift_ref, slope_ref, acc_ref, wide_acc_ref, sem):
    i = pl.program_id(0)
    n = pl.num_programs(0)
    rows, width = mixed_ref.shape
    hidden = win_ref.shape[1]
    loads = [pltpu.make_async_copy(a, b, sem.at[k]) for k, (a, b) in enumerate(((wo_hbm, wo_ref), (win_hbm, win_ref), (wout_hbm, wout_ref)))]

    @pl.when(i == 0)
    def _():
        for d in loads:
            d.start()
        small = small_ref[...].astype(F32)
        shards = small.shape[0] // ROWS
        unit = width // shards
        for k in range(2, 8):
            vec_ref[k : k + 1, :] = spread_rows(small, [f * ROWS + k for f in range(shards)], 0, shards, unit)
        count = hidden // unit
        shift_ref[0:1, :] = spread_rows(small, [k // 4 * ROWS + 8 + k % 4 for k in range(count)], 0, count, unit)
        acc_ref[...] = jnp.zeros_like(acc_ref)
        wide_acc_ref[...] = jnp.zeros_like(wide_acc_ref)
        for d in loads:
            d.wait()

    first_stream = i < n // 2
    vec = lambda k: vec_ref[k : k + 1, :]

    def add_sum(k, value):
        acc_ref[k] = acc_ref[k] + fold8(value)

    residual = jnp.where(first_stream, content_ref[...], query_ref[...]).astype(F32)
    branch = nn(mixed_ref[...], wo_ref[...]) + vec(2)
    normed_one, inverse_one = norm_rows(residual + branch)
    first_low = (normed_one * vec(3) + vec(4)).astype(BF16)
    first_ref[...] = first_low
    for c in range(0, hidden, chunk):
        cols = slice(c, c + chunk)
        value, slope = gelu_pair(nn(first_low, win_ref[:, cols]) + shift_ref[0:1, cols])
        hid_ref[:, cols] = value.astype(BF16)
        slope_ref[:, cols] = slope.astype(BF16)
    ffn = nn(hid_ref[...], wout_ref[...]) + vec(5)
    normed_two, inverse_two = norm_rows(first_low.astype(F32) + ffn)
    final = (normed_two * vec(6) + vec(7)).astype(BF16)

    @pl.when(first_stream)
    def _():
        cout_ref[...] = final

    @pl.when(jnp.logical_not(first_stream))
    def _():
        qout_ref[...] = final

    per_stream = n // 2
    at = jnp.where(first_stream, i, i - per_stream) * rows
    seq_len = per_stream * rows // len_ref.shape[0]
    seq = at // seq_len
    place = at - seq * seq_len + lax.broadcasted_iota(jnp.int32, (rows, 1), 0)
    upstream = jnp.where(first_stream, ccot_ref[...], qcot_ref[...]).astype(F32)
    upstream = jnp.where(place < len_ref[seq], upstream, 0.0)
    add_sum(5, upstream * normed_two)
    add_sum(6, upstream)
    grad_two = norm_rows_back(upstream * vec(6), normed_two, inverse_two)
    grad_ffn = grad_two.astype(BF16)
    dffn_ref[...] = grad_ffn
    add_sum(4, grad_ffn.astype(F32))
    for c in range(0, hidden, chunk):
        cols = slice(c, c + chunk)
        grad = nt(grad_ffn, wout_ref[cols, :]) * slope_ref[:, cols].astype(F32)
        wide_acc_ref[:, cols] = wide_acc_ref[:, cols] + fold8(grad)
        dz_ref[:, cols] = grad.astype(BF16)
    grad_first = grad_two + nt(dz_ref[...], win_ref[...])
    add_sum(2, grad_first * normed_one)
    add_sum(3, grad_first)
    grad_branch = norm_rows_back(grad_first * vec(3), normed_one, inverse_one).astype(BF16)
    dbranch_ref[...] = grad_branch
    add_sum(1, grad_branch.astype(F32))
    dmixed_ref[...] = nt(grad_branch, wo_ref[...]).astype(BF16)

    @pl.when(i == n - 1)
    def _():
        for k in range(8):
            sums_ref[k : k + 1, :] = jnp.sum(acc_ref[k], 0, keepdims=True)
        wide_sums_ref[...] = jnp.sum(wide_acc_ref[...], 0, keepdims=True)


def ffn_stage(mixed, content_rows, query_rows, content_cot, query_cot, lengths, small, out_proj, in_proj, out_ffn, rows=256, chunk=768):
    total, width = mixed.shape
    hidden = in_proj.shape[1]
    n = total // rows
    half = n // 2
    anywhere = pl.BlockSpec(memory_space=pl.ANY)
    row_block = lambda cols: pl.BlockSpec((rows, cols), lambda i: (i, 0))
    low = pl.BlockSpec((rows, width), lambda i: (jnp.minimum(i, half - 1), 0))
    high = pl.BlockSpec((rows, width), lambda i: (jnp.maximum(i - half, 0), 0))
    whole = lambda shape: pl.BlockSpec(shape, lambda i: (0,) * len(shape))
    shape = jax.ShapeDtypeStruct
    return pl.pallas_call(
        functools.partial(ffn_kernel, chunk),
        grid=(n,),
        in_specs=[pl.BlockSpec(memory_space=pltpu.SMEM), row_block(width), low, high, low, high, whole(small.shape)] + [anywhere] * 3,
        out_specs=[low, high, row_block(hidden), row_block(hidden)] + [row_block(width)] * 4 + [whole((8, width)), whole((1, hidden))],
        out_shape=[shape((total // 2, width), BF16)] * 2 + [shape((total, hidden), BF16)] * 2 + [shape((total, width), BF16)] * 4
        + [shape((8, width), F32), shape((1, hidden), F32)],
        scratch_shapes=[
            pltpu.VMEM((width, width), BF16),
            pltpu.VMEM((width, hidden), BF16),
            pltpu.VMEM((hidden, width), BF16),
            pltpu.VMEM((8, width), F32),
            pltpu.VMEM((8, hidden), F32),
            pltpu.VMEM((rows, hidden), BF16),
            pltpu.VMEM((8, 8, width), F32),
            pltpu.VMEM((8, hidden), F32),
            pltpu.SemaphoreType.DMA((3,)),
        ],
        cost_estimate=pl.CostEstimate(flops=4 * total * width * (2 * hidden + width), bytes_accessed=60 * 2**20, transcendentals=2 * total * hidden),
        compiler_params=pltpu.CompilerParams(dimension_semantics=("arbitrary",), vmem_limit_bytes=VMEM_BYTES),
        name="ffn_stage",
    )(lengths, mixed, content_rows, query_rows, content_cot, query_cot, small, out_proj, in_proj, out_ffn)


def rows_inner(left_op, right_op):
    return lax.dot_general(
        left_op, right_op, (((0,), (0,)), ((), ())), preferred_element_type=jnp.float32
    )


def times_transpose(left_op, right_op):
    return lax.dot_general(
        left_op, right_op, (((1,), (1,)), ((), ())), preferred_element_type=jnp.float32
    )


def pack_small(groups, shards):
    rows = []
    for g in groups:
        g = g.reshape(shards, -1, g.shape[-1]) if g.ndim > 1 else g
        rows.append(g)
    wide = [jnp.pad(g, ((0, 0), (0, 0), (0, LANE - g.shape[2]))) for g in rows]
    joined = jnp.concatenate(wide, 1)
    joined = jnp.pad(joined, ((0, 0), (0, ROWS - joined.shape[1]), (0, 0)))
    return joined.reshape(shards * ROWS, LANE)


def on_device(axes, content_stream, query_stream, lengths, factor_order, qkv_weight, qv_bias, out_weight, out_bias, norm1_gain, norm1_bias, rel_table, ffn_in_weight, ffn_in_bias, ffn_out_weight, ffn_out_bias, norm2_gain, norm2_bias, content_cot, query_cot):
    linked = axes == (4, 8)
    shards = axes[1]
    seq_count, seq_len, width = content_stream.shape
    row_count = seq_count * seq_len
    unit = width // shards
    small_args = (qv_bias, out_bias, norm1_gain, norm1_bias, ffn_out_bias, norm2_gain, norm2_bias, ffn_in_bias)
    weights = (qkv_weight, out_weight, ffn_in_weight, ffn_out_weight)
    if linked:
        small, weights = prepare(small_args, rel_table, weights, unit)
    else:
        small = pack_small([p.reshape(1, -1, unit) for p in small_args] + [rel_table[None]], 1).astype(BF16)
        weights = [w.astype(BF16) for w in weights]
    content_rows = content_stream.reshape(row_count, width)
    query_rows = query_stream.reshape(row_count, width)
    if linked:
        out_proj, in_proj, out_ffn, joined_proj, small, mixed, totals, proj = forward_attention(
            True, content_rows, query_rows, lengths, factor_order, weights, small)
    else:
        gather = lambda a: lax.all_gather(a, "fsdp", axis=0, tiled=True)
        joined_proj, out_proj, in_proj, out_ffn = [gather(w) for w in weights]
        small = gather(small)
        mixed, totals, proj = forward_attention(False, content_rows, query_rows, lengths, factor_order, [joined_proj], small)
    mixed_rows = mixed.reshape(2 * row_count, width)
    flat_cot = lambda a: a.reshape(row_count, width)
    content_out, query_out, hidden_low, grad_hidden, first_low, grad_ffn, grad_branch, grad_mixed, sums, wide_sums = ffn_stage(
        mixed_rows, content_rows, query_rows, flat_cot(content_cot), flat_cot(query_cot), lengths, small, out_proj, in_proj, out_ffn)
    grad_out_ffn = rows_inner(hidden_low, grad_ffn).astype(BF16)
    grad_in_proj = rows_inner(first_low, grad_hidden).astype(BF16)
    grad_out_proj = rows_inner(mixed_rows, grad_branch).astype(BF16)
    ready = [grad_in_proj, grad_out_ffn, grad_out_proj] if linked else []
    early, grads, low_sums, grad_table = backward_attention(linked, proj, grad_mixed, mixed_rows, totals, lengths, factor_order, small, ready)
    grad_q = rows_inner(content_rows, grads[0]) + rows_inner(query_rows, grads[3])
    grad_joined = jnp.concatenate([grad_q, rows_inner(content_rows, grads[1]), rows_inner(content_rows, grads[2])], 1).astype(BF16)
    grad_proj_shift = jnp.concatenate([low_sums[0] + low_sums[3], low_sums[2]])
    rows_of = lambda g: g.reshape(shards, -1, unit) if g.ndim == 1 or g.shape[0] == 1 else g.reshape(-1, shards, unit).transpose(1, 0, 2)
    packed = pack_small([rows_of(grad_proj_shift), rows_of(sums[1:7]), rows_of(wide_sums), grad_table.reshape(shards, -1, HEADS)], shards)
    if linked:
        packed = packed.reshape(4, 2, ROWS, LANE).transpose(1, 0, 2, 3).reshape(8 * ROWS, LANE)
        sum_joined, mine, content_grad_rows, query_grad_rows = reduce_rest([grad_joined], packed, grads, joined_proj, grad_branch)
        sum_in, sum_out, sum_proj = early
    else:
        scatter = lambda a: lax.psum(lax.psum_scatter(a, "fsdp", scatter_dimension=0, tiled=True), "rep")
        sum_joined, sum_in, sum_out, sum_proj = [scatter(a) for a in (grad_joined, grad_in_proj, grad_out_ffn, grad_out_proj)]
        mine = scatter(packed)
        content_grad_rows = grad_branch[:row_count].astype(F32) + (
            times_transpose(grads[0], joined_proj[:, :width])
            + times_transpose(grads[1], joined_proj[:, width : 2 * width])
            + times_transpose(grads[2], joined_proj[:, 2 * width :])
        )
        query_grad_rows = grad_branch[row_count:].astype(F32) + times_transpose(grads[3], joined_proj[:, :width])
    sum_joined, sum_in, sum_out, sum_proj = [a.astype(F32) for a in (sum_joined, sum_in, sum_out, sum_proj)]
    vec = lambda k: mine[k, :unit]
    block_shape = (seq_count, seq_len, width)
    return (
        content_out.reshape(block_shape),
        query_out.reshape(block_shape),
        content_grad_rows.reshape(block_shape).astype(BF16),
        query_grad_rows.reshape(block_shape).astype(BF16),
        sum_joined,
        mine[0:2, :unit].reshape(-1),
        sum_proj,
        vec(2),
        vec(3),
        vec(4),
        mine[TABLE_ROW : TABLE_ROW + rel_table.shape[0], :HEADS],
        sum_in,
        mine[8:12, :unit].reshape(-1),
        sum_out,
        vec(5),
        vec(6),
        vec(7),
    )


def solution(mesh):
    in_specs = (
        P(("rep", "fsdp"), None, None),
        P(("rep", "fsdp"), None, None),
        P(("rep", "fsdp")),
        P(("rep", "fsdp"), None),
        P("fsdp", None),
        P("fsdp"),
        P("fsdp", None),
        P("fsdp"),
        P("fsdp"),
        P("fsdp"),
        P("fsdp", None),
        P("fsdp", None),
        P("fsdp"),
        P("fsdp", None),
        P("fsdp"),
        P("fsdp"),
        P("fsdp"),
        P(("rep", "fsdp"), None, None),
        P(("rep", "fsdp"), None, None),
    )
    out_specs = (
        P(("rep", "fsdp"), None, None),
        P(("rep", "fsdp"), None, None),
        P(("rep", "fsdp"), None, None),
        P(("rep", "fsdp"), None, None),
        P("fsdp", None),
        P("fsdp"),
        P("fsdp", None),
        P("fsdp"),
        P("fsdp"),
        P("fsdp"),
        P("fsdp", None),
        P("fsdp", None),
        P("fsdp"),
        P("fsdp", None),
        P("fsdp"),
        P("fsdp"),
        P("fsdp"),
    )
    return jax.shard_map(
        functools.partial(on_device, tuple(mesh.shape[a] for a in mesh.axis_names)),
        mesh=mesh,
        in_specs=in_specs,
        out_specs=out_specs,
        check_vma=False,
    )
```

```python
import functools
import math

import jax
import jax.numpy as jnp
import numpy as np
from jax import lax
from jax.experimental import pallas as pl
from jax.experimental.pallas import tpu as pltpu
from jax.sharding import PartitionSpec as P

HEADS = 12
HEAD = 64
BUCKETS = 32
MAX_DIST = 128
LANE = 128
NEAR = 512
ROWS = 16
TABLE_ROW = 12
MASKED = -1e30
LOG2E = 1.4426950408889634
LN2 = 0.6931471805599453
F32 = jnp.float32
BF16 = jnp.bfloat16
MESH = pl.DeviceIdType.MESH
VMEM_BYTES = 60 * 2**20
eps_norm = 1e-05
inv_root_tau = 0.3989422804014327


def bucket_of(offset):
    half_count = BUCKETS // 2
    result = (offset < 0).astype(np.int64) * half_count
    distance = np.abs(offset)
    exact_count = half_count // 2
    fraction = np.log(np.maximum(distance, 1) / exact_count) / np.log(MAX_DIST / exact_count)
    beyond = exact_count + (fraction * (half_count - exact_count)).astype(np.int64)
    beyond = np.minimum(beyond, half_count - 1)
    result = result + np.where(distance < exact_count, distance, beyond)
    return result.astype(np.int32)


def nt(a, b):
    return lax.dot_general(a, b, (((1,), (1,)), ((), ())), preferred_element_type=F32)


def nn(a, b):
    return lax.dot_general(a, b, (((1,), (0,)), ((), ())), preferred_element_type=F32)


def signed_places():
    places = np.arange(NEAR)
    return np.where(places < NEAR - LANE, places, places - NEAR)


def near_onehot(sign):
    offset = sign * (signed_places() - LANE)
    return (bucket_of(offset)[None, :] == np.arange(BUCKETS)[:, None]).astype(np.float32)


def skewed(row, width):
    wide = jnp.broadcast_to(row, (LANE, NEAR))
    return pltpu.roll(wide, 0, 1, stride=1, stride_axis=0)[:, :width]


def tile_bias(near, far_pos, far_neg, seq_len, sign):
    blocks = seq_len // LANE
    rows = []
    for rb in range(blocks):
        parts = []
        for cb in range(blocks):
            e = cb - rb
            if abs(e) <= 1:
                parts.append(near[:, (e + 1) * LANE : (e + 2) * LANE])
            else:
                parts.append(jnp.broadcast_to(far_pos if e * sign > 0 else far_neg, (LANE, LANE)))
        rows.append(jnp.concatenate(parts, 1))
    return rows


def head_lanes(shape, t):
    lane = lax.broadcasted_iota(jnp.int32, shape, 1)
    return (lane >= t * HEAD) & (lane < (t + 1) * HEAD)


def flip(v, m):
    a, b = v // 2, v % 2
    if m & 2:
        a = 1 - a
    if m & 1:
        b = 1 - b
    return a * 2 + b


def table_onehot(sign, shards):
    per_shard = BUCKETS // shards
    result = np.zeros((shards * ROWS, NEAR + LANE), np.float32)
    near = near_onehot(sign)
    for bucket in range(BUCKETS):
        row = bucket // per_shard * ROWS + TABLE_ROW + bucket % per_shard
        result[row, :NEAR] = near[bucket]
        result[row, NEAR] = bucket == BUCKETS // 2 - 1
        result[row, NEAR + 1] = bucket == BUCKETS - 1
    return jnp.asarray(result, BF16)


class Links:
    def __init__(self, send, recv):
        self.send, self.recv = send, recv
        self.r = lax.axis_index("rep")
        self.f = lax.axis_index("fsdp")
        self.y, self.x = self.r // 2, self.r % 2
        self.z, self.c = self.f // 2, self.f % 2
        self.xr, self.yr = flip(self.r, 1), flip(self.r, 2)
        self.sib = self.z * 2 + 1 - self.c

    def along(self, s):
        return ((self.z + s) % 4) * 2 + self.c

    def copy(self, at, src, dst, rep, fsdp):
        return pltpu.make_async_remote_copy(
            src_ref=src, dst_ref=dst, send_sem=self.send.at[at], recv_sem=self.recv.at[at],
            device_id={"rep": rep, "fsdp": fsdp}, device_id_type=MESH)

    def barrier(self):
        sem = pltpu.get_barrier_semaphore()
        peers = [(self.r, self.along(s)) for s in (1, 2, 3)]
        peers += [(self.xr, self.f), (self.yr, self.f), (self.r, self.sib)]
        for rep, fsdp in peers:
            pl.semaphore_signal(sem, inc=1, device_id={"rep": rep, "fsdp": fsdp}, device_id_type=MESH)
        pl.semaphore_wait(sem, len(peers))


def quarter_of(ref, rows, cols, owner, q, part=None):
    pr, pc = rows // 2, cols // 2
    r0, c0 = owner * rows + (q // 2) * pr, (q % 2) * pc
    if part is not None:
        if pr % 32 == 0:
            r0, pr = r0 + part * (pr // 2), pr // 2
        else:
            first = (pc // LANE + 1) // 2 * LANE
            c0, pc = (c0, first) if part == 0 else (c0 + first, pc - first)
    return ref.at[pl.ds(pl.multiple_of(r0, 16), pr), pl.ds(pl.multiple_of(c0, LANE), pc)]


class Gather(Links):
    SLOTS = 12

    def __init__(self, shapes, shards, fulls, send, recv):
        super().__init__(send, recv)
        self.shapes, self.shards, self.fulls = shapes, shards, fulls

    def z_send(self, w, s):
        rows, cols = self.shapes[w]
        src = quarter_of(self.shards[w], rows, cols, 0, self.r)
        dst = quarter_of(self.fulls[w], rows, cols, self.f, self.r)
        return self.copy((w, s, 0), src, dst, self.r, self.along(s))

    def hop(self, w, s, slot, q, rep, fsdp, part=None):
        rows, cols = self.shapes[w]
        place = quarter_of(self.fulls[w], rows, cols, self.along(4 - s), q, part)
        return self.copy((w, s, slot), place, place, rep, fsdp)

    def own_place(self, w):
        rows = self.shapes[w][0]
        return self.fulls[w].at[pl.ds(pl.multiple_of(self.f * rows, 16), rows), :]

    def own_sib(self, w):
        return self.copy((w, 0, 0), self.shards[w], self.own_place(w), self.r, self.sib)

    def own_here(self, w):
        return pltpu.make_async_copy(self.shards[w], self.own_place(w), self.send.at[w, 0, 1])

    def h_x(self, w, s):
        return self.hop(w, s, 1, self.r, self.xr, self.f)

    def h_y(self, w, s):
        return self.hop(w, s, 2, self.r, self.yr, self.f)

    def h_dy(self, w, s):
        return self.hop(w, s, 3, self.xr, self.yr, self.f, 0)

    def h_dx(self, w, s):
        return self.hop(w, s, 4, self.yr, self.xr, self.f, 1)

    def h_sib(self, w, s, m):
        return self.hop(w, s, 5 + m, flip(self.r, m), self.r, self.sib)

    def start(self, w):
        for s in (1, 2, 3):
            self.z_send(w, s).start()
        self.own_sib(w).start()
        self.own_here(w).start()

    def relay_z(self, w, s):
        self.z_send(w, s).wait_recv()
        self.h_x(w, s).start()
        self.h_y(w, s).start()
        self.h_sib(w, s, 0).start()

    def relay_xy(self, w, s):
        self.h_x(w, s).wait_recv()
        self.h_dy(w, s).start()
        self.h_sib(w, s, 1).start()
        self.h_y(w, s).wait_recv()
        self.h_dx(w, s).start()
        self.h_sib(w, s, 2).start()

    def relay_diag(self, w, s):
        self.h_dy(w, s).wait_recv()
        self.h_dx(w, s).wait_recv()
        self.h_sib(w, s, 3).start()

    def arrive(self, w):
        for s in (1, 2, 3):
            for m in range(4):
                self.h_sib(w, s, m).wait_recv()
        self.own_sib(w).wait_recv()
        self.own_here(w).wait()

    def drain(self, w):
        for s in (1, 2, 3):
            for d in (self.z_send(w, s), self.h_x(w, s), self.h_y(w, s), self.h_dy(w, s), self.h_dx(w, s)):
                d.wait_send()
            for m in range(4):
                self.h_sib(w, s, m).wait_send()
        self.own_sib(w).wait_send()

    def small_place(self, owner):
        return self.small_full.at[pl.ds(pl.multiple_of(owner * ROWS, ROWS), ROWS), :]

    def small_copies(self):
        w = len(self.shapes)
        far = [self.copy((w, s, 0), self.small_shard, self.small_place(self.f), self.r, self.along(s)) for s in (1, 2, 3)]
        own = self.copy((w, 0, 0), self.small_shard, self.small_place(self.f), self.r, self.sib)
        here = pltpu.make_async_copy(self.small_shard, self.small_place(self.f), self.send.at[w, 0, 1])
        sib = []
        for s in (1, 2, 3):
            place = self.small_place(self.along(4 - s))
            sib.append(self.copy((w, s, 1), place, place, self.r, self.sib))
        return far, own, here, sib


def add_tiles(into, term):
    tile = 48 if into.shape[0] % 32 else 32

    @pl.loop(0, into.shape[0] // tile)
    def _(k):
        rows = pl.ds(pl.multiple_of(k * tile, 16), tile)
        into[rows, :] = into[rows, :] + term[rows, :]


class Reduce(Links):
    SLOTS = 8

    def __init__(self, shapes, grads, outs, bufs, send, recv):
        super().__init__(send, recv)
        self.shapes, self.grads, self.outs, self.bufs = shapes, grads, outs, bufs

    @staticmethod
    def scratch(shapes):
        out = []
        for rows, cols in shapes:
            out += [
                pltpu.VMEM((4, rows, cols), BF16),
                pltpu.VMEM((4, rows, cols), BF16),
                pltpu.VMEM((2, rows, cols // 2), BF16),
                pltpu.VMEM((2, rows // 2, cols), BF16),
                pltpu.VMEM((4, rows // 2, cols // 2), BF16),
                pltpu.VMEM((3, rows // 2, cols // 2), BF16),
                pltpu.VMEM((rows // 2, cols // 2), BF16),
            ]
        return out

    def shard(self, w, s, core):
        rows = self.shapes[w][0]
        at = pl.multiple_of((((self.z + s) % 4) * 2 + core) * rows, 16)
        return self.grads[w].at[pl.ds(at, rows), :]

    def half_rows(self, w, bit):
        h = self.shapes[w][0] // 2
        return pl.ds(pl.multiple_of(bit * h, 16), h)

    def half_cols(self, w, bit):
        h = self.shapes[w][1] // 2
        return pl.ds(pl.multiple_of(bit * h, 128), h)

    def core_copy(self, w, s):
        return self.copy((w, s, 0), self.shard(w, s, 1 - self.c), self.bufs[w][1].at[s], self.r, self.sib)

    def core_load(self, w, s):
        return pltpu.make_async_copy(self.shard(w, s, self.c), self.bufs[w][0].at[s], self.send.at[w, s, 7])

    def start(self, w, s):
        self.core_copy(w, s).start()
        self.core_load(w, s).start()

    def x_first(self, s):
        return s % 2 == 1

    def first_copy(self, w, s):
        own, hx, hy = self.bufs[w][0], self.bufs[w][2], self.bufs[w][3]
        if self.x_first(s):
            return self.copy((w, s, 1), own.at[s, :, self.half_cols(w, 1 - self.x)], hx.at[s // 2], self.xr, self.f)
        return self.copy((w, s, 1), own.at[s, self.half_rows(w, 1 - self.y), :], hy.at[s // 2], self.yr, self.f)

    def add_core(self, w, s):
        self.core_copy(w, s).wait_recv()
        self.core_load(w, s).wait()
        own, got = self.bufs[w][0], self.bufs[w][1]
        add_tiles(own.at[s], got.at[s])
        self.first_copy(w, s).start()

    def second_copy(self, w, s):
        own, quarter = self.bufs[w][0], self.bufs[w][4]
        if self.x_first(s):
            src = own.at[s, self.half_rows(w, 1 - self.y), self.half_cols(w, self.x)]
            return self.copy((w, s, 2), src, quarter.at[s], self.yr, self.f)
        src = own.at[s, self.half_rows(w, self.y), self.half_cols(w, 1 - self.x)]
        return self.copy((w, s, 2), src, quarter.at[s], self.xr, self.f)

    def add_first(self, w, s):
        self.first_copy(w, s).wait_recv()
        own, hx, hy = self.bufs[w][0], self.bufs[w][2], self.bufs[w][3]
        if self.x_first(s):
            at = (s, slice(None), self.half_cols(w, self.x))
            add_tiles(own.at[at], hx.at[s // 2])
        else:
            at = (s, self.half_rows(w, self.y), slice(None))
            add_tiles(own.at[at], hy.at[s // 2])
        self.second_copy(w, s).start()

    def far_copy(self, w, s):
        own, far = self.bufs[w][0], self.bufs[w][5]
        src = own.at[s, self.half_rows(w, self.y), self.half_cols(w, self.x)]
        return self.copy((w, s, 3), src, far.at[s - 1], self.r, self.along(s))

    def add_second(self, w, s):
        self.second_copy(w, s).wait_recv()
        own, quarter = self.bufs[w][0], self.bufs[w][4]
        at = (s, self.half_rows(w, self.y), self.half_cols(w, self.x))
        add_tiles(own.at[at], quarter.at[s])
        if s > 0:
            self.far_copy(w, s).start()

    def place(self, w, q, part=None):
        rows, cols = self.shapes[w]
        h = rows // 2
        r0, n = (q // 2) * h, h
        if part is not None:
            n = h // 32 * 16 if part == 0 else h - h // 32 * 16
            r0 = r0 if part == 0 else r0 + h // 32 * 16
        return self.outs[w].at[pl.ds(pl.multiple_of(r0, 16), n), self.half_cols(w, q % 2)]

    def out_local(self, w):
        return pltpu.make_async_copy(self.bufs[w][6], self.place(w, self.r), self.send.at[w, 0, 3])

    def out_x(self, w):
        return self.copy((w, 0, 4), self.bufs[w][6], self.place(w, self.r), self.xr, self.f)

    def out_y(self, w):
        return self.copy((w, 0, 5), self.bufs[w][6], self.place(w, self.r), self.yr, self.f)

    def out_dy(self, w):
        p = self.place(w, flip(self.r, 1), 0)
        return self.copy((w, 1, 4), p, p, self.yr, self.f)

    def out_dx(self, w):
        p = self.place(w, flip(self.r, 2), 1)
        return self.copy((w, 1, 5), p, p, self.xr, self.f)

    def total(self, w):
        own, far, done = self.bufs[w][0], self.bufs[w][5], self.bufs[w][6]
        for s in (1, 2, 3):
            self.far_copy(w, s).wait_recv()
        at = (0, self.half_rows(w, self.y), self.half_cols(w, self.x))
        done[...] = (own[at].astype(F32) + far[0].astype(F32) + far[1].astype(F32) + far[2].astype(F32)).astype(BF16)
        self.out_x(w).start()
        self.out_y(w).start()
        self.out_local(w).start()

    def relay(self, w):
        self.out_x(w).wait_recv()
        self.out_dy(w).start()
        self.out_y(w).wait_recv()
        self.out_dx(w).start()

    def finish(self, w):
        for s in range(4):
            self.core_copy(w, s).wait_send()
            self.first_copy(w, s).wait_send()
            self.second_copy(w, s).wait_send()
            if s:
                self.far_copy(w, s).wait_send()
        self.out_local(w).wait()
        self.out_x(w).wait_send()
        self.out_y(w).wait_send()
        for d in (self.out_dy(w), self.out_dx(w)):
            d.wait_send()
            d.wait_recv()


def plan(red, n, order):
    items = [(w, s) for w in order for s in (1, 2, 3, 0)]
    ticks = []
    m = len(items)
    for k in range(m + 4):
        acts = []
        if k < m:
            acts.append(functools.partial(red.add_core, *items[k]))
        if 0 <= k - 2 < m:
            acts.append(functools.partial(red.add_first, *items[k - 2]))
        if 0 <= k - 4 < m:
            w, s = items[k - 4]
            acts.append(functools.partial(red.add_second, w, s))
            if s == 0:
                j = order.index(w)
                if j > 0:
                    acts.append(functools.partial(red.total, order[j - 1]))
                if j > 1:
                    acts.append(functools.partial(red.relay, order[j - 2]))
        ticks.append(acts)
    tail = [functools.partial(red.total, order[-1])]
    if n > 1:
        tail.append(functools.partial(red.relay, order[-2]))
    tail.append(functools.partial(red.relay, order[-1]))
    ticks.append(tail)
    ticks.append([functools.partial(red.finish, w) for w in order])
    return items, ticks


def spread_rows(small, row, step, count, unit):
    width = count * unit
    lane = lax.broadcasted_iota(jnp.int32, (8, width), 1)
    total = jnp.zeros((8, width), F32)
    for k in range(count):
        one = jnp.broadcast_to(small[row[k] : row[k] + 1, :], (8, LANE))
        wide = jnp.concatenate([one, jnp.zeros((8, width - LANE), F32)], 1)
        wide = jnp.where(lane < unit, wide, 0.0)
        total = total + (pltpu.roll(wide, k * unit, 1) if k else wide)
    return total[0:1]


def fill_mask(mask_ref, ord_ref, limit, s, seq_len, turned):
    blocks = seq_len // LANE
    own = ord_ref[pl.ds(s, 1), :].astype(F32)
    cols = jnp.broadcast_to(own, (LANE, seq_len)).T
    for rb in range(blocks):
        col = cols[rb * LANE : (rb + 1) * LANE, :]
        rank = jnp.concatenate([col] * blocks, 1)
        place = lax.broadcasted_iota(jnp.int32, (LANE, seq_len), 0 if turned else 1)
        if turned:
            place = place + rb * LANE
        order = (rank <= own) if turned else (own <= rank)
        ok = (place < limit) & ((place == 0) | order)
        mask_ref[s, rb * LANE : (rb + 1) * LANE, :] = jnp.where(ok, 0.0, MASKED)


def fill_near(near_ref, small, onehot_ref):
    near_ref[...] = lax.dot_general(small, onehot_ref[...], (((0,), (0,)), ((), ())), preferred_element_type=F32) * LOG2E


def attention_step(hp, s, proj, mask_ref, near_ref, put_out, put_total):
    query_c, keys, value, query_g = proj
    seq_len = keys.shape[0]
    blocks = seq_len // LANE
    values = jnp.concatenate([value, jnp.ones((seq_len, LANE), BF16)], 1)
    lane = lax.broadcasted_iota(jnp.int32, (seq_len, LANE), 1)
    diag_r = lax.broadcasted_iota(jnp.int32, (LANE, LANE), 0)
    diag_c = lax.broadcasted_iota(jnp.int32, (LANE, LANE), 1)
    outs = [[], []]
    totals = [jnp.zeros((seq_len, LANE), F32), jnp.zeros((seq_len, LANE), F32)]
    for t in range(2):
        head = hp * 2 + t
        sel = head_lanes((seq_len, LANE), t)
        head_row = near_ref[pl.ds(head, 1), :]
        near = skewed(head_row[:, :NEAR], 3 * LANE)
        bias = tile_bias(near, head_row[:, NEAR : NEAR + 1], head_row[:, NEAR + 1 : NEAR + 2], seq_len, -1)
        for stream in range(2):
            query = jnp.where(sel, query_g if stream else query_c, jnp.zeros((), BF16))
            raw = nt(query, keys)
            probs = []
            maxes = []
            for rb in range(blocks):
                part = raw[rb * LANE : (rb + 1) * LANE, :] + (bias[rb] + mask_ref[s, rb * LANE : (rb + 1) * LANE, :])
                if stream == 1:
                    hit = diag_r == diag_c
                    if rb == 0:
                        hit = hit & (diag_c != 0)
                    pieces = []
                    if rb > 0:
                        pieces.append(part[:, : rb * LANE])
                    pieces.append(jnp.where(hit, MASKED, part[:, rb * LANE : (rb + 1) * LANE]))
                    if rb < blocks - 1:
                        pieces.append(part[:, (rb + 1) * LANE :])
                    part = jnp.concatenate(pieces, 1)
                top = jnp.max(part, 1, keepdims=True)
                probs.append(jnp.exp2(part - top).astype(BF16))
                maxes.append(jnp.broadcast_to(top, (LANE, LANE)))
            mixed = nn(jnp.concatenate(probs, 0), values)
            total = mixed[:, LANE:]
            outs[stream].append(mixed[:, :LANE] / total)
            log_total = jnp.concatenate(maxes, 0) + jnp.log2(total)
            hi = log_total.astype(BF16).astype(F32)
            totals[stream] = jnp.where(lane == head, -hi, jnp.where(lane == head + HEAD, hi - log_total, totals[stream]))
    first = head_lanes((seq_len, LANE), 0)
    mine = (lane == hp * 2) | (lane == hp * 2 + 1) | (lane == hp * 2 + HEAD) | (lane == hp * 2 + 1 + HEAD)
    for stream in range(2):
        put_out(stream, jnp.where(first, outs[stream][0], outs[stream][1]).astype(BF16))
        put_total(stream, totals[stream].astype(BF16), mine)


def forward_kernel(shapes, linked, len_ref, content_ref, query_ref, ord_ref, onehot_ref, *refs):
    n = len(shapes)
    if linked:
        shards, small_shard, refs = refs[:n], refs[n], refs[n + 1 :]
        full_refs, refs = refs[: n - 1], refs[n - 1 :]
        joined_out, small_out, refs = refs[0], refs[1], refs[2:]
    else:
        joined_in, small_in, refs = refs[0], refs[1], refs[2:]
    mixed_ref, total_ref, proj_out, joined_ref, small_ref, proj_ref, mask_ref, near_ref, own_sem = refs[:9]
    hp = pl.program_id(0)
    s = pl.program_id(1)
    step = hp * pl.num_programs(1) + s
    steps = (HEADS // 2) * total_ref.shape[1]
    seqs = total_ref.shape[1]
    seq_len = total_ref.shape[2]
    row_count, width = content_ref.shape
    if linked:
        send, recv = refs[9:]
        net = Gather(shapes, shards, (joined_ref,) + tuple(full_refs), send, recv)
        net.small_shard, net.small_full = small_shard, small_ref
    proj_copy = pltpu.make_async_copy(proj_ref, proj_out, own_sem.at[0])

    @pl.when(step == 0)
    def _():
        if linked:
            net.barrier()
            far, own, here, sib = net.small_copies()
            for d in far + [own, here]:
                d.start()
            for w in range(n):
                net.start(w)
            for s0 in range(seqs):
                fill_mask(mask_ref, ord_ref, len_ref[s0], s0, seq_len, False)
            for d, e in zip(far, sib):
                d.wait_recv()
                e.start()
            for k in (1, 2, 3):
                net.relay_z(0, k)
            for k in (1, 2, 3):
                net.relay_xy(0, k)
            for k in (1, 2, 3):
                net.relay_z(1, k)
            for k in (1, 2, 3):
                net.relay_diag(0, k)
            for k in (1, 2, 3):
                net.relay_z(2, k)
            for d in far:
                d.wait_send()
            for d in [own] + sib:
                d.wait_send()
                d.wait_recv()
            here.wait()
            net.arrive(0)
            pltpu.make_async_copy(joined_ref, joined_out, own_sem.at[1]).start()
            pltpu.make_async_copy(small_ref, small_out, own_sem.at[2]).start()
        else:
            fetch = (pltpu.make_async_copy(joined_in, joined_ref, own_sem.at[1]), pltpu.make_async_copy(small_in, small_ref, own_sem.at[2]))
            for d in fetch:
                d.start()
            for s0 in range(seqs):
                fill_mask(mask_ref, ord_ref, len_ref[s0], s0, seq_len, False)
            for d in fetch:
                d.wait()
        fill_near(near_ref, small_ref[...], onehot_ref)
        small = small_ref[...].astype(F32)
        shards_all = small.shape[0] // ROWS
        unit = width // shards_all
        half = shards_all // 2
        shift_q = spread_rows(small, [k // 2 * ROWS + k % 2 for k in range(2 * half)], 0, 2 * half, unit)
        shift_v = spread_rows(small, [(half + k // 2) * ROWS + k % 2 for k in range(2 * half)], 0, 2 * half, unit)
        scale = LOG2E / math.sqrt(HEAD)
        chunk = 256

        @pl.loop(0, row_count // chunk)
        def _(i):
            rows = pl.ds(pl.multiple_of(i * chunk, chunk), chunk)
            rows_c = content_ref[rows, :]
            proj_ref[rows, 0:width] = ((nn(rows_c, joined_ref[:, 0:width]) + shift_q) * scale).astype(BF16)
            proj_ref[rows, width : 2 * width] = nn(rows_c, joined_ref[:, width : 2 * width]).astype(BF16)
            proj_ref[rows, 2 * width : 3 * width] = (nn(rows_c, joined_ref[:, 2 * width : 3 * width]) + shift_v).astype(BF16)
            proj_ref[rows, 3 * width : 4 * width] = ((nn(query_ref[rows, :], joined_ref[:, 0:width]) + shift_q) * scale).astype(BF16)

        proj_copy.start()

    if linked:
        agenda = {
            1: [(net.relay_xy, 1, (1, 2, 3))],
            3: [(net.relay_z, 3, (1, 2, 3))],
            4: [(net.relay_xy, 2, (1,))],
            5: [(net.relay_xy, 2, (2,)), (net.relay_diag, 1, (1, 2, 3))],
            6: [(net.relay_xy, 2, (3,))],
            8: [(net.relay_diag, 2, (1, 2)), (net.relay_xy, 3, (1,))],
            9: [(net.relay_diag, 2, (3,)), (net.relay_xy, 3, (2,))],
            10: [(net.relay_xy, 3, (3,))],
        }
        for at, acts in agenda.items():

            @pl.when(step == min(at, steps - 1))
            def _():
                for act, w, ks in acts:
                    for k in ks:
                        act(w, k)

    here_rows = pl.ds(pl.multiple_of(s * seq_len, seq_len), seq_len)
    column = lambda k: pl.ds(pl.multiple_of(k * width + hp * LANE, LANE), LANE)
    proj = [proj_ref[here_rows, column(k)] for k in range(4)]

    def put_out(stream, value):
        mixed_ref[stream] = value

    def put_total(stream, value, mine):
        @pl.when(hp == 0)
        def _():
            total_ref[stream, s] = value

        @pl.when(hp > 0)
        def _():
            total_ref[stream, s] = jnp.where(mine, value, total_ref[stream, s])

    attention_step(hp, s, proj, mask_ref, near_ref, put_out, put_total)

    @pl.when(step == steps - 1)
    def _():
        proj_copy.wait()
        if linked:
            pltpu.make_async_copy(joined_ref, joined_out, own_sem.at[1]).wait()
            pltpu.make_async_copy(small_ref, small_out, own_sem.at[2]).wait()
            for k in (1, 2, 3):
                net.relay_diag(3, k)
            for w in range(n):
                if w:
                    net.arrive(w)
                net.drain(w)


def forward_attention(linked, content_rows, query_rows, lengths, order, weights, small):
    row_count, width = content_rows.shape
    seqs, seq_len = order.shape
    pairs = width // LANE
    shards = 8 if linked else small.shape[0] // ROWS
    onehot = table_onehot(-1, shards)
    shapes = [w.shape for w in weights] if linked else []
    n = len(shapes)
    anywhere = pl.BlockSpec(memory_space=pl.ANY)
    inside = pl.BlockSpec(memory_space=pltpu.VMEM)
    block3 = pl.BlockSpec((2, seq_len, LANE), lambda h, s: (0, s, h))
    joined_shape = (width, 3 * width)
    small_shape = (shards * ROWS, LANE)
    out_specs, out_shape = [], []
    if linked:
        out_specs += [anywhere] * (n + 1)
        out_shape += [jax.ShapeDtypeStruct((8 * a, b), BF16) for a, b in shapes[1:]]
        out_shape += [jax.ShapeDtypeStruct(joined_shape, BF16), jax.ShapeDtypeStruct(small_shape, BF16)]
    out_specs += [block3, pl.BlockSpec((2, seqs, seq_len, LANE), lambda h, s: (0, 0, 0, 0)), anywhere]
    out_shape += [
        jax.ShapeDtypeStruct((2, row_count, width), BF16),
        jax.ShapeDtypeStruct((2, seqs, seq_len, LANE), BF16),
        jax.ShapeDtypeStruct((row_count, 4 * width), BF16),
    ]
    scratch = [
        pltpu.VMEM(joined_shape, BF16),
        pltpu.VMEM(small_shape, BF16),
        pltpu.VMEM((row_count, 4 * width), BF16),
        pltpu.VMEM((seqs, seq_len, seq_len), F32),
        pltpu.VMEM((LANE, NEAR + LANE), F32),
        pltpu.SemaphoreType.DMA((3,)),
    ]
    if linked:
        scratch += [pltpu.SemaphoreType.DMA((n + 1, 4, Gather.SLOTS)), pltpu.SemaphoreType.DMA((n + 1, 4, Gather.SLOTS))]
    flops = 2 * row_count * width * 4 * width + 8 * row_count * seq_len * width
    return pl.pallas_call(
        functools.partial(forward_kernel, shapes, linked),
        grid=(pairs, seqs),
        in_specs=[pl.BlockSpec(memory_space=pltpu.SMEM), inside, inside, inside, inside] + [anywhere] * (n + 1 if linked else 2),
        out_specs=out_specs,
        out_shape=out_shape,
        scratch_shapes=scratch,
        cost_estimate=pl.CostEstimate(flops=flops, bytes_accessed=30 * 2**20, transcendentals=4 * row_count * seq_len * HEADS),
        compiler_params=pltpu.CompilerParams(
            dimension_semantics=("arbitrary", "arbitrary"), vmem_limit_bytes=VMEM_BYTES,
            **(dict(collective_id=0, has_side_effects=True) if linked else {})),
        name="attention_forward",
    )(lengths, content_rows, query_rows, order, onehot, *(list(weights) + [small]))


def backward_kernel(shapes, linked, len_ref, q_ref, k_ref, v_ref, g_ref, dc_ref, dg_ref, oc_ref, og_ref, tot_ref, ord_ref, small_ref, onehot_ref, *refs):
    n = len(shapes)
    grads, refs = refs[:n], refs[n:]
    outs, refs = refs[:n], refs[n:]
    grad_ref, lows_ref, sums_ref, mask_ref, acc_ref, near_ref = refs[:6]
    refs = refs[6:]
    hp = pl.program_id(0)
    s = pl.program_id(1)
    last = pl.num_programs(1) - 1
    step = hp * pl.num_programs(1) + s
    seq_len = q_ref.shape[0]
    blocks = seq_len // LANE
    half = seq_len // 2
    steps = (HEADS // 2) * ord_ref.shape[0]
    if linked:
        bufs = [refs[7 * w : 7 * w + 7] for w in range(n)]
        send, recv = refs[7 * n :]
        net = Reduce(shapes, grads, outs, bufs, send, recv)
        items, ticks = plan(net, n, list(range(n)))

        @pl.when(step == 0)
        def _():
            net.barrier()
            for w, k in items:
                net.start(w, k)

        tail = ticks[-2:]
        ticks = ticks[:-2]
        for at in range(1, steps):
            acts = [a for i, t in enumerate(ticks) if 1 + i * (steps - 1) // len(ticks) == at for a in t]

            @pl.when(step == at)
            def _():
                for act in acts:
                    act()

    @pl.when(hp == 0)
    def _():
        fill_mask(mask_ref, ord_ref, len_ref[s], s, seq_len, True)

    @pl.when(step == 0)
    def _():
        fill_near(near_ref, small_ref[...], onehot_ref)

    lane = lax.broadcasted_iota(jnp.int32, (seq_len, LANE), 1)
    ones = jnp.ones((seq_len, LANE), BF16)
    zero = jnp.zeros((), BF16)
    keys = k_ref[...]
    keys_wide = jnp.concatenate([keys, ones], 1)
    values_wide = jnp.concatenate([v_ref[...], ones], 1)
    keys_turned = keys.astype(F32).T.astype(BF16)
    lane_r = lax.broadcasted_iota(jnp.int32, (LANE, LANE), 0)
    lane_c = lax.broadcasted_iota(jnp.int32, (LANE, LANE), 1)
    pick = (lane_r // HEAD == lane_c).astype(BF16)
    grad_keys = None
    grad_values = None
    grad_query = [[], []]
    streams = []
    for src, grad, out, tot in ((q_ref, dc_ref, oc_ref, tot_ref[0, 0]), (g_ref, dg_ref, og_ref, tot_ref[1, 0])):
        g = grad[...]
        delta = nn((g.astype(F32) * out[...].astype(F32)).astype(BF16), pick)
        streams.append((src[...], g, -delta, tot))
    for t in range(2):
        head = hp * 2 + t
        sel = head_lanes((seq_len, LANE), t)
        head_row = near_ref[pl.ds(head, 1), :]
        near = skewed(head_row[:, :NEAR], 3 * LANE)
        bias = tile_bias(near, head_row[:, NEAR : NEAR + 1], head_row[:, NEAR + 1 : NEAR + 2], seq_len, 1)
        for c0 in range(0, seq_len, half):
            both = None
            for stream in range(2):
                q, g, delta, tot = streams[stream]
                q = jnp.where(sel, q, zero)[c0 : c0 + half]
                g = jnp.where(sel, g, zero)[c0 : c0 + half]
                d = delta[c0 : c0 + half]
                ln = lane[c0 : c0 + half]
                tt = jnp.where((ln == head) | (ln == head + HEAD), tot[c0 : c0 + half], zero)
                dd = jnp.where(ln == t, d, 0.0)
                dhi = dd.astype(BF16)
                dlo = pltpu.roll(dd - dhi.astype(F32), HEAD, 1).astype(BF16)
                raw = nt(keys_wide, jnp.concatenate([q, tt], 1))
                dpr = nt(values_wide, jnp.concatenate([g, dhi + dlo], 1))
                probs, grads = [], []
                for rb in range(blocks):
                    sl = slice(rb * LANE, (rb + 1) * LANE)
                    part = raw[sl] + (bias[rb][:, c0 : c0 + half] + mask_ref[s, sl, c0 : c0 + half])
                    r0 = rb * LANE
                    if stream == 1 and c0 <= r0 < c0 + half:
                        hit = lane_r == lane_c
                        if rb == 0:
                            hit = hit & (lane_r != 0)
                        x0 = r0 - c0
                        diag = jnp.where(hit, MASKED, part[:, x0 : x0 + LANE])
                        pieces = []
                        if x0 > 0:
                            pieces.append(part[:, :x0])
                        pieces.append(diag)
                        if x0 + LANE < half:
                            pieces.append(part[:, x0 + LANE :])
                        part = jnp.concatenate(pieces, 1)
                    p = jnp.exp2(part)
                    probs.append(p.astype(BF16))
                    grads.append(p * dpr[sl])
                low = [x.astype(BF16) for x in grads]
                prob = jnp.concatenate(probs, 0)
                gl = jnp.concatenate(low, 0)
                gv = nn(prob, g)
                gk = nn(gl, q)
                grad_values = gv if grad_values is None else grad_values + gv
                grad_keys = gk if grad_keys is None else grad_keys + gk
                grad_query[stream].append(nn(keys_turned[t * HEAD : (t + 1) * HEAD], gl))
                both = grads if both is None else [a + b for a, b in zip(both, grads)]
            sums = {}
            for rb in range(blocks):
                for cb in range(half // LANE):
                    e = cb + c0 // LANE - rb
                    e = max(-2, min(2, e))
                    x = both[rb][:, cb * LANE : (cb + 1) * LANE]
                    sums[e] = x if e not in sums else sums[e] + x
            for e, x in sums.items():
                lanes = slice((e + 2) * LANE, (e + 3) * LANE)
                fresh = c0 == 0
                if fresh:
                    @pl.when(s == 0)
                    def _():
                        acc_ref[t, :, lanes] = x

                    @pl.when(s > 0)
                    def _():
                        acc_ref[t, :, lanes] = acc_ref[t, :, lanes] + x
                else:
                    acc_ref[t, :, lanes] = acc_ref[t, :, lanes] + x
            if c0 == 0:
                for e in range(-2, 3):
                    if e not in sums:
                        @pl.when(s == 0)
                        def _():
                            acc_ref[t, :, (e + 2) * LANE : (e + 3) * LANE] = jnp.zeros((LANE, LANE), F32)
    count = seq_len // half
    scale = 1.0 / math.sqrt(HEAD)

    @pl.when(s == 0)
    def _():
        lows_ref[...] = jnp.zeros_like(lows_ref)

    def put_grad(k, value):
        grad_ref[k] = value
        lows_ref[k] = lows_ref[k] + fold8(value.astype(F32))

    for stream, ref in ((0, 0), (1, 3)):
        pieces = grad_query[stream]
        top = jnp.concatenate(pieces[:count], 1)
        bot = jnp.concatenate(pieces[count:], 1)
        put_grad(ref, (jnp.concatenate([top, bot], 0) * scale).T.astype(BF16))
    put_grad(1, (grad_keys * LN2).astype(BF16))
    put_grad(2, grad_values.astype(BF16))

    @pl.when(s == last)
    def _():
        for t in range(2):
            near = jnp.concatenate([acc_ref[t, :, LANE : 4 * LANE], jnp.zeros((LANE, LANE), F32)], 1)
            mirror = (lane_r + lane_c == LANE - 1).astype(F32)
            flipped = lax.dot_general(mirror, near, (((1,), (0,)), ((), ())), precision=lax.Precision.HIGHEST, preferred_element_type=F32)
            turned = pltpu.roll(flipped, 0, 1, stride=1, stride_axis=0)
            row = jnp.sum(turned, 0, keepdims=True)
            below = jnp.sum(acc_ref[t, :, :LANE], 0, keepdims=True)
            above = jnp.sum(acc_ref[t, :, 4 * LANE :], 0, keepdims=True)
            sums_ref[pl.ds(hp * 2 + t, 1), :] = jnp.concatenate([row, below, above], 1)

    if linked:

        @pl.when(step == steps - 1)
        def _():
            for acts in tail:
                for act in acts:
                    act()


def backward_attention(linked, proj, grad_mixed, mixed, totals, lengths, order, small, weight_grads):
    rows, width = grad_mixed.shape
    seqs, seq_len = order.shape
    pairs = width // LANE
    onehot = table_onehot(1, small.shape[0] // ROWS)
    shapes = [(g.shape[0] // 8, g.shape[1]) for g in weight_grads]
    n = len(shapes)
    block = lambda off: pl.BlockSpec((seq_len, LANE), lambda h, s, off=off: (s, off + h))
    low = pl.BlockSpec((seq_len, LANE), lambda h, s: (seqs + s, h))
    anywhere = pl.BlockSpec(memory_space=pl.ANY)
    inside = pl.BlockSpec(memory_space=pltpu.VMEM)
    sums_shape = (2 * pairs, NEAR + 2 * LANE)
    scratch = [
        pltpu.VMEM((seqs, seq_len, seq_len), F32),
        pltpu.VMEM((2, LANE, 5 * LANE), F32),
        pltpu.VMEM((LANE, NEAR + LANE), F32),
    ]
    if linked:
        scratch += Reduce.scratch(shapes)
        scratch += [pltpu.SemaphoreType.DMA((n, 4, Reduce.SLOTS)), pltpu.SemaphoreType.DMA((n, 4, Reduce.SLOTS))]
    outs = pl.pallas_call(
        functools.partial(backward_kernel, shapes, linked),
        grid=(pairs, seqs),
        in_specs=[
            pl.BlockSpec(memory_space=pltpu.SMEM),
            block(0), block(pairs), block(2 * pairs), block(3 * pairs),
            block(0), low, block(0), low,
            pl.BlockSpec((2, 1, seq_len, LANE), lambda h, s: (0, s, 0, 0)),
            inside, inside, inside,
        ] + [anywhere] * n,
        out_specs=[anywhere] * n + [pl.BlockSpec((4, seq_len, LANE), lambda h, s: (0, s, h)), pl.BlockSpec((4, 8, LANE), lambda h, s: (0, 0, h)), pl.BlockSpec(sums_shape, lambda h, s: (0, 0))],
        out_shape=[jax.ShapeDtypeStruct(a, BF16) for a in shapes] + [jax.ShapeDtypeStruct((4, rows // 2, width), BF16), jax.ShapeDtypeStruct((4, 8, width), F32), jax.ShapeDtypeStruct(sums_shape, F32)],
        scratch_shapes=scratch,
        cost_estimate=pl.CostEstimate(flops=20 * rows * seq_len * width, bytes_accessed=30 * 2**20, transcendentals=2 * rows * seq_len * HEADS),
        compiler_params=pltpu.CompilerParams(
            dimension_semantics=("arbitrary", "arbitrary"), vmem_limit_bytes=VMEM_BYTES,
            **(dict(collective_id=1, has_side_effects=True) if linked else {})),
        name="attention_backward",
    )(lengths, proj, proj, proj, proj, grad_mixed, grad_mixed, mixed, mixed, totals, order, small, onehot, *weight_grads)
    sums = outs[n + 2]
    fold = np.zeros((sums_shape[1], BUCKETS), np.float32)
    fold[:NEAR] = np.roll(near_onehot(1).T, LANE - 1, 0)
    fold[NEAR : NEAR + LANE, BUCKETS - 1] = 1
    fold[NEAR + LANE :, BUCKETS // 2 - 1] = 1
    grad_table = jnp.dot(sums, jnp.asarray(fold), precision=lax.Precision.HIGHEST).T
    return outs[:n], outs[n], jnp.sum(outs[n + 1], 1), grad_table


def small_reduce(net, w, part, out, bufs):
    own, core, across_x, across_y, far = bufs
    rows = 4 * ROWS
    mine = part.at[pl.ds(pl.multiple_of(net.c * rows, rows), rows), :]
    other = part.at[pl.ds(pl.multiple_of((1 - net.c) * rows, rows), rows), :]
    load = pltpu.make_async_copy(mine, own.at[0], net.send.at[w, 0, 7])
    to_core = net.copy((w, 0, 0), other, core, net.r, net.sib)
    to_x = net.copy((w, 0, 1), own.at[1], across_x, net.xr, net.f)
    to_y = net.copy((w, 0, 2), own.at[2], across_y, net.yr, net.f)
    z_rows = lambda s: pl.ds(pl.multiple_of((net.z + s) % 4 * ROWS, ROWS), ROWS)
    to_far = [net.copy((w, s, 3), own.at[3, z_rows(s), :], far.at[s - 1], net.r, net.along(s)) for s in (1, 2, 3)]

    def first():
        load.start()
        to_core.start()

    def second():
        load.wait()
        to_core.wait_recv()
        own[1] = own[0] + core[...]
        to_x.start()

    def third():
        to_x.wait_recv()
        own[2] = own[1] + across_x[...]
        to_y.start()

    def fourth():
        to_y.wait_recv()
        own[3] = own[2] + across_y[...]
        for d in to_far:
            d.start()

    def fifth():
        for d in to_far:
            d.wait_recv()
        out[...] = own[3, z_rows(0), :] + far[0] + far[1] + far[2]
        for d in [to_core, to_x, to_y] + to_far:
            d.wait_send()

    return first, second, third, fourth, fifth


def input_grads(rows, grads, joined, branch):
    width = branch.shape[1]
    total = grads.shape[1]
    low = pl.ds(pl.multiple_of(total + rows.start, 256), rows.size)
    content = branch[rows, :].astype(F32)
    for k in range(3):
        content = content + nt(grads[k, rows, :], joined[:, k * width : (k + 1) * width])
    query = branch[low, :].astype(F32) + nt(grads[3, rows, :], joined[:, :width])
    return content.astype(BF16), query.astype(BF16)


def reduce_kernel(shapes, n, *refs):
    grads, small_part, sources, refs = refs[:n], refs[n], refs[n + 1 : n + 4], refs[n + 4 :]
    outs, small_out, stream_outs, refs = refs[:n], refs[n], refs[n + 1 : n + 3], refs[n + 3 :]
    held, results, own_sem, refs = refs[:3], refs[3:5], refs[5], refs[6:]
    bufs = [refs[7 * w : 7 * w + 7] for w in range(n)]
    small_bufs, (send, recv) = refs[7 * n : 7 * n + 5], refs[7 * n + 5 :]
    net = Reduce(shapes, grads, outs, bufs, send, recv)
    first, second, third, fourth, fifth = small_reduce(net, n, small_part, small_out, small_bufs)
    fetch = [pltpu.make_async_copy(a, b, own_sem.at[k]) for k, (a, b) in enumerate(zip(sources, held))]
    store = [pltpu.make_async_copy(a, b, own_sem.at[3 + k]) for k, (a, b) in enumerate(zip(results, stream_outs))]
    net.barrier()
    items, ticks = plan(net, n, list(range(n)))
    first()
    for w, k in items:
        net.start(w, k)
    for d in fetch:
        d.start()
    for d in fetch:
        d.wait()
    pieces = 4
    chunk = results[0].shape[0] // pieces
    extra = {1: second, 4: third, 6: fourth}
    for i, acts in enumerate(ticks):
        for act in acts:
            act()
        if i in extra:
            extra[i]()
        if i == 3:

            @pl.loop(0, pieces)
            def _(k):
                rows = pl.ds(pl.multiple_of(k * chunk, chunk), chunk)
                content, query = input_grads(rows, *held)
                results[0][rows, :] = content
                results[1][rows, :] = query

            for d in store:
                d.start()
    fifth()
    for d in store:
        d.wait()


def reduce_rest(weight_grads, small_grads, grads, joined, branch):
    n = len(weight_grads)
    shapes = [(g.shape[0] // 8, g.shape[1]) for g in weight_grads]
    anywhere = pl.BlockSpec(memory_space=pl.ANY)
    inside = pl.BlockSpec(memory_space=pltpu.VMEM)
    rows = 4 * ROWS
    stream = grads.shape[1:]
    scratch = [pltpu.VMEM(a.shape, BF16) for a in (grads, joined, branch)] + [pltpu.VMEM(stream, BF16)] * 2 + [pltpu.SemaphoreType.DMA((5,))]
    scratch += Reduce.scratch(shapes)
    scratch += [pltpu.VMEM((4, rows, LANE), F32)] + [pltpu.VMEM((rows, LANE), F32)] * 3 + [pltpu.VMEM((3, ROWS, LANE), F32)]
    scratch += [pltpu.SemaphoreType.DMA((n + 1, 4, Reduce.SLOTS)), pltpu.SemaphoreType.DMA((n + 1, 4, Reduce.SLOTS))]
    return pl.pallas_call(
        functools.partial(reduce_kernel, shapes, n),
        out_shape=[jax.ShapeDtypeStruct(a, BF16) for a in shapes] + [jax.ShapeDtypeStruct((ROWS, LANE), F32)] + [jax.ShapeDtypeStruct(stream, BF16)] * 2,
        in_specs=[anywhere] * (n + 4),
        out_specs=[anywhere] * n + [inside] + [anywhere] * 2,
        scratch_shapes=scratch,
        compiler_params=pltpu.CompilerParams(collective_id=2, has_side_effects=True, vmem_limit_bytes=VMEM_BYTES),
        name="reduce_rest",
    )(*weight_grads, small_grads, grads, joined, branch)


def prepare_kernel(unit, places, *refs):
    count = len(places)
    vectors, table, weights, refs = refs[:count], refs[count], refs[count + 1 : count + 5], refs[count + 5 :]
    small_ref, outs, wide_ref, part_ref = refs[0], refs[1:5], refs[5], refs[6]
    part_ref[...] = jnp.zeros_like(part_ref)
    lane = lax.broadcasted_iota(jnp.int32, (8, LANE), 1)
    for (row, chunks), ref in zip(places, vectors):
        if chunks == 1:
            part_ref[row : row + 1, :unit] = ref[...][None, :]
            continue
        size = chunks * unit
        wide = wide_ref.shape[1]
        wide_ref[0:1, :size] = ref[...][None, :]
        value = jnp.broadcast_to(wide_ref[0:1, :], (8, wide))
        for k in range(chunks):
            turned = pltpu.roll(value, wide - k * unit, 1) if k else value
            part_ref[row + k : row + k + 1, :] = jnp.where(lane < unit, turned[:, :LANE], 0.0)[0:1]
    part_ref[TABLE_ROW : TABLE_ROW + table.shape[0], : table.shape[1]] = table[...]
    small_ref[...] = part_ref[...].astype(BF16)
    for a, b in zip(weights, outs):
        b[...] = a[...].astype(BF16)


def prepare(vectors, table, weights, unit):
    places, row = [], 0
    for v in vectors:
        places.append((row, v.shape[0] // unit))
        row += v.shape[0] // unit
    widest = max(v.shape[0] for v in vectors)
    widest = (widest + LANE - 1) // LANE * LANE
    outs = pl.pallas_call(
        functools.partial(prepare_kernel, unit, places),
        out_shape=[jax.ShapeDtypeStruct((ROWS, LANE), BF16)] + [jax.ShapeDtypeStruct(w.shape, BF16) for w in weights],
        scratch_shapes=[pltpu.VMEM((8, widest), F32), pltpu.VMEM((ROWS, LANE), F32)],
        compiler_params=pltpu.CompilerParams(vmem_limit_bytes=VMEM_BYTES),
        name="prepare",
    )(*vectors, table, *weights)
    return outs[0], outs[1:]


ERF_P = 0.3275911 * 0.7071067811865476
ERF_A = (0.254829592 * 0.5, -0.284496736 * 0.5, 1.421413741 * 0.5, -1.453152027 * 0.5, 1.061405429 * 0.5)


def gelu_pair(z):
    bell = jnp.exp2(z * z * (-0.5 * LOG2E))
    t = 1.0 / (1.0 + ERF_P * jnp.abs(z))
    tail = ERF_A[4]
    for a in ERF_A[3::-1]:
        tail = tail * t + a
    tail = tail * t * bell
    share = jnp.where(z < 0.0, tail, 1.0 - tail)
    return z * share, share + z * bell * inv_root_tau


def norm_rows(summed):
    row_mean = jnp.mean(summed, -1, keepdims=True)
    centered = summed - row_mean
    inverse = lax.rsqrt(jnp.mean(centered * centered, -1, keepdims=True) + eps_norm)
    return centered * inverse, inverse


def norm_rows_back(scaled, normed, inverse):
    return inverse * (scaled - jnp.mean(scaled, -1, keepdims=True) - normed * jnp.mean(scaled * normed, -1, keepdims=True))


def fold8(value):
    rows, cols = value.shape
    return jnp.sum(value.reshape(rows // 8, 8, cols), 0)


def ffn_kernel(chunk, len_ref, mixed_ref, content_ref, query_ref, ccot_ref, qcot_ref, small_ref, wo_hbm, win_hbm, wout_hbm,
               cout_ref, qout_ref, hid_ref, dz_ref, first_ref, dffn_ref, dbranch_ref, dmixed_ref, sums_ref, wide_sums_ref,
               wo_ref, win_ref, wout_ref, vec_ref, shift_ref, slope_ref, acc_ref, wide_acc_ref, sem):
    i = pl.program_id(0)
    n = pl.num_programs(0)
    rows, width = mixed_ref.shape
    hidden = win_ref.shape[1]
    loads = [pltpu.make_async_copy(a, b, sem.at[k]) for k, (a, b) in enumerate(((wo_hbm, wo_ref), (win_hbm, win_ref), (wout_hbm, wout_ref)))]

    @pl.when(i == 0)
    def _():
        for d in loads:
            d.start()
        small = small_ref[...].astype(F32)
        shards = small.shape[0] // ROWS
        unit = width // shards
        for k in range(2, 8):
            vec_ref[k : k + 1, :] = spread_rows(small, [f * ROWS + k for f in range(shards)], 0, shards, unit)
        count = hidden // unit
        shift_ref[0:1, :] = spread_rows(small, [k // 4 * ROWS + 8 + k % 4 for k in range(count)], 0, count, unit)
        acc_ref[...] = jnp.zeros_like(acc_ref)
        wide_acc_ref[...] = jnp.zeros_like(wide_acc_ref)
        for d in loads:
            d.wait()

    first_stream = i < n // 2
    vec = lambda k: vec_ref[k : k + 1, :]

    def add_sum(k, value):
        acc_ref[k] = acc_ref[k] + fold8(value)

    residual = jnp.where(first_stream, content_ref[...], query_ref[...]).astype(F32)
    branch = nn(mixed_ref[...], wo_ref[...]) + vec(2)
    normed_one, inverse_one = norm_rows(residual + branch)
    first_low = (normed_one * vec(3) + vec(4)).astype(BF16)
    first_ref[...] = first_low
    for c in range(0, hidden, chunk):
        cols = slice(c, c + chunk)
        value, slope = gelu_pair(nn(first_low, win_ref[:, cols]) + shift_ref[0:1, cols])
        hid_ref[:, cols] = value.astype(BF16)
        slope_ref[:, cols] = slope.astype(BF16)
    ffn = nn(hid_ref[...], wout_ref[...]) + vec(5)
    normed_two, inverse_two = norm_rows(first_low.astype(F32) + ffn)
    final = (normed_two * vec(6) + vec(7)).astype(BF16)

    @pl.when(first_stream)
    def _():
        cout_ref[...] = final

    @pl.when(jnp.logical_not(first_stream))
    def _():
        qout_ref[...] = final

    per_stream = n // 2
    at = jnp.where(first_stream, i, i - per_stream) * rows
    seq_len = per_stream * rows // len_ref.shape[0]
    seq = at // seq_len
    place = at - seq * seq_len + lax.broadcasted_iota(jnp.int32, (rows, 1), 0)
    upstream = jnp.where(first_stream, ccot_ref[...], qcot_ref[...]).astype(F32)
    upstream = jnp.where(place < len_ref[seq], upstream, 0.0)
    add_sum(5, upstream * normed_two)
    add_sum(6, upstream)
    grad_two = norm_rows_back(upstream * vec(6), normed_two, inverse_two)
    grad_ffn = grad_two.astype(BF16)
    dffn_ref[...] = grad_ffn
    add_sum(4, grad_ffn.astype(F32))
    for c in range(0, hidden, chunk):
        cols = slice(c, c + chunk)
        grad = nt(grad_ffn, wout_ref[cols, :]) * slope_ref[:, cols].astype(F32)
        wide_acc_ref[:, cols] = wide_acc_ref[:, cols] + fold8(grad)
        dz_ref[:, cols] = grad.astype(BF16)
    grad_first = grad_two + nt(dz_ref[...], win_ref[...])
    add_sum(2, grad_first * normed_one)
    add_sum(3, grad_first)
    grad_branch = norm_rows_back(grad_first * vec(3), normed_one, inverse_one).astype(BF16)
    dbranch_ref[...] = grad_branch
    add_sum(1, grad_branch.astype(F32))
    dmixed_ref[...] = nt(grad_branch, wo_ref[...]).astype(BF16)

    @pl.when(i == n - 1)
    def _():
        for k in range(8):
            sums_ref[k : k + 1, :] = jnp.sum(acc_ref[k], 0, keepdims=True)
        wide_sums_ref[...] = jnp.sum(wide_acc_ref[...], 0, keepdims=True)


def ffn_stage(mixed, content_rows, query_rows, content_cot, query_cot, lengths, small, out_proj, in_proj, out_ffn, rows=256, chunk=768):
    total, width = mixed.shape
    hidden = in_proj.shape[1]
    n = total // rows
    half = n // 2
    anywhere = pl.BlockSpec(memory_space=pl.ANY)
    row_block = lambda cols: pl.BlockSpec((rows, cols), lambda i: (i, 0))
    low = pl.BlockSpec((rows, width), lambda i: (jnp.minimum(i, half - 1), 0))
    high = pl.BlockSpec((rows, width), lambda i: (jnp.maximum(i - half, 0), 0))
    whole = lambda shape: pl.BlockSpec(shape, lambda i: (0,) * len(shape))
    shape = jax.ShapeDtypeStruct
    return pl.pallas_call(
        functools.partial(ffn_kernel, chunk),
        grid=(n,),
        in_specs=[pl.BlockSpec(memory_space=pltpu.SMEM), row_block(width), low, high, low, high, whole(small.shape)] + [anywhere] * 3,
        out_specs=[low, high, row_block(hidden), row_block(hidden)] + [row_block(width)] * 4 + [whole((8, width)), whole((1, hidden))],
        out_shape=[shape((total // 2, width), BF16)] * 2 + [shape((total, hidden), BF16)] * 2 + [shape((total, width), BF16)] * 4
        + [shape((8, width), F32), shape((1, hidden), F32)],
        scratch_shapes=[
            pltpu.VMEM((width, width), BF16),
            pltpu.VMEM((width, hidden), BF16),
            pltpu.VMEM((hidden, width), BF16),
            pltpu.VMEM((8, width), F32),
            pltpu.VMEM((8, hidden), F32),
            pltpu.VMEM((rows, hidden), BF16),
            pltpu.VMEM((8, 8, width), F32),
            pltpu.VMEM((8, hidden), F32),
            pltpu.SemaphoreType.DMA((3,)),
        ],
        cost_estimate=pl.CostEstimate(flops=4 * total * width * (2 * hidden + width), bytes_accessed=60 * 2**20, transcendentals=2 * total * hidden),
        compiler_params=pltpu.CompilerParams(dimension_semantics=("arbitrary",), vmem_limit_bytes=VMEM_BYTES),
        name="ffn_stage",
    )(lengths, mixed, content_rows, query_rows, content_cot, query_cot, small, out_proj, in_proj, out_ffn)


def rows_inner(left_op, right_op):
    return lax.dot_general(
        left_op, right_op, (((0,), (0,)), ((), ())), preferred_element_type=jnp.float32
    )


def times_transpose(left_op, right_op):
    return lax.dot_general(
        left_op, right_op, (((1,), (1,)), ((), ())), preferred_element_type=jnp.float32
    )


def pack_small(groups, shards):
    rows = []
    for g in groups:
        g = g.reshape(shards, -1, g.shape[-1]) if g.ndim > 1 else g
        rows.append(g)
    wide = [jnp.pad(g, ((0, 0), (0, 0), (0, LANE - g.shape[2]))) for g in rows]
    joined = jnp.concatenate(wide, 1)
    joined = jnp.pad(joined, ((0, 0), (0, ROWS - joined.shape[1]), (0, 0)))
    return joined.reshape(shards * ROWS, LANE)


def on_device(axes, content_stream, query_stream, lengths, factor_order, qkv_weight, qv_bias, out_weight, out_bias, norm1_gain, norm1_bias, rel_table, ffn_in_weight, ffn_in_bias, ffn_out_weight, ffn_out_bias, norm2_gain, norm2_bias, content_cot, query_cot):
    linked = axes == (4, 8)
    shards = axes[1]
    seq_count, seq_len, width = content_stream.shape
    row_count = seq_count * seq_len
    unit = width // shards
    small_args = (qv_bias, out_bias, norm1_gain, norm1_bias, ffn_out_bias, norm2_gain, norm2_bias, ffn_in_bias)
    weights = (qkv_weight, out_weight, ffn_in_weight, ffn_out_weight)
    if linked:
        small, weights = prepare(small_args, rel_table, weights, unit)
    else:
        small = pack_small([p.reshape(1, -1, unit) for p in small_args] + [rel_table[None]], 1).astype(BF16)
        weights = [w.astype(BF16) for w in weights]
    content_rows = content_stream.reshape(row_count, width)
    query_rows = query_stream.reshape(row_count, width)
    if linked:
        out_proj, in_proj, out_ffn, joined_proj, small, mixed, totals, proj = forward_attention(
            True, content_rows, query_rows, lengths, factor_order, weights, small)
    else:
        gather = lambda a: lax.all_gather(a, "fsdp", axis=0, tiled=True)
        joined_proj, out_proj, in_proj, out_ffn = [gather(w) for w in weights]
        small = gather(small)
        mixed, totals, proj = forward_attention(False, content_rows, query_rows, lengths, factor_order, [joined_proj], small)
    mixed_rows = mixed.reshape(2 * row_count, width)
    flat_cot = lambda a: a.reshape(row_count, width)
    content_out, query_out, hidden_low, grad_hidden, first_low, grad_ffn, grad_branch, grad_mixed, sums, wide_sums = ffn_stage(
        mixed_rows, content_rows, query_rows, flat_cot(content_cot), flat_cot(query_cot), lengths, small, out_proj, in_proj, out_ffn)
    grad_out_ffn = rows_inner(hidden_low, grad_ffn).astype(BF16)
    grad_in_proj = rows_inner(first_low, grad_hidden).astype(BF16)
    grad_out_proj = rows_inner(mixed_rows, grad_branch).astype(BF16)
    ready = [grad_in_proj, grad_out_ffn, grad_out_proj] if linked else []
    early, grads, low_sums, grad_table = backward_attention(linked, proj, grad_mixed, mixed_rows, totals, lengths, factor_order, small, ready)
    grad_q = rows_inner(content_rows, grads[0]) + rows_inner(query_rows, grads[3])
    grad_joined = jnp.concatenate([grad_q, rows_inner(content_rows, grads[1]), rows_inner(content_rows, grads[2])], 1).astype(BF16)
    grad_proj_shift = jnp.concatenate([low_sums[0] + low_sums[3], low_sums[2]])
    rows_of = lambda g: g.reshape(shards, -1, unit) if g.ndim == 1 or g.shape[0] == 1 else g.reshape(-1, shards, unit).transpose(1, 0, 2)
    packed = pack_small([rows_of(grad_proj_shift), rows_of(sums[1:7]), rows_of(wide_sums), grad_table.reshape(shards, -1, HEADS)], shards)
    if linked:
        packed = packed.reshape(4, 2, ROWS, LANE).transpose(1, 0, 2, 3).reshape(8 * ROWS, LANE)
        sum_joined, mine, content_grad_rows, query_grad_rows = reduce_rest([grad_joined], packed, grads, joined_proj, grad_branch)
        sum_in, sum_out, sum_proj = early
    else:
        scatter = lambda a: lax.psum(lax.psum_scatter(a, "fsdp", scatter_dimension=0, tiled=True), "rep")
        sum_joined, sum_in, sum_out, sum_proj = [scatter(a) for a in (grad_joined, grad_in_proj, grad_out_ffn, grad_out_proj)]
        mine = scatter(packed)
        content_grad_rows = grad_branch[:row_count].astype(F32) + (
            times_transpose(grads[0], joined_proj[:, :width])
            + times_transpose(grads[1], joined_proj[:, width : 2 * width])
            + times_transpose(grads[2], joined_proj[:, 2 * width :])
        )
        query_grad_rows = grad_branch[row_count:].astype(F32) + times_transpose(grads[3], joined_proj[:, :width])
    sum_joined, sum_in, sum_out, sum_proj = [a.astype(F32) for a in (sum_joined, sum_in, sum_out, sum_proj)]
    vec = lambda k: mine[k, :unit]
    block_shape = (seq_count, seq_len, width)
    return (
        content_out.reshape(block_shape),
        query_out.reshape(block_shape),
        content_grad_rows.reshape(block_shape).astype(BF16),
        query_grad_rows.reshape(block_shape).astype(BF16),
        sum_joined,
        mine[0:2, :unit].reshape(-1),
        sum_proj,
        vec(2),
        vec(3),
        vec(4),
        mine[TABLE_ROW : TABLE_ROW + rel_table.shape[0], :HEADS],
        sum_in,
        mine[8:12, :unit].reshape(-1),
        sum_out,
        vec(5),
        vec(6),
        vec(7),
    )


def solution(mesh):
    in_specs = (
        P(("rep", "fsdp"), None, None),
        P(("rep", "fsdp"), None, None),
        P(("rep", "fsdp")),
        P(("rep", "fsdp"), None),
        P("fsdp", None),
        P("fsdp"),
        P("fsdp", None),
        P("fsdp"),
        P("fsdp"),
        P("fsdp"),
        P("fsdp", None),
        P("fsdp", None),
        P("fsdp"),
        P("fsdp", None),
        P("fsdp"),
        P("fsdp"),
        P("fsdp"),
        P(("rep", "fsdp"), None, None),
        P(("rep", "fsdp"), None, None),
    )
    out_specs = (
        P(("rep", "fsdp"), None, None),
        P(("rep", "fsdp"), None, None),
        P(("rep", "fsdp"), None, None),
        P(("rep", "fsdp"), None, None),
        P("fsdp", None),
        P("fsdp"),
        P("fsdp", None),
        P("fsdp"),
        P("fsdp"),
        P("fsdp"),
        P("fsdp", None),
        P("fsdp", None),
        P("fsdp"),
        P("fsdp", None),
        P("fsdp"),
        P("fsdp"),
        P("fsdp"),
    )
    return jax.shard_map(
        functools.partial(on_device, tuple(mesh.shape[a] for a in mesh.axis_names)),
        mesh=mesh,
        in_specs=in_specs,
        out_specs=out_specs,
        check_vma=False,
    )
```
